512 devices in a mesh: dp: 8 (over x, z_hi), seq: 64 (over y, z_lo, core).
Axes of the slice: x: 4, y: 8, z: 8 (z_hi: 2, z_lo: 4; z = z_hi * 4 + z_lo), core: 2. Of those that a mesh axis runs over, the one named last changes fastest.
Arguments:
- clean: bfloat16 [8, 16384, 768], P('dp', 'seq'), may hold values from -12 to 12
- out_cot: bfloat16 [8, 16384, 768], P('dp', 'seq'), may hold values from -6 to 6
- mask_bits: int32 [8, 1024], P('dp', 'seq'), may hold values from 0 to 65535
- levels: int32 [8, 1024], P('dp', 'seq'), may hold values from 1 to 16
- importance: int32 [8, 1024, 2], P('dp', 'seq'), may hold values from 1 to 8
- w_query: bfloat16 [768, 768], replicated, may hold values from -0.21875 to 0.21875
- w_key: bfloat16 [768, 768], replicated, may hold values from -0.21875 to 0.21875
- w_value: bfloat16 [768, 768], replicated, may hold values from -0.21875 to 0.21875
- mask_embed: bfloat16 [768], replicated, may hold values from -6 to 6
Outputs:
- attn_out: bfloat16 [8, 16384, 768], P('dp', 'seq')
- clean_grad: float32 [8, 16384, 768], P('dp', 'seq')
The draws below stay inside these ranges and needn't reach their ends.
All inputs are finite; a program needn't handle non-finite values.
Results may differ from the reference program's by a relative error of at most 0.025.
Values may be sent and summed in bfloat16 or wider, within the bound.
A program may use at most 64 MiB of HBM per device.

```python
import math
import jax
import jax.numpy as jnp
from jax import lax

HEADS = 12
HEAD_DIM = 64
D = 768
BLOCK = 16
WINDOW = 1024
TOK_DEV = 256
LEVELS = 16
IMP_MAX = 8
SEQLEN = 16384
NBLOCKS = 1024
BATCH = 8


def draw_clean(key, part):
    return jnp.clip(jax.random.normal(key, (BATCH, SEQLEN, D), jnp.float32), -4.0, 4.0).astype(jnp.bfloat16)


def set_ends(drawn, own_key, smallest, high):
    extent = drawn.shape
    spot = [jax.random.randint(jax.random.fold_in(own_key, axis), (), 0, extent[axis]) for axis in range(len(extent))]
    drawn = drawn.at[tuple(spot)].set(smallest)
    longest = extent.index(max(extent))
    spot[longest] = (spot[longest] + 1) % extent[longest]
    return drawn.at[tuple(spot)].set(high)


def steps_of(key, dims, pieces, low, largest):
    def one(dim, shards_of):
        steps = jax.random.uniform(jax.random.fold_in(jax.random.fold_in(key, 6), dim), (shards_of,), jnp.float32, low / len(pieces), largest / len(pieces))
        return jnp.repeat(jnp.exp(steps), dims[dim] // shards_of).reshape((-1,) + (1,) * (len(dims) - dim - 1))

    gain = one(*pieces[0])
    for cut in pieces[1:]:
        gain = gain * one(*cut)
    return gain


def scatter_about(own_key, shape, scale, most, cuts=(), held_as=jnp.bfloat16):
    gain = steps_of(own_key, shape, cuts, -0.22, 0.18) if cuts else 1.0
    array = jax.random.normal(own_key, shape, jnp.float32) * scale * gain
    return jnp.minimum(jnp.maximum(array, -most), most).astype(held_as)


def setup_inputs(seed: int = 0) -> dict:
    splits = jax.random.split(jax.random.key(seed), 10)
    clean = draw_clean(jax.random.fold_in(splits[9], 71), 0)
    out_cot = scatter_about(splits[1], (BATCH, SEQLEN, D), 1.0, 6.0, ((0, 8), (1, 64)))
    mask_bits = set_ends(jax.random.randint(splits[2], (BATCH, NBLOCKS), 0, 65536), jax.random.fold_in(splits[2], 1), 0, 65535).astype(jnp.int32)
    levels = set_ends(jax.random.randint(splits[3], (BATCH, NBLOCKS), 1, LEVELS + 1), jax.random.fold_in(splits[3], 1), 1, LEVELS).astype(jnp.int32)
    importance = set_ends(jax.random.randint(splits[4], (BATCH, NBLOCKS, 2), 1, IMP_MAX + 1), jax.random.fold_in(splits[4], 1), 1, IMP_MAX).astype(jnp.int32)
    w_query = scatter_about(splits[5], (D, D), D ** -0.5, 0.21875)
    w_key = scatter_about(splits[6], (D, D), D ** -0.5, 0.21875)
    w_value = scatter_about(splits[7], (D, D), D ** -0.5, 0.21875)
    mask_embed = scatter_about(splits[8], (D,), 1.0, 6.0)
    return {"clean": clean, "out_cot": out_cot, "mask_bits": mask_bits, "levels": levels, "importance": importance, "w_query": w_query, "w_key": w_key, "w_value": w_value, "mask_embed": mask_embed}


EPS = 1e-06
CLIP = 0.25

def heads_of(rows):
    return rows.reshape(rows.shape[0], HEADS, HEAD_DIM).astype(jnp.float32)

def one_sequence(items, w_query, w_key, w_value, mask_embed):
    clean, cotangent, bits_row, level_row, ratio_row = items
    length = clean.shape[0]
    width = clean.shape[1]
    scale = 1.0 / math.sqrt(HEAD_DIM)
    place = jnp.arange(length, dtype=jnp.int32)
    block = place // BLOCK
    within = place % BLOCK
    bits = jnp.right_shift(bits_row[block], within) & 1
    masked = bits == 1
    noisy = jnp.where(masked[:, None], mask_embed[None, :], clean)
    key_clean = jnp.dot(clean, w_key, preferred_element_type=jnp.float32).astype(jnp.bfloat16)
    value_clean = jnp.dot(clean, w_value, preferred_element_type=jnp.float32).astype(jnp.bfloat16)
    query = jnp.dot(noisy, w_query, preferred_element_type=jnp.float32).astype(jnp.bfloat16)
    key_noisy = jnp.dot(noisy, w_key, preferred_element_type=jnp.float32).astype(jnp.bfloat16)
    value_noisy = jnp.dot(noisy, w_value, preferred_element_type=jnp.float32).astype(jnp.bfloat16)
    level_f = level_row.astype(jnp.float32)
    ratio_f = ratio_row.astype(jnp.float32)
    block_weight = LEVELS / level_f * (ratio_f[:, 0] / ratio_f[:, 1])
    token_weight = block_weight[block] * bits.astype(jnp.float32)
    grad_out = (cotangent.astype(jnp.float32) * token_weight[:, None]).astype(jnp.bfloat16)
    front = jnp.zeros((WINDOW, width), jnp.bfloat16)
    key_pad = jnp.concatenate([front, key_clean], axis=0)
    value_pad = jnp.concatenate([front, value_clean], axis=0)
    slab = WINDOW + TOK_DEV
    offsets = jnp.arange(slab, dtype=jnp.int32) - WINDOW
    local = jnp.arange(TOK_DEV, dtype=jnp.int32)
    local_block = local // BLOCK
    allow_noisy = local_block[None, :] == local_block[:, None]

    def tile(carry, index):
        key_grad, value_grad = carry
        start = (index * TOK_DEV).astype(jnp.int32)
        query_heads = heads_of(lax.dynamic_slice_in_dim(query, start, TOK_DEV, 0))
        nkey_heads = heads_of(lax.dynamic_slice_in_dim(key_noisy, start, TOK_DEV, 0))
        nvalue_heads = heads_of(lax.dynamic_slice_in_dim(value_noisy, start, TOK_DEV, 0))
        grad_rows = lax.dynamic_slice_in_dim(grad_out, start, TOK_DEV, 0)
        grad_heads = heads_of(grad_rows)
        key_heads = heads_of(lax.dynamic_slice_in_dim(key_pad, start, slab, 0))
        value_heads = heads_of(lax.dynamic_slice_in_dim(value_pad, start, slab, 0))
        key_pos = start + offsets
        q_start = (start + local) // BLOCK * BLOCK
        allow_clean = (key_pos[None, :] < q_start[:, None]) & (key_pos[None, :] >= q_start[:, None] - WINDOW) & (key_pos[None, :] >= 0)
        score_clean = jnp.einsum('qhe,khe->hqk', query_heads, key_heads) * scale
        score_noisy = jnp.einsum('qhe,khe->hqk', query_heads, nkey_heads) * scale
        score_clean = jnp.where(allow_clean[None], score_clean, -jnp.inf)
        score_noisy = jnp.where(allow_noisy[None], score_noisy, -jnp.inf)
        peak = jnp.maximum(lax.optimization_barrier(jnp.max(score_clean, axis=-1)), lax.optimization_barrier(jnp.max(score_noisy, axis=-1)))
        exp_clean = jnp.where(allow_clean[None], jnp.exp(score_clean - peak[..., None]), 0.0)
        exp_noisy = jnp.where(allow_noisy[None], jnp.exp(score_noisy - peak[..., None]), 0.0)
        denom = lax.optimization_barrier(jnp.sum(exp_clean, axis=-1)) + lax.optimization_barrier(jnp.sum(exp_noisy, axis=-1))
        prob_clean = exp_clean / denom[..., None]
        prob_noisy = exp_noisy / denom[..., None]
        weight_clean = prob_clean.astype(jnp.bfloat16).astype(jnp.float32)
        weight_noisy = prob_noisy.astype(jnp.bfloat16).astype(jnp.float32)
        mixed = jnp.einsum('hqk,khe->qhe', weight_clean, value_heads)
        mixed = mixed + jnp.einsum('hqk,khe->qhe', weight_noisy, nvalue_heads)
        attn_tile = mixed.reshape(TOK_DEV, width).astype(jnp.bfloat16)
        delta = lax.optimization_barrier(jnp.sum((grad_rows.astype(jnp.float32) * attn_tile.astype(jnp.float32)).reshape(TOK_DEV, HEADS, HEAD_DIM), axis=-1))
        dprob = jnp.einsum('qhe,khe->hqk', grad_heads, value_heads)
        dscore = (prob_clean * (dprob - delta.T[:, :, None]) * scale).astype(jnp.bfloat16).astype(jnp.float32)
        dkey = jnp.einsum('hqk,qhe->khe', dscore, query_heads).reshape(slab, width)
        dvalue = jnp.einsum('hqk,qhe->khe', weight_clean, grad_heads).reshape(slab, width)
        old_key = lax.dynamic_slice_in_dim(key_grad, start, slab, 0)
        old_value = lax.dynamic_slice_in_dim(value_grad, start, slab, 0)
        key_grad = lax.dynamic_update_slice_in_dim(key_grad, old_key + dkey, start, 0)
        value_grad = lax.dynamic_update_slice_in_dim(value_grad, old_value + dvalue, start, 0)
        return ((key_grad, value_grad), attn_tile)
    zeros = jnp.zeros((WINDOW + length, width), jnp.float32)
    tiles = jnp.arange(length // TOK_DEV, dtype=jnp.int32)
    (key_grad, value_grad), attn_tiles = lax.scan(tile, (zeros, zeros), tiles)
    attn_rows = attn_tiles.reshape(length, width)
    raw = jnp.dot(key_grad[WINDOW:], w_key.astype(jnp.float32).T, precision=lax.Precision.HIGHEST)
    raw = raw + jnp.dot(value_grad[WINDOW:], w_value.astype(jnp.float32).T, precision=lax.Precision.HIGHEST)
    return (attn_rows, raw)

def reference(clean, out_cot, mask_bits, levels, importance, w_query, w_key, w_value, mask_embed):

    def per_sequence(items):
        return one_sequence(items, w_query, w_key, w_value, mask_embed)
    attn_out, raw = lax.map(per_sequence, (clean, out_cot, mask_bits, levels, importance))
    rms = jnp.sqrt(jnp.mean(raw * raw) + EPS)
    factor = jnp.minimum(1.0, CLIP / rms)
    return (attn_out, raw * factor)
```

```python
import functools
import math

import jax
import jax.numpy as jnp
from jax import lax
from jax.sharding import PartitionSpec as P
from jax.experimental import pallas as pl
from jax.experimental.pallas import tpu as pltpu

HEADS = 12
HEAD_DIM = 64
BLOCK = 16
WINDOW = 1024
LEVELS = 16


EPS = 1e-06
CLIP = 0.25


def from_behind(block, axis, distance):
    devices = range(lax.axis_size(axis))
    route = [(i - distance, i) for i in devices if i - distance in devices]
    return lax.ppermute(block, axis, route)


def group_stages(axes):
    stages = []
    for axis in axes:
        rest, stride = lax.axis_size(axis), 1
        while rest > 1:
            size = max(g for g in range(1, 9) if rest % g == 0)
            stages.append((axis, stride, size))
            stride, rest = stride * size, rest // size
    return stages


def stage_peer(axis, stride, size, offset):
    index = lax.axis_index(axis)
    digit = (index // stride) % size
    return index + ((digit + offset) % size - digit) * stride


def device_of(axes, axis, peer):
    return tuple(peer if name == axis else lax.axis_index(name) for name in axes)


def total_kernel(axes, stages, part_ref, out_ref, slots, send_sems, recv_sems):
    barrier = pltpu.get_barrier_semaphore()
    greeted = 0
    for axis, stride, size in stages:
        for offset in range(1, size):
            peer = stage_peer(axis, stride, size, offset)
            pl.semaphore_signal(
                barrier, 1, device_id=device_of(axes, axis, peer),
                device_id_type=pl.DeviceIdType.MESH,
            )
            greeted += 1
    pl.semaphore_wait(barrier, greeted)
    current = part_ref[...]
    for number, (axis, stride, size) in enumerate(stages):
        digit = (lax.axis_index(axis) // stride) % size
        slots[number, digit] = current
        copies = []
        for offset in range(1, size):
            peer = stage_peer(axis, stride, size, offset)
            copy = pltpu.make_async_remote_copy(
                src_ref=slots.at[number, digit],
                dst_ref=slots.at[number, digit],
                send_sem=send_sems.at[number, offset],
                recv_sem=recv_sems.at[number, offset],
                device_id=device_of(axes, axis, peer),
                device_id_type=pl.DeviceIdType.MESH,
            )
            copy.start()
            copies.append(copy)
        for copy in copies:
            copy.wait()
        current = slots[number, 0]
        for member in range(1, size):
            current = current + slots[number, member]
    out_ref[...] = current


def global_total(value, axes):
    stages = group_stages(axes)
    widest = max(size for _, _, size in stages)
    part = jnp.broadcast_to(value.astype(jnp.float32), (8, 128))
    summed = pl.pallas_call(
        functools.partial(total_kernel, axes, stages),
        out_shape=jax.ShapeDtypeStruct((8, 128), jnp.float32),
        in_specs=[pl.BlockSpec(memory_space=pltpu.VMEM)],
        out_specs=pl.BlockSpec(memory_space=pltpu.VMEM),
        scratch_shapes=[
            pltpu.VMEM((len(stages), widest, 8, 128), jnp.float32),
            pltpu.SemaphoreType.DMA((len(stages), widest)),
            pltpu.SemaphoreType.DMA((len(stages), widest)),
        ],
        compiler_params=pltpu.CompilerParams(collective_id=0, has_side_effects=True),
    )(part)
    return summed[0, 0]


def to_heads(rows):
    return rows.reshape(rows.shape[0], HEADS, HEAD_DIM).transpose(1, 0, 2)


def from_heads(stacked):
    return stacked.transpose(1, 0, 2).reshape(stacked.shape[1], HEADS * HEAD_DIM)


def forward_head(
    query_h, key_h, value_h, nkey_h, nvalue_h, grad_h, allow_clean, allow_noisy, scale
):
    score_clean = (
        jnp.einsum("qe,ke->qk", query_h, key_h, preferred_element_type=jnp.float32) * scale
    )
    score_noisy = (
        jnp.einsum("qe,ke->qk", query_h, nkey_h, preferred_element_type=jnp.float32) * scale
    )
    score_clean = jnp.where(allow_clean, score_clean, -jnp.inf)
    score_noisy = jnp.where(allow_noisy, score_noisy, -jnp.inf)
    peak = jnp.maximum(jnp.max(score_clean, axis=-1), jnp.max(score_noisy, axis=-1))
    exp_clean = jnp.where(allow_clean, jnp.exp(score_clean - peak[:, None]), 0.0)
    exp_noisy = jnp.where(allow_noisy, jnp.exp(score_noisy - peak[:, None]), 0.0)
    denom = jnp.sum(exp_clean, axis=-1) + jnp.sum(exp_noisy, axis=-1)
    prob_clean = exp_clean / denom[:, None]
    prob_noisy = exp_noisy / denom[:, None]
    weight_clean = prob_clean.astype(jnp.bfloat16)
    weight_noisy = prob_noisy.astype(jnp.bfloat16)
    mixed = jnp.einsum("qk,ke->qe", weight_clean, value_h, preferred_element_type=jnp.float32)
    mixed = mixed + jnp.einsum(
        "qk,ke->qe", weight_noisy, nvalue_h, preferred_element_type=jnp.float32
    )
    out_h = mixed.astype(jnp.bfloat16)
    delta = jnp.sum(grad_h.astype(jnp.float32) * out_h.astype(jnp.float32), axis=-1)
    return (out_h, prob_clean, weight_clean, peak, denom, delta)


def on_device(clean, out_cot, mask_bits, levels, importance, w_query, w_key, w_value, mask_embed):
    clean_rows = clean[0]
    cotangent = out_cot[0]
    tok_count = clean_rows.shape[0]
    width = clean_rows.shape[1]
    span = WINDOW // tok_count
    scale = 1.0 / math.sqrt(HEAD_DIM)
    position = lax.axis_index("seq") * tok_count
    local = jnp.arange(tok_count, dtype=jnp.int32)
    local_block = local // BLOCK
    within = local % BLOCK
    bits = jnp.right_shift(mask_bits[0][local_block], within) & 1
    masked = bits == 1
    noisy = jnp.where(masked[:, None], mask_embed[None, :], clean_rows)
    query = jnp.dot(noisy, w_query, preferred_element_type=jnp.float32).astype(jnp.bfloat16)
    key_noisy = jnp.dot(noisy, w_key, preferred_element_type=jnp.float32).astype(jnp.bfloat16)
    value_noisy = jnp.dot(noisy, w_value, preferred_element_type=jnp.float32).astype(jnp.bfloat16)
    key_wide = w_key.astype(jnp.float32).T
    value_wide = w_value.astype(jnp.float32).T
    key_mine = jnp.dot(clean_rows, w_key, preferred_element_type=jnp.float32).astype(jnp.bfloat16)
    value_mine = jnp.dot(clean_rows, w_value, preferred_element_type=jnp.float32).astype(
        jnp.bfloat16
    )
    carried = jnp.stack([key_mine, value_mine])
    collected = [carried]
    for step in range(span):
        carried = from_behind(carried, "seq", 1)
        collected.insert(0, carried)
    window_kv = jnp.concatenate(collected, axis=1)
    key_clean = window_kv[0]
    value_clean = window_kv[1]
    context = key_clean.shape[0]
    ctx_pos = position - span * tok_count + jnp.arange(context, dtype=jnp.int32)
    q_start = (position + local) // BLOCK * BLOCK
    allow_clean = (
        (ctx_pos[None, :] < q_start[:, None])
        & (ctx_pos[None, :] >= q_start[:, None] - WINDOW)
        & (ctx_pos[None, :] >= 0)
    )
    allow_noisy = local_block[None, :] == local_block[:, None]
    level_f = levels[0].astype(jnp.float32)
    ratio_f = importance[0].astype(jnp.float32)
    block_weight = LEVELS / level_f * (ratio_f[:, 0] / ratio_f[:, 1])
    token_weight = block_weight[local_block] * bits.astype(jnp.float32)
    grad_out = (cotangent.astype(jnp.float32) * token_weight[:, None]).astype(jnp.bfloat16)
    head_inputs = (
        to_heads(query),
        to_heads(key_clean),
        to_heads(value_clean),
        to_heads(key_noisy),
        to_heads(value_noisy),
        to_heads(grad_out),
    )

    def full_pass(items):
        query_h, key_h, value_h, nkey_h, nvalue_h, grad_h = items
        out_h, prob_clean, weight_clean, peak, denom, delta = forward_head(
            query_h, key_h, value_h, nkey_h, nvalue_h, grad_h, allow_clean, allow_noisy, scale
        )
        dprob = jnp.einsum("qe,ke->qk", grad_h, value_h, preferred_element_type=jnp.float32)
        dscore = (prob_clean * (dprob - delta[:, None]) * scale).astype(jnp.bfloat16)
        dkey_h = jnp.einsum("qk,qe->ke", dscore, query_h, preferred_element_type=jnp.float32)
        dvalue_h = jnp.einsum("qk,qe->ke", weight_clean, grad_h, preferred_element_type=jnp.float32)
        return (out_h, dkey_h, dvalue_h)

    out_heads, dkey_heads, dvalue_heads = lax.map(full_pass, head_inputs)
    terms = jnp.stack([from_heads(dkey_heads), from_heads(dvalue_heads)])
    running = terms[:, :tok_count]
    for step in range(span):
        running = from_behind(running, "seq", -1)
        running = running + terms[:, (step + 1) * tok_count : (step + 2) * tok_count]
    raw = jnp.dot(running[0], key_wide, precision=lax.Precision.HIGHEST)
    raw = raw + jnp.dot(running[1], value_wide, precision=lax.Precision.HIGHEST)
    attn_rows = from_heads(out_heads)
    squares = jnp.sum(raw * raw)
    total_squares = global_total(squares, ("dp", "seq"))
    entries = float(tok_count * width * lax.axis_size("dp") * lax.axis_size("seq"))
    rms = jnp.sqrt(total_squares / entries + EPS)
    factor = jnp.minimum(1.0, CLIP / rms)
    return (attn_rows[None], (raw * factor)[None])


def solution(mesh):
    in_specs = (
        P("dp", "seq", None),
        P("dp", "seq", None),
        P("dp", "seq"),
        P("dp", "seq"),
        P("dp", "seq", None),
        P(),
        P(),
        P(),
        P(),
    )
    out_specs = (P("dp", "seq", None), P("dp", "seq", None))
    return jax.shard_map(
        on_device, mesh=mesh, in_specs=in_specs, out_specs=out_specs, check_vma=False
    )
```

```python
import functools
import math

import jax
import jax.numpy as jnp
from jax import lax
from jax.sharding import PartitionSpec as P
from jax.experimental import pallas as pl
from jax.experimental.pallas import tpu as pltpu

HEADS = 12
HEAD_DIM = 64
BLOCK = 16
WINDOW = 1024
LEVELS = 16


EPS = 1e-06
CLIP = 0.25


def from_behind(block, axis, distance):
    devices = range(lax.axis_size(axis))
    route = [(i - distance, i) for i in devices if i - distance in devices]
    return lax.ppermute(block, axis, route)


def group_stages(axes):
    stages = []
    for axis in axes:
        rest, stride = lax.axis_size(axis), 1
        while rest > 1:
            size = max(g for g in range(1, 9) if rest % g == 0)
            stages.append((axis, stride, size))
            stride, rest = stride * size, rest // size
    return stages


def stage_peer(axis, stride, size, offset):
    index = lax.axis_index(axis)
    digit = (index // stride) % size
    return index + ((digit + offset) % size - digit) * stride


def device_of(axes, axis, peer):
    return tuple(peer if name == axis else lax.axis_index(name) for name in axes)


def total_kernel(axes, stages, part_ref, out_ref, slots, send_sems, recv_sems):
    barrier = pltpu.get_barrier_semaphore()
    greeted = 0
    for axis, stride, size in stages:
        for offset in range(1, size):
            peer = stage_peer(axis, stride, size, offset)
            pl.semaphore_signal(
                barrier, 1, device_id=device_of(axes, axis, peer),
                device_id_type=pl.DeviceIdType.MESH,
            )
            greeted += 1
    pl.semaphore_wait(barrier, greeted)
    current = part_ref[...]
    for number, (axis, stride, size) in enumerate(stages):
        digit = (lax.axis_index(axis) // stride) % size
        slots[number, digit] = current
        copies = []
        for offset in range(1, size):
            peer = stage_peer(axis, stride, size, offset)
            copy = pltpu.make_async_remote_copy(
                src_ref=slots.at[number, digit],
                dst_ref=slots.at[number, digit],
                send_sem=send_sems.at[number, offset],
                recv_sem=recv_sems.at[number, offset],
                device_id=device_of(axes, axis, peer),
                device_id_type=pl.DeviceIdType.MESH,
            )
            copy.start()
            copies.append(copy)
        for copy in copies:
            copy.wait()
        current = slots[number, 0]
        for member in range(1, size):
            current = current + slots[number, member]
    out_ref[...] = current


def global_total(value, axes):
    stages = group_stages(axes)
    widest = max(size for _, _, size in stages)
    part = jnp.broadcast_to(value.astype(jnp.float32), (8, 128))
    summed = pl.pallas_call(
        functools.partial(total_kernel, axes, stages),
        out_shape=jax.ShapeDtypeStruct((8, 128), jnp.float32),
        in_specs=[pl.BlockSpec(memory_space=pltpu.VMEM)],
        out_specs=pl.BlockSpec(memory_space=pltpu.VMEM),
        scratch_shapes=[
            pltpu.VMEM((len(stages), widest, 8, 128), jnp.float32),
            pltpu.SemaphoreType.DMA((len(stages), widest)),
            pltpu.SemaphoreType.DMA((len(stages), widest)),
        ],
        compiler_params=pltpu.CompilerParams(collective_id=0, has_side_effects=True),
    )(part)
    return summed[0, 0]


def to_heads(rows):
    return rows.reshape(rows.shape[0], HEADS, HEAD_DIM).transpose(1, 0, 2)


def from_heads(stacked):
    return stacked.transpose(1, 0, 2).reshape(stacked.shape[1], HEADS * HEAD_DIM)


def forward_head(
    query_h, key_h, value_h, nkey_h, nvalue_h, grad_h, allow_clean, allow_noisy, scale
):
    score_clean = (
        jnp.einsum("qe,ke->qk", query_h, key_h, preferred_element_type=jnp.float32) * scale
    )
    score_noisy = (
        jnp.einsum("qe,ke->qk", query_h, nkey_h, preferred_element_type=jnp.float32) * scale
    )
    score_clean = jnp.where(allow_clean, score_clean, -jnp.inf)
    score_noisy = jnp.where(allow_noisy, score_noisy, -jnp.inf)
    peak = jnp.maximum(jnp.max(score_clean, axis=-1), jnp.max(score_noisy, axis=-1))
    exp_clean = jnp.where(allow_clean, jnp.exp(score_clean - peak[:, None]), 0.0)
    exp_noisy = jnp.where(allow_noisy, jnp.exp(score_noisy - peak[:, None]), 0.0)
    denom = jnp.sum(exp_clean, axis=-1) + jnp.sum(exp_noisy, axis=-1)
    prob_clean = exp_clean / denom[:, None]
    prob_noisy = exp_noisy / denom[:, None]
    weight_clean = prob_clean.astype(jnp.bfloat16)
    weight_noisy = prob_noisy.astype(jnp.bfloat16)
    mixed = jnp.einsum("qk,ke->qe", weight_clean, value_h, preferred_element_type=jnp.float32)
    mixed = mixed + jnp.einsum(
        "qk,ke->qe", weight_noisy, nvalue_h, preferred_element_type=jnp.float32
    )
    out_h = mixed.astype(jnp.bfloat16)
    delta = jnp.sum(grad_h.astype(jnp.float32) * out_h.astype(jnp.float32), axis=-1)
    return (out_h, prob_clean, weight_clean, peak, denom, delta)


def attention_kernel(place_ref, q_ref, kc_ref, vc_ref, kn_ref, vn_ref, g_ref,
                     out_ref, dk_ref, dv_ref):
    scale = 1.0 / math.sqrt(HEAD_DIM)
    query = q_ref[0]
    key_clean = kc_ref[0]
    value_clean = vc_ref[0]
    grad = g_ref[0]
    rows, context = query.shape[0], key_clean.shape[0]
    row_block = lax.broadcasted_iota(jnp.int32, (rows, context), 0) // BLOCK * BLOCK
    col = lax.broadcasted_iota(jnp.int32, (rows, context), 1)
    allow_clean = (col >= row_block) & (col < row_block + WINDOW) & (col >= place_ref[0])
    own_row = lax.broadcasted_iota(jnp.int32, (rows, rows), 0) // BLOCK
    own_col = lax.broadcasted_iota(jnp.int32, (rows, rows), 1) // BLOCK
    allow_noisy = own_row == own_col
    contract = (((1,), (1,)), ((), ()))
    score_clean = lax.dot_general(query, key_clean, contract, preferred_element_type=jnp.float32) * scale
    score_noisy = lax.dot_general(query, kn_ref[0], contract, preferred_element_type=jnp.float32) * scale
    score_clean = jnp.where(allow_clean, score_clean, -jnp.inf)
    score_noisy = jnp.where(allow_noisy, score_noisy, -jnp.inf)
    peak = jnp.maximum(
        jnp.max(score_clean, axis=-1, keepdims=True), jnp.max(score_noisy, axis=-1, keepdims=True)
    )
    exp_clean = jnp.where(allow_clean, jnp.exp(score_clean - peak), 0.0)
    exp_noisy = jnp.where(allow_noisy, jnp.exp(score_noisy - peak), 0.0)
    denom = jnp.sum(exp_clean, axis=-1, keepdims=True) + jnp.sum(exp_noisy, axis=-1, keepdims=True)
    inverse = 1.0 / denom
    prob_clean = exp_clean * inverse
    weight_clean = prob_clean.astype(jnp.bfloat16)
    weight_noisy = (exp_noisy * inverse).astype(jnp.bfloat16)
    mixed = jnp.dot(weight_clean, value_clean, preferred_element_type=jnp.float32)
    mixed = mixed + jnp.dot(weight_noisy, vn_ref[0], preferred_element_type=jnp.float32)
    out_h = mixed.astype(jnp.bfloat16)
    out_ref[0] = out_h
    delta = jnp.sum(grad.astype(jnp.float32) * out_h.astype(jnp.float32), axis=-1, keepdims=True)
    dprob = lax.dot_general(grad, value_clean, contract, preferred_element_type=jnp.float32)
    dscore = (prob_clean * (dprob - delta) * scale).astype(jnp.bfloat16)
    lead = (((0,), (0,)), ((), ()))
    dk_ref[0] = lax.dot_general(dscore, query, lead, preferred_element_type=jnp.float32)
    dv_ref[0] = lax.dot_general(weight_clean, grad, lead, preferred_element_type=jnp.float32)


def attention_heads(place, query_h, key_h, value_h, nkey_h, nvalue_h, grad_h):
    heads, rows, dim = query_h.shape
    context = key_h.shape[1]
    row_spec = pl.BlockSpec((1, rows, dim), lambda h, place: (h, 0, 0))
    ctx_spec = pl.BlockSpec((1, context, dim), lambda h, place: (h, 0, 0))
    flops = heads * 2 * dim * (5 * rows * context + 3 * rows * rows)
    return pl.pallas_call(
        attention_kernel,
        out_shape=(
            jax.ShapeDtypeStruct((heads, rows, dim), jnp.bfloat16),
            jax.ShapeDtypeStruct((heads, context, dim), jnp.float32),
            jax.ShapeDtypeStruct((heads, context, dim), jnp.float32),
        ),
        grid_spec=pltpu.PrefetchScalarGridSpec(
            num_scalar_prefetch=1,
            grid=(heads,),
            in_specs=[row_spec, ctx_spec, ctx_spec, row_spec, row_spec, row_spec],
            out_specs=[row_spec, ctx_spec, ctx_spec],
        ),
        cost_estimate=pl.CostEstimate(
            flops=flops,
            transcendentals=heads * rows * (context + rows),
            bytes_accessed=heads * dim * (8 * rows + 4 * context + 8 * context),
        ),
    )(place, query_h, key_h, value_h, nkey_h, nvalue_h, grad_h)


def on_device(clean, out_cot, mask_bits, levels, importance, w_query, w_key, w_value, mask_embed):
    clean_rows = clean[0]
    cotangent = out_cot[0]
    tok_count = clean_rows.shape[0]
    width = clean_rows.shape[1]
    span = WINDOW // tok_count
    scale = 1.0 / math.sqrt(HEAD_DIM)
    position = lax.axis_index("seq") * tok_count
    local = jnp.arange(tok_count, dtype=jnp.int32)
    local_block = local // BLOCK
    within = local % BLOCK
    bits = jnp.right_shift(mask_bits[0][local_block], within) & 1
    masked = bits == 1
    noisy = jnp.where(masked[:, None], mask_embed[None, :], clean_rows)
    query = jnp.dot(noisy, w_query, preferred_element_type=jnp.float32).astype(jnp.bfloat16)
    key_noisy = jnp.dot(noisy, w_key, preferred_element_type=jnp.float32).astype(jnp.bfloat16)
    value_noisy = jnp.dot(noisy, w_value, preferred_element_type=jnp.float32).astype(jnp.bfloat16)
    key_wide = w_key.astype(jnp.float32).T
    value_wide = w_value.astype(jnp.float32).T
    key_mine = jnp.dot(clean_rows, w_key, preferred_element_type=jnp.float32).astype(jnp.bfloat16)
    value_mine = jnp.dot(clean_rows, w_value, preferred_element_type=jnp.float32).astype(
        jnp.bfloat16
    )
    carried = jnp.stack([key_mine, value_mine])
    collected = [carried]
    for step in range(span):
        carried = from_behind(carried, "seq", 1)
        collected.insert(0, carried)
    window_kv = jnp.concatenate(collected, axis=1)
    key_clean = window_kv[0]
    value_clean = window_kv[1]
    context = key_clean.shape[0]
    ctx_pos = position - span * tok_count + jnp.arange(context, dtype=jnp.int32)
    q_start = (position + local) // BLOCK * BLOCK
    allow_clean = (
        (ctx_pos[None, :] < q_start[:, None])
        & (ctx_pos[None, :] >= q_start[:, None] - WINDOW)
        & (ctx_pos[None, :] >= 0)
    )
    allow_noisy = local_block[None, :] == local_block[:, None]
    level_f = levels[0].astype(jnp.float32)
    ratio_f = importance[0].astype(jnp.float32)
    block_weight = LEVELS / level_f * (ratio_f[:, 0] / ratio_f[:, 1])
    token_weight = block_weight[local_block] * bits.astype(jnp.float32)
    grad_out = (cotangent.astype(jnp.float32) * token_weight[:, None]).astype(jnp.bfloat16)
    head_inputs = (
        to_heads(query),
        to_heads(key_clean),
        to_heads(value_clean),
        to_heads(key_noisy),
        to_heads(value_noisy),
        to_heads(grad_out),
    )

    place = jnp.reshape(span * tok_count - position, (1,)).astype(jnp.int32)
    out_heads, dkey_heads, dvalue_heads = attention_heads(place, *head_inputs)
    terms = jnp.stack([from_heads(dkey_heads), from_heads(dvalue_heads)])
    running = terms[:, :tok_count]
    for step in range(span):
        running = from_behind(running, "seq", -1)
        running = running + terms[:, (step + 1) * tok_count : (step + 2) * tok_count]
    raw = jnp.dot(running[0], key_wide, precision=lax.Precision.HIGHEST)
    raw = raw + jnp.dot(running[1], value_wide, precision=lax.Precision.HIGHEST)
    attn_rows = from_heads(out_heads)
    squares = jnp.sum(raw * raw)
    total_squares = global_total(squares, ("dp", "seq"))
    entries = float(tok_count * width * lax.axis_size("dp") * lax.axis_size("seq"))
    rms = jnp.sqrt(total_squares / entries + EPS)
    factor = jnp.minimum(1.0, CLIP / rms)
    return (attn_rows[None], (raw * factor)[None])


def solution(mesh):
    in_specs = (
        P("dp", "seq", None),
        P("dp", "seq", None),
        P("dp", "seq"),
        P("dp", "seq"),
        P("dp", "seq", None),
        P(),
        P(),
        P(),
        P(),
    )
    out_specs = (P("dp", "seq", None), P("dp", "seq", None))
    return jax.shard_map(
        on_device, mesh=mesh, in_specs=in_specs, out_specs=out_specs, check_vma=False
    )
```

```python
import functools
import math

import jax
import jax.numpy as jnp
from jax import lax
from jax.sharding import PartitionSpec as P
from jax.experimental import pallas as pl
from jax.experimental.pallas import tpu as pltpu

HEADS = 12
HEAD_DIM = 64
BLOCK = 16
WINDOW = 1024
LEVELS = 16


EPS = 1e-06
CLIP = 0.25


def from_behind(block, axis, distance):
    devices = range(lax.axis_size(axis))
    route = [(i - distance, i) for i in devices if i - distance in devices]
    return lax.ppermute(block, axis, route)


def group_stages(axes):
    stages = []
    for axis in axes:
        rest, stride = lax.axis_size(axis), 1
        while rest > 1:
            size = max(g for g in range(1, 9) if rest % g == 0)
            stages.append((axis, stride, size))
            stride, rest = stride * size, rest // size
    return stages


def stage_peer(axis, stride, size, offset):
    index = lax.axis_index(axis)
    digit = (index // stride) % size
    return index + ((digit + offset) % size - digit) * stride


def device_of(axes, axis, peer):
    return tuple(peer if name == axis else lax.axis_index(name) for name in axes)


def total_kernel(axes, stages, part_ref, out_ref, slots, send_sems, recv_sems):
    barrier = pltpu.get_barrier_semaphore()
    greeted = 0
    for axis, stride, size in stages:
        for offset in range(1, size):
            peer = stage_peer(axis, stride, size, offset)
            pl.semaphore_signal(
                barrier, 1, device_id=device_of(axes, axis, peer),
                device_id_type=pl.DeviceIdType.MESH,
            )
            greeted += 1
    pl.semaphore_wait(barrier, greeted)
    current = part_ref[...]
    for number, (axis, stride, size) in enumerate(stages):
        digit = (lax.axis_index(axis) // stride) % size
        slots[number, digit] = current
        copies = []
        for offset in range(1, size):
            peer = stage_peer(axis, stride, size, offset)
            copy = pltpu.make_async_remote_copy(
                src_ref=slots.at[number, digit],
                dst_ref=slots.at[number, digit],
                send_sem=send_sems.at[number, offset],
                recv_sem=recv_sems.at[number, offset],
                device_id=device_of(axes, axis, peer),
                device_id_type=pl.DeviceIdType.MESH,
            )
            copy.start()
            copies.append(copy)
        for copy in copies:
            copy.wait()
        current = slots[number, 0]
        for member in range(1, size):
            current = current + slots[number, member]
    out_ref[...] = current


def global_total(value, axes):
    stages = group_stages(axes)
    widest = max(size for _, _, size in stages)
    part = jnp.broadcast_to(value.astype(jnp.float32), (8, 128))
    summed = pl.pallas_call(
        functools.partial(total_kernel, axes, stages),
        out_shape=jax.ShapeDtypeStruct((8, 128), jnp.float32),
        in_specs=[pl.BlockSpec(memory_space=pltpu.VMEM)],
        out_specs=pl.BlockSpec(memory_space=pltpu.VMEM),
        scratch_shapes=[
            pltpu.VMEM((len(stages), widest, 8, 128), jnp.float32),
            pltpu.SemaphoreType.DMA((len(stages), widest)),
            pltpu.SemaphoreType.DMA((len(stages), widest)),
        ],
        compiler_params=pltpu.CompilerParams(collective_id=0, has_side_effects=True),
    )(part)
    return summed[0, 0]


def to_heads(rows):
    return rows.reshape(rows.shape[0], HEADS, HEAD_DIM).transpose(1, 0, 2)


def from_heads(stacked):
    return stacked.transpose(1, 0, 2).reshape(stacked.shape[1], HEADS * HEAD_DIM)


def forward_head(
    query_h, key_h, value_h, nkey_h, nvalue_h, grad_h, allow_clean, allow_noisy, scale
):
    score_clean = (
        jnp.einsum("qe,ke->qk", query_h, key_h, preferred_element_type=jnp.float32) * scale
    )
    score_noisy = (
        jnp.einsum("qe,ke->qk", query_h, nkey_h, preferred_element_type=jnp.float32) * scale
    )
    score_clean = jnp.where(allow_clean, score_clean, -jnp.inf)
    score_noisy = jnp.where(allow_noisy, score_noisy, -jnp.inf)
    peak = jnp.maximum(jnp.max(score_clean, axis=-1), jnp.max(score_noisy, axis=-1))
    exp_clean = jnp.where(allow_clean, jnp.exp(score_clean - peak[:, None]), 0.0)
    exp_noisy = jnp.where(allow_noisy, jnp.exp(score_noisy - peak[:, None]), 0.0)
    denom = jnp.sum(exp_clean, axis=-1) + jnp.sum(exp_noisy, axis=-1)
    prob_clean = exp_clean / denom[:, None]
    prob_noisy = exp_noisy / denom[:, None]
    weight_clean = prob_clean.astype(jnp.bfloat16)
    weight_noisy = prob_noisy.astype(jnp.bfloat16)
    mixed = jnp.einsum("qk,ke->qe", weight_clean, value_h, preferred_element_type=jnp.float32)
    mixed = mixed + jnp.einsum(
        "qk,ke->qe", weight_noisy, nvalue_h, preferred_element_type=jnp.float32
    )
    out_h = mixed.astype(jnp.bfloat16)
    delta = jnp.sum(grad_h.astype(jnp.float32) * out_h.astype(jnp.float32), axis=-1)
    return (out_h, prob_clean, weight_clean, peak, denom, delta)


def attention_kernel(place_ref, q_ref, kc_ref, vc_ref, kn_ref, vn_ref, g_ref,
                     out_ref, dk_ref, dv_ref):
    scale = 1.0 / math.sqrt(HEAD_DIM)
    query = q_ref[0]
    key_clean = kc_ref[0]
    value_clean = vc_ref[0]
    grad = g_ref[0]
    rows, context = query.shape[0], key_clean.shape[0]
    row_block = lax.broadcasted_iota(jnp.int32, (rows, context), 0) // BLOCK * BLOCK
    col = lax.broadcasted_iota(jnp.int32, (rows, context), 1)
    allow_clean = (col >= row_block) & (col < row_block + WINDOW) & (col >= place_ref[0])
    own_row = lax.broadcasted_iota(jnp.int32, (rows, rows), 0) // BLOCK
    own_col = lax.broadcasted_iota(jnp.int32, (rows, rows), 1) // BLOCK
    allow_noisy = own_row == own_col
    contract = (((1,), (1,)), ((), ()))
    score_clean = lax.dot_general(query, key_clean, contract, preferred_element_type=jnp.float32) * scale
    score_noisy = lax.dot_general(query, kn_ref[0], contract, preferred_element_type=jnp.float32) * scale
    score_clean = jnp.where(allow_clean, score_clean, -jnp.inf)
    score_noisy = jnp.where(allow_noisy, score_noisy, -jnp.inf)
    peak = jnp.maximum(
        jnp.max(score_clean, axis=-1, keepdims=True), jnp.max(score_noisy, axis=-1, keepdims=True)
    )
    exp_clean = jnp.where(allow_clean, jnp.exp(score_clean - peak), 0.0)
    exp_noisy = jnp.where(allow_noisy, jnp.exp(score_noisy - peak), 0.0)
    denom = jnp.sum(exp_clean, axis=-1, keepdims=True) + jnp.sum(exp_noisy, axis=-1, keepdims=True)
    inverse = 1.0 / denom
    prob_clean = exp_clean * inverse
    weight_clean = prob_clean.astype(jnp.bfloat16)
    weight_noisy = (exp_noisy * inverse).astype(jnp.bfloat16)
    mixed = jnp.dot(weight_clean, value_clean, preferred_element_type=jnp.float32)
    mixed = mixed + jnp.dot(weight_noisy, vn_ref[0], preferred_element_type=jnp.float32)
    out_h = mixed.astype(jnp.bfloat16)
    out_ref[0] = out_h
    delta = jnp.sum(grad.astype(jnp.float32) * out_h.astype(jnp.float32), axis=-1, keepdims=True)
    dprob = lax.dot_general(grad, value_clean, contract, preferred_element_type=jnp.float32)
    dscore = (prob_clean * (dprob - delta) * scale).astype(jnp.bfloat16)
    lead = (((0,), (0,)), ((), ()))
    dk_ref[0] = lax.dot_general(dscore, query, lead, preferred_element_type=jnp.float32)
    dv_ref[0] = lax.dot_general(weight_clean, grad, lead, preferred_element_type=jnp.float32)


def attention_heads(place, query_h, key_h, value_h, nkey_h, nvalue_h, grad_h):
    heads, rows, dim = query_h.shape
    context = key_h.shape[1]
    row_spec = pl.BlockSpec((1, rows, dim), lambda h, place: (h, 0, 0))
    ctx_spec = pl.BlockSpec((1, context, dim), lambda h, place: (h, 0, 0))
    flops = heads * 2 * dim * (5 * rows * context + 3 * rows * rows)
    return pl.pallas_call(
        attention_kernel,
        out_shape=(
            jax.ShapeDtypeStruct((heads, rows, dim), jnp.bfloat16),
            jax.ShapeDtypeStruct((heads, context, dim), jnp.float32),
            jax.ShapeDtypeStruct((heads, context, dim), jnp.float32),
        ),
        grid_spec=pltpu.PrefetchScalarGridSpec(
            num_scalar_prefetch=1,
            grid=(heads,),
            in_specs=[row_spec, ctx_spec, ctx_spec, row_spec, row_spec, row_spec],
            out_specs=[row_spec, ctx_spec, ctx_spec],
        ),
        cost_estimate=pl.CostEstimate(
            flops=flops,
            transcendentals=heads * rows * (context + rows),
            bytes_accessed=heads * dim * (8 * rows + 4 * context + 8 * context),
        ),
    )(place, query_h, key_h, value_h, nkey_h, nvalue_h, grad_h)


def project(rows, weight):
    high = rows.astype(jnp.bfloat16)
    low = (rows - high.astype(jnp.float32)).astype(jnp.bfloat16)
    contract = (((1,), (1,)), ((), ()))
    product = lax.dot_general(high, weight, contract, preferred_element_type=jnp.float32)
    return product + lax.dot_general(low, weight, contract, preferred_element_type=jnp.float32)


def on_device(clean, out_cot, mask_bits, levels, importance, w_query, w_key, w_value, mask_embed):
    clean_rows = clean[0]
    cotangent = out_cot[0]
    tok_count = clean_rows.shape[0]
    width = clean_rows.shape[1]
    span = WINDOW // tok_count
    scale = 1.0 / math.sqrt(HEAD_DIM)
    position = lax.axis_index("seq") * tok_count
    local = jnp.arange(tok_count, dtype=jnp.int32)
    local_block = local // BLOCK
    within = local % BLOCK
    bits = jnp.right_shift(mask_bits[0][local_block], within) & 1
    masked = bits == 1
    noisy = jnp.where(masked[:, None], mask_embed[None, :], clean_rows)
    query = jnp.dot(noisy, w_query, preferred_element_type=jnp.float32).astype(jnp.bfloat16)
    key_noisy = jnp.dot(noisy, w_key, preferred_element_type=jnp.float32).astype(jnp.bfloat16)
    value_noisy = jnp.dot(noisy, w_value, preferred_element_type=jnp.float32).astype(jnp.bfloat16)
    carried = clean_rows
    collected = [carried]
    for step in range(span):
        carried = from_behind(carried, "seq", 1)
        collected.insert(0, carried)
    window_rows = jnp.concatenate(collected, axis=0)
    key_clean = jnp.dot(window_rows, w_key, preferred_element_type=jnp.float32).astype(jnp.bfloat16)
    value_clean = jnp.dot(window_rows, w_value, preferred_element_type=jnp.float32).astype(
        jnp.bfloat16
    )
    context = key_clean.shape[0]
    ctx_pos = position - span * tok_count + jnp.arange(context, dtype=jnp.int32)
    q_start = (position + local) // BLOCK * BLOCK
    allow_clean = (
        (ctx_pos[None, :] < q_start[:, None])
        & (ctx_pos[None, :] >= q_start[:, None] - WINDOW)
        & (ctx_pos[None, :] >= 0)
    )
    allow_noisy = local_block[None, :] == local_block[:, None]
    level_f = levels[0].astype(jnp.float32)
    ratio_f = importance[0].astype(jnp.float32)
    block_weight = LEVELS / level_f * (ratio_f[:, 0] / ratio_f[:, 1])
    token_weight = block_weight[local_block] * bits.astype(jnp.float32)
    grad_out = (cotangent.astype(jnp.float32) * token_weight[:, None]).astype(jnp.bfloat16)
    head_inputs = (
        to_heads(query),
        to_heads(key_clean),
        to_heads(value_clean),
        to_heads(key_noisy),
        to_heads(value_noisy),
        to_heads(grad_out),
    )

    place = jnp.reshape(span * tok_count - position, (1,)).astype(jnp.int32)
    out_heads, dkey_heads, dvalue_heads = attention_heads(place, *head_inputs)
    terms = project(from_heads(dkey_heads), w_key) + project(from_heads(dvalue_heads), w_value)
    running = terms[:tok_count]
    for step in range(span):
        running = from_behind(running.astype(jnp.bfloat16), "seq", -1).astype(jnp.float32)
        running = running + terms[(step + 1) * tok_count : (step + 2) * tok_count]
    raw = running
    attn_rows = from_heads(out_heads)
    squares = jnp.sum(raw * raw)
    total_squares = global_total(squares, ("dp", "seq"))
    entries = float(tok_count * width * lax.axis_size("dp") * lax.axis_size("seq"))
    rms = jnp.sqrt(total_squares / entries + EPS)
    factor = jnp.minimum(1.0, CLIP / rms)
    return (attn_rows[None], (raw * factor)[None])


def solution(mesh):
    in_specs = (
        P("dp", "seq", None),
        P("dp", "seq", None),
        P("dp", "seq"),
        P("dp", "seq"),
        P("dp", "seq", None),
        P(),
        P(),
        P(),
        P(),
    )
    out_specs = (P("dp", "seq", None), P("dp", "seq", None))
    return jax.shard_map(
        on_device, mesh=mesh, in_specs=in_specs, out_specs=out_specs, check_vma=False
    )
```

```python
import functools
import math

import jax
import jax.numpy as jnp
from jax import lax
from jax.sharding import PartitionSpec as P
from jax.experimental import pallas as pl
from jax.experimental.pallas import tpu as pltpu

HEADS = 12
HEAD_DIM = 64
BLOCK = 16
WINDOW = 1024
LEVELS = 16


EPS = 1e-06
CLIP = 0.25


def from_behind(block, axis, distance):
    devices = range(lax.axis_size(axis))
    route = [(i - distance, i) for i in devices if i - distance in devices]
    return lax.ppermute(block, axis, route)


def group_stages(axes):
    stages = []
    for axis in axes:
        rest, stride = lax.axis_size(axis), 1
        while rest > 1:
            size = max(g for g in range(1, 9) if rest % g == 0)
            stages.append((axis, stride, size))
            stride, rest = stride * size, rest // size
    return stages


def stage_peer(axis, stride, size, offset):
    index = lax.axis_index(axis)
    digit = (index // stride) % size
    return index + ((digit + offset) % size - digit) * stride


def device_of(axes, axis, peer):
    return tuple(peer if name == axis else lax.axis_index(name) for name in axes)


def total_kernel(axes, stages, part_ref, out_ref, slots, send_sems, recv_sems):
    barrier = pltpu.get_barrier_semaphore()
    greeted = 0
    for axis, stride, size in stages:
        for offset in range(1, size):
            peer = stage_peer(axis, stride, size, offset)
            pl.semaphore_signal(
                barrier, 1, device_id=device_of(axes, axis, peer),
                device_id_type=pl.DeviceIdType.MESH,
            )
            greeted += 1
    pl.semaphore_wait(barrier, greeted)
    current = part_ref[...]
    for number, (axis, stride, size) in enumerate(stages):
        digit = (lax.axis_index(axis) // stride) % size
        slots[number, digit] = current
        copies = []
        for offset in range(1, size):
            peer = stage_peer(axis, stride, size, offset)
            copy = pltpu.make_async_remote_copy(
                src_ref=slots.at[number, digit],
                dst_ref=slots.at[number, digit],
                send_sem=send_sems.at[number, offset],
                recv_sem=recv_sems.at[number, offset],
                device_id=device_of(axes, axis, peer),
                device_id_type=pl.DeviceIdType.MESH,
            )
            copy.start()
            copies.append(copy)
        for copy in copies:
            copy.wait()
        current = slots[number, 0]
        for member in range(1, size):
            current = current + slots[number, member]
    out_ref[...] = current


def global_total(value, axes):
    stages = group_stages(axes)
    widest = max(size for _, _, size in stages)
    part = jnp.broadcast_to(value.astype(jnp.float32), (8, 128))
    summed = pl.pallas_call(
        functools.partial(total_kernel, axes, stages),
        out_shape=jax.ShapeDtypeStruct((8, 128), jnp.float32),
        in_specs=[pl.BlockSpec(memory_space=pltpu.VMEM)],
        out_specs=pl.BlockSpec(memory_space=pltpu.VMEM),
        scratch_shapes=[
            pltpu.VMEM((len(stages), widest, 8, 128), jnp.float32),
            pltpu.SemaphoreType.DMA((len(stages), widest)),
            pltpu.SemaphoreType.DMA((len(stages), widest)),
        ],
        compiler_params=pltpu.CompilerParams(collective_id=0, has_side_effects=True),
    )(part)
    return summed[0, 0]


def attention_kernel(place_ref, q_ref, kc_ref, vc_ref, kn_ref, vn_ref, g_ref,
                     out_ref, dk_ref, dv_ref):
    scale = 1.0 / math.sqrt(HEAD_DIM)
    query = q_ref[...]
    key_clean = kc_ref[...]
    value_clean = vc_ref[...]
    key_noisy = kn_ref[...]
    value_noisy = vn_ref[...]
    grad = g_ref[...]
    rows, lanes = query.shape
    context = key_clean.shape[0]
    row_block = lax.broadcasted_iota(jnp.int32, (rows, context), 0) // BLOCK * BLOCK
    col = lax.broadcasted_iota(jnp.int32, (rows, context), 1)
    allow_clean = (col >= row_block) & (col < row_block + WINDOW) & (col >= place_ref[0])
    own_row = lax.broadcasted_iota(jnp.int32, (rows, rows), 0) // BLOCK
    own_col = lax.broadcasted_iota(jnp.int32, (rows, rows), 1) // BLOCK
    allow_noisy = own_row == own_col
    lane = lax.broadcasted_iota(jnp.int32, (1, lanes), 1) // HEAD_DIM
    contract = (((1,), (1,)), ((), ()))
    lead = (((0,), (0,)), ((), ()))
    zero = jnp.zeros((), jnp.bfloat16)
    outs, dks, dvs = [], [], []
    for head in range(lanes // HEAD_DIM):
        mine = lane == head
        query_h = jnp.where(mine, query, zero)
        grad_h = jnp.where(mine, grad, zero)
        score_clean = lax.dot_general(query_h, key_clean, contract, preferred_element_type=jnp.float32) * scale
        score_noisy = lax.dot_general(query_h, key_noisy, contract, preferred_element_type=jnp.float32) * scale
        score_clean = jnp.where(allow_clean, score_clean, -jnp.inf)
        score_noisy = jnp.where(allow_noisy, score_noisy, -jnp.inf)
        peak = jnp.maximum(
            jnp.max(score_clean, axis=-1, keepdims=True), jnp.max(score_noisy, axis=-1, keepdims=True)
        )
        exp_clean = jnp.where(allow_clean, jnp.exp(score_clean - peak), 0.0)
        exp_noisy = jnp.where(allow_noisy, jnp.exp(score_noisy - peak), 0.0)
        denom = jnp.sum(exp_clean, axis=-1, keepdims=True) + jnp.sum(exp_noisy, axis=-1, keepdims=True)
        inverse = 1.0 / denom
        prob_clean = exp_clean * inverse
        weight_clean = prob_clean.astype(jnp.bfloat16)
        weight_noisy = (exp_noisy * inverse).astype(jnp.bfloat16)
        mixed = jnp.dot(weight_clean, value_clean, preferred_element_type=jnp.float32)
        mixed = mixed + jnp.dot(weight_noisy, value_noisy, preferred_element_type=jnp.float32)
        out_h = mixed.astype(jnp.bfloat16)
        delta = jnp.sum(
            jnp.where(mine, grad.astype(jnp.float32) * out_h.astype(jnp.float32), 0.0),
            axis=-1, keepdims=True,
        )
        dprob = lax.dot_general(grad_h, value_clean, contract, preferred_element_type=jnp.float32)
        dscore = (prob_clean * (dprob - delta) * scale).astype(jnp.bfloat16)
        outs.append(out_h)
        dks.append(lax.dot_general(dscore, query, lead, preferred_element_type=jnp.float32))
        dvs.append(lax.dot_general(weight_clean, grad, lead, preferred_element_type=jnp.float32))
    out, dk, dv = outs[0], dks[0], dvs[0]
    for head in range(1, len(outs)):
        mine = lane == head
        out = jnp.where(mine, outs[head], out)
        dk = jnp.where(mine, dks[head], dk)
        dv = jnp.where(mine, dvs[head], dv)
    out_ref[...] = out
    dk_ref[...] = dk
    dv_ref[...] = dv


def attention_heads(place, query, key_clean, value_clean, key_noisy, value_noisy, grad):
    rows, width = query.shape
    context = key_clean.shape[0]
    lanes = 2 * HEAD_DIM
    pairs = width // lanes
    row_spec = pl.BlockSpec((rows, lanes), lambda p, place: (0, p))
    ctx_spec = pl.BlockSpec((context, lanes), lambda p, place: (0, p))
    flops = pairs * 2 * 2 * lanes * (5 * rows * context + 3 * rows * rows)
    return pl.pallas_call(
        attention_kernel,
        out_shape=(
            jax.ShapeDtypeStruct((rows, width), jnp.bfloat16),
            jax.ShapeDtypeStruct((context, width), jnp.float32),
            jax.ShapeDtypeStruct((context, width), jnp.float32),
        ),
        grid_spec=pltpu.PrefetchScalarGridSpec(
            num_scalar_prefetch=1,
            grid=(pairs,),
            in_specs=[row_spec, ctx_spec, ctx_spec, row_spec, row_spec, row_spec],
            out_specs=[row_spec, ctx_spec, ctx_spec],
        ),
        cost_estimate=pl.CostEstimate(
            flops=flops,
            transcendentals=width // HEAD_DIM * rows * (context + rows),
            bytes_accessed=width * (8 * rows + 4 * context + 8 * context),
        ),
    )(place, query, key_clean, value_clean, key_noisy, value_noisy, grad)


def project(rows, weight):
    high = rows.astype(jnp.bfloat16)
    low = (rows - high.astype(jnp.float32)).astype(jnp.bfloat16)
    contract = (((1,), (1,)), ((), ()))
    product = lax.dot_general(high, weight, contract, preferred_element_type=jnp.float32)
    return product + lax.dot_general(low, weight, contract, preferred_element_type=jnp.float32)


def on_device(clean, out_cot, mask_bits, levels, importance, w_query, w_key, w_value, mask_embed):
    clean_rows = clean[0]
    cotangent = out_cot[0]
    tok_count = clean_rows.shape[0]
    width = clean_rows.shape[1]
    span = WINDOW // tok_count
    scale = 1.0 / math.sqrt(HEAD_DIM)
    position = lax.axis_index("seq") * tok_count
    within = jnp.arange(BLOCK, dtype=jnp.int32)
    block_bits = jnp.right_shift(mask_bits[0][:, None], within[None, :]) & 1
    bits = block_bits.reshape(tok_count)
    masked = bits == 1
    noisy = jnp.where(masked[:, None], mask_embed[None, :], clean_rows)
    query = jnp.dot(noisy, w_query, preferred_element_type=jnp.float32).astype(jnp.bfloat16)
    key_noisy = jnp.dot(noisy, w_key, preferred_element_type=jnp.float32).astype(jnp.bfloat16)
    value_noisy = jnp.dot(noisy, w_value, preferred_element_type=jnp.float32).astype(jnp.bfloat16)
    carried = clean_rows
    collected = [carried]
    for step in range(span):
        carried = from_behind(carried, "seq", 1)
        collected.insert(0, carried)
    window_rows = jnp.concatenate(collected, axis=0)
    key_clean = jnp.dot(window_rows, w_key, preferred_element_type=jnp.float32).astype(jnp.bfloat16)
    value_clean = jnp.dot(window_rows, w_value, preferred_element_type=jnp.float32).astype(
        jnp.bfloat16
    )
    level_f = levels[0].astype(jnp.float32)
    ratio_f = importance[0].astype(jnp.float32)
    block_weight = LEVELS / level_f * (ratio_f[:, 0] / ratio_f[:, 1])
    token_weight = (block_weight[:, None] * block_bits.astype(jnp.float32)).reshape(tok_count)
    grad_out = (cotangent.astype(jnp.float32) * token_weight[:, None]).astype(jnp.bfloat16)
    place = jnp.reshape(span * tok_count - position, (1,)).astype(jnp.int32)
    attn_rows, dkey_rows, dvalue_rows = attention_heads(
        place, query, key_clean, value_clean, key_noisy, value_noisy, grad_out
    )
    terms = project(dkey_rows, w_key) + project(dvalue_rows, w_value)
    running = terms[:tok_count]
    for step in range(span):
        running = from_behind(running.astype(jnp.bfloat16), "seq", -1).astype(jnp.float32)
        running = running + terms[(step + 1) * tok_count : (step + 2) * tok_count]
    raw = running
    squares = jnp.sum(raw * raw)
    total_squares = global_total(squares, ("dp", "seq"))
    entries = float(tok_count * width * lax.axis_size("dp") * lax.axis_size("seq"))
    rms = jnp.sqrt(total_squares / entries + EPS)
    factor = jnp.minimum(1.0, CLIP / rms)
    return (attn_rows[None], (raw * factor)[None])


def solution(mesh):
    in_specs = (
        P("dp", "seq", None),
        P("dp", "seq", None),
        P("dp", "seq"),
        P("dp", "seq"),
        P("dp", "seq", None),
        P(),
        P(),
        P(),
        P(),
    )
    out_specs = (P("dp", "seq", None), P("dp", "seq", None))
    return jax.shard_map(
        on_device, mesh=mesh, in_specs=in_specs, out_specs=out_specs, check_vma=False
    )
```

```python
import functools
import math

import jax
import jax.numpy as jnp
from jax import lax
from jax.sharding import PartitionSpec as P
from jax.experimental import pallas as pl
from jax.experimental.pallas import tpu as pltpu

HEADS = 12
HEAD_DIM = 64
BLOCK = 16
WINDOW = 1024
LEVELS = 16


EPS = 1e-06
CLIP = 0.25


def from_behind(block, axis, distance):
    devices = range(lax.axis_size(axis))
    route = [(i - distance, i) for i in devices if i - distance in devices]
    return lax.ppermute(block, axis, route)


def group_stages(axes):
    stages = []
    for axis in axes:
        rest, stride = lax.axis_size(axis), 1
        while rest > 1:
            size = max(g for g in range(1, 9) if rest % g == 0)
            stages.append((axis, stride, size))
            stride, rest = stride * size, rest // size
    return stages


def stage_peer(axis, stride, size, offset):
    index = lax.axis_index(axis)
    digit = (index // stride) % size
    return index + ((digit + offset) % size - digit) * stride


def device_of(axes, axis, peer):
    return tuple(peer if name == axis else lax.axis_index(name) for name in axes)


def total_kernel(axes, stages, part_ref, out_ref, slots, send_sems, recv_sems):
    barrier = pltpu.get_barrier_semaphore()
    greeted = 0
    for axis, stride, size in stages:
        for offset in range(1, size):
            peer = stage_peer(axis, stride, size, offset)
            pl.semaphore_signal(
                barrier, 1, device_id=device_of(axes, axis, peer),
                device_id_type=pl.DeviceIdType.MESH,
            )
            greeted += 1
    pl.semaphore_wait(barrier, greeted)
    current = part_ref[...]
    for number, (axis, stride, size) in enumerate(stages):
        digit = (lax.axis_index(axis) // stride) % size
        slots[number, digit] = current
        copies = []
        for offset in range(1, size):
            peer = stage_peer(axis, stride, size, offset)
            copy = pltpu.make_async_remote_copy(
                src_ref=slots.at[number, digit],
                dst_ref=slots.at[number, digit],
                send_sem=send_sems.at[number, offset],
                recv_sem=recv_sems.at[number, offset],
                device_id=device_of(axes, axis, peer),
                device_id_type=pl.DeviceIdType.MESH,
            )
            copy.start()
            copies.append(copy)
        for copy in copies:
            copy.wait()
        current = slots[number, 0]
        for member in range(1, size):
            current = current + slots[number, member]
    out_ref[...] = current


def global_total(value, axes):
    stages = group_stages(axes)
    widest = max(size for _, _, size in stages)
    part = jnp.broadcast_to(value.astype(jnp.float32), (8, 128))
    summed = pl.pallas_call(
        functools.partial(total_kernel, axes, stages),
        out_shape=jax.ShapeDtypeStruct((8, 128), jnp.float32),
        in_specs=[pl.BlockSpec(memory_space=pltpu.VMEM)],
        out_specs=pl.BlockSpec(memory_space=pltpu.VMEM),
        scratch_shapes=[
            pltpu.VMEM((len(stages), widest, 8, 128), jnp.float32),
            pltpu.SemaphoreType.DMA((len(stages), widest)),
            pltpu.SemaphoreType.DMA((len(stages), widest)),
        ],
        compiler_params=pltpu.CompilerParams(collective_id=0, has_side_effects=True),
    )(part)
    return summed[0, 0]


def attention_kernel(place_ref, q_ref, kc_ref, vc_ref, kn_ref, vn_ref, g_ref,
                     out_ref, dk_ref, dv_ref):
    scale = 1.0 / math.sqrt(HEAD_DIM)
    query = q_ref[...]
    key_clean = kc_ref[...]
    value_clean = vc_ref[...]
    key_noisy = kn_ref[...]
    value_noisy = vn_ref[...]
    grad = g_ref[...]
    rows, lanes = query.shape
    context = key_clean.shape[0]
    row_block = lax.broadcasted_iota(jnp.int32, (rows, context), 0) // BLOCK * BLOCK
    col = lax.broadcasted_iota(jnp.int32, (rows, context), 1)
    allow_clean = (col >= row_block) & (col < row_block + WINDOW) & (col >= place_ref[0])
    own_row = lax.broadcasted_iota(jnp.int32, (rows, rows), 0) // BLOCK
    own_col = lax.broadcasted_iota(jnp.int32, (rows, rows), 1) // BLOCK
    allow_noisy = own_row == own_col
    lane = lax.broadcasted_iota(jnp.int32, (1, lanes), 1) // HEAD_DIM
    contract = (((1,), (1,)), ((), ()))
    lead = (((0,), (0,)), ((), ()))
    zero = jnp.zeros((), jnp.bfloat16)
    outs, dks, dvs = [], [], []
    for head in range(lanes // HEAD_DIM):
        mine = lane == head
        query_h = jnp.where(mine, query, zero)
        grad_h = jnp.where(mine, grad, zero)
        score_clean = lax.dot_general(query_h, key_clean, contract, preferred_element_type=jnp.float32) * scale
        score_noisy = lax.dot_general(query_h, key_noisy, contract, preferred_element_type=jnp.float32) * scale
        score_clean = jnp.where(allow_clean, score_clean, -jnp.inf)
        score_noisy = jnp.where(allow_noisy, score_noisy, -jnp.inf)
        peak = jnp.maximum(
            jnp.max(score_clean, axis=-1, keepdims=True), jnp.max(score_noisy, axis=-1, keepdims=True)
        )
        exp_clean = jnp.where(allow_clean, jnp.exp(score_clean - peak), 0.0)
        exp_noisy = jnp.where(allow_noisy, jnp.exp(score_noisy - peak), 0.0)
        denom = jnp.sum(exp_clean, axis=-1, keepdims=True) + jnp.sum(exp_noisy, axis=-1, keepdims=True)
        inverse = 1.0 / denom
        prob_clean = exp_clean * inverse
        weight_clean = prob_clean.astype(jnp.bfloat16)
        weight_noisy = (exp_noisy * inverse).astype(jnp.bfloat16)
        mixed = jnp.dot(weight_clean, value_clean, preferred_element_type=jnp.float32)
        mixed = mixed + jnp.dot(weight_noisy, value_noisy, preferred_element_type=jnp.float32)
        out_h = mixed.astype(jnp.bfloat16)
        delta = jnp.sum(
            jnp.where(mine, grad.astype(jnp.float32) * out_h.astype(jnp.float32), 0.0),
            axis=-1, keepdims=True,
        )
        dprob = lax.dot_general(grad_h, value_clean, contract, preferred_element_type=jnp.float32)
        dscore = (prob_clean * (dprob - delta) * scale).astype(jnp.bfloat16)
        outs.append(out_h)
        dks.append(lax.dot_general(dscore, query, lead, preferred_element_type=jnp.float32))
        dvs.append(lax.dot_general(weight_clean, grad, lead, preferred_element_type=jnp.float32))
    out, dk, dv = outs[0], dks[0], dvs[0]
    for head in range(1, len(outs)):
        mine = lane == head
        out = jnp.where(mine, outs[head], out)
        dk = jnp.where(mine, dks[head], dk)
        dv = jnp.where(mine, dvs[head], dv)
    out_ref[...] = out
    dk_ref[...] = dk
    dv_ref[...] = dv


def attention_heads(place, query, key_clean, value_clean, key_noisy, value_noisy, grad):
    rows, width = query.shape
    context = key_clean.shape[0]
    lanes = 2 * HEAD_DIM
    pairs = width // lanes
    row_spec = pl.BlockSpec((rows, lanes), lambda p, place: (0, p))
    ctx_spec = pl.BlockSpec((context, lanes), lambda p, place: (0, p))
    flops = pairs * 2 * 2 * lanes * (5 * rows * context + 3 * rows * rows)
    return pl.pallas_call(
        attention_kernel,
        out_shape=(
            jax.ShapeDtypeStruct((rows, width), jnp.bfloat16),
            jax.ShapeDtypeStruct((context, width), jnp.float32),
            jax.ShapeDtypeStruct((context, width), jnp.float32),
        ),
        grid_spec=pltpu.PrefetchScalarGridSpec(
            num_scalar_prefetch=1,
            grid=(pairs,),
            in_specs=[row_spec, ctx_spec, ctx_spec, row_spec, row_spec, row_spec],
            out_specs=[row_spec, ctx_spec, ctx_spec],
        ),
        cost_estimate=pl.CostEstimate(
            flops=flops,
            transcendentals=width // HEAD_DIM * rows * (context + rows),
            bytes_accessed=width * (8 * rows + 4 * context + 8 * context),
        ),
    )(place, query, key_clean, value_clean, key_noisy, value_noisy, grad)


def chain_barrier(axes, left, right, has_left, has_right):
    barrier = pltpu.get_barrier_semaphore()
    for peer, present in ((left, has_left), (right, has_right)):
        @pl.when(present)
        def _():
            pl.semaphore_signal(
                barrier, 1, device_id=device_of(axes, "seq", peer),
                device_id_type=pl.DeviceIdType.MESH,
            )
    pl.semaphore_wait(barrier, has_left.astype(jnp.int32) + has_right.astype(jnp.int32))


def chain_ends(axes):
    me = lax.axis_index("seq")
    size = lax.axis_size("seq")
    left = jnp.maximum(me - 1, 0)
    right = jnp.minimum(me + 1, size - 1)
    return me, left, right, me > 0, me < size - 1


def sum_back_kernel(axes, span, chunks, terms_ref, raw_ref, sent, got, send_sems, recv_sems):
    me, left, right, has_left, has_right = chain_ends(axes)
    chain_barrier(axes, left, right, has_left, has_right)
    rows = raw_ref.shape[0]
    piece = rows // chunks

    @pl.when(jnp.logical_not(has_right))
    def _():
        got[...] = jnp.zeros(got.shape, got.dtype)

    def copy(step, chunk):
        return pltpu.make_async_remote_copy(
            src_ref=sent.at[step, chunk], dst_ref=got.at[step, chunk],
            send_sem=send_sems.at[step, chunk], recv_sem=recv_sems.at[step, chunk],
            device_id=device_of(axes, "seq", left), device_id_type=pl.DeviceIdType.MESH,
        )

    for step in range(span + 1):
        for chunk in range(chunks):
            value = terms_ref[pl.ds(step * rows + chunk * piece, piece), :]
            if step > 0:
                @pl.when(has_right)
                def _():
                    copy(step - 1, chunk).wait_recv()

                value = value + got[step - 1, chunk].astype(jnp.float32)
            if step < span:
                sent[step, chunk] = value.astype(jnp.bfloat16)

                @pl.when(has_left)
                def _():
                    copy(step, chunk).start()
            else:
                raw_ref[pl.ds(chunk * piece, piece), :] = value
    for step in range(span):
        for chunk in range(chunks):
            @pl.when(has_left)
            def _():
                copy(step, chunk).wait_send()


def sum_back(terms, span, rows, axes, chunks=4):
    width = terms.shape[1]
    piece = rows // chunks
    return pl.pallas_call(
        functools.partial(sum_back_kernel, axes, span, chunks),
        out_shape=jax.ShapeDtypeStruct((rows, width), jnp.float32),
        in_specs=[pl.BlockSpec(memory_space=pltpu.VMEM)],
        out_specs=pl.BlockSpec(memory_space=pltpu.VMEM),
        scratch_shapes=[
            pltpu.VMEM((span, chunks, piece, width), jnp.bfloat16),
            pltpu.VMEM((span, chunks, piece, width), jnp.bfloat16),
            pltpu.SemaphoreType.DMA((span, chunks)),
            pltpu.SemaphoreType.DMA((span, chunks)),
        ],
        compiler_params=pltpu.CompilerParams(collective_id=1, has_side_effects=True),
    )(terms)


def gather_front_kernel(axes, span, chunks, own_ref, window_ref, got, send_sems, recv_sems):
    me, left, right, has_left, has_right = chain_ends(axes)
    chain_barrier(axes, left, right, has_left, has_right)
    rows = own_ref.shape[0]
    piece = rows // chunks
    for step in range(span):
        @pl.when(step >= me)
        def _():
            got[step] = jnp.zeros(got.shape[1:], got.dtype)

    def copy(step, chunk):
        if step == 0:
            source = own_ref.at[pl.ds(chunk * piece, piece)]
        else:
            source = got.at[step - 1, chunk]
        return pltpu.make_async_remote_copy(
            src_ref=source, dst_ref=got.at[step, chunk],
            send_sem=send_sems.at[step, chunk], recv_sem=recv_sems.at[step, chunk],
            device_id=device_of(axes, "seq", right), device_id_type=pl.DeviceIdType.MESH,
        )

    for step in range(span + 1):
        for chunk in range(chunks):
            if step > 0:
                @pl.when(step <= me)
                def _():
                    copy(step - 1, chunk).wait_recv()
            if step < span:
                @pl.when(has_right & (step <= me))
                def _():
                    copy(step, chunk).start()
    for step in range(span):
        window_ref[pl.ds((span - 1 - step) * rows, rows), :] = got[step].reshape(rows, -1)
    window_ref[pl.ds(span * rows, rows), :] = own_ref[...]
    for step in range(span):
        for chunk in range(chunks):
            @pl.when(has_right & (step <= me))
            def _():
                copy(step, chunk).wait_send()


def gather_front(own, span, axes, chunks=4):
    rows, width = own.shape
    piece = rows // chunks
    return pl.pallas_call(
        functools.partial(gather_front_kernel, axes, span, chunks),
        out_shape=jax.ShapeDtypeStruct(((span + 1) * rows, width), own.dtype),
        in_specs=[pl.BlockSpec(memory_space=pltpu.VMEM)],
        out_specs=pl.BlockSpec(memory_space=pltpu.VMEM),
        scratch_shapes=[
            pltpu.VMEM((span, chunks, piece, width), own.dtype),
            pltpu.SemaphoreType.DMA((span, chunks)),
            pltpu.SemaphoreType.DMA((span, chunks)),
        ],
        compiler_params=pltpu.CompilerParams(collective_id=2, has_side_effects=True),
    )(own)


def project(rows, weight):
    high = rows.astype(jnp.bfloat16)
    low = (rows - high.astype(jnp.float32)).astype(jnp.bfloat16)
    contract = (((1,), (1,)), ((), ()))
    product = lax.dot_general(high, weight, contract, preferred_element_type=jnp.float32)
    return product + lax.dot_general(low, weight, contract, preferred_element_type=jnp.float32)


def on_device(clean, out_cot, mask_bits, levels, importance, w_query, w_key, w_value, mask_embed):
    clean_rows = clean[0]
    cotangent = out_cot[0]
    tok_count = clean_rows.shape[0]
    width = clean_rows.shape[1]
    span = WINDOW // tok_count
    scale = 1.0 / math.sqrt(HEAD_DIM)
    position = lax.axis_index("seq") * tok_count
    within = jnp.arange(BLOCK, dtype=jnp.int32)
    block_bits = jnp.right_shift(mask_bits[0][:, None], within[None, :]) & 1
    bits = block_bits.reshape(tok_count)
    masked = bits == 1
    noisy = jnp.where(masked[:, None], mask_embed[None, :], clean_rows)
    query = jnp.dot(noisy, w_query, preferred_element_type=jnp.float32).astype(jnp.bfloat16)
    key_noisy = jnp.dot(noisy, w_key, preferred_element_type=jnp.float32).astype(jnp.bfloat16)
    value_noisy = jnp.dot(noisy, w_value, preferred_element_type=jnp.float32).astype(jnp.bfloat16)
    window_rows = gather_front(clean_rows, span, ("dp", "seq"))
    key_clean = jnp.dot(window_rows, w_key, preferred_element_type=jnp.float32).astype(jnp.bfloat16)
    value_clean = jnp.dot(window_rows, w_value, preferred_element_type=jnp.float32).astype(
        jnp.bfloat16
    )
    level_f = levels[0].astype(jnp.float32)
    ratio_f = importance[0].astype(jnp.float32)
    block_weight = LEVELS / level_f * (ratio_f[:, 0] / ratio_f[:, 1])
    token_weight = (block_weight[:, None] * block_bits.astype(jnp.float32)).reshape(tok_count)
    grad_out = (cotangent.astype(jnp.float32) * token_weight[:, None]).astype(jnp.bfloat16)
    place = jnp.reshape(span * tok_count - position, (1,)).astype(jnp.int32)
    attn_rows, dkey_rows, dvalue_rows = attention_heads(
        place, query, key_clean, value_clean, key_noisy, value_noisy, grad_out
    )
    terms = project(dkey_rows, w_key) + project(dvalue_rows, w_value)
    raw = sum_back(terms, span, tok_count, ("dp", "seq"))
    squares = jnp.sum(raw * raw)
    total_squares = global_total(squares, ("dp", "seq"))
    entries = float(tok_count * width * lax.axis_size("dp") * lax.axis_size("seq"))
    rms = jnp.sqrt(total_squares / entries + EPS)
    factor = jnp.minimum(1.0, CLIP / rms)
    return (attn_rows[None], (raw * factor)[None])


def solution(mesh):
    in_specs = (
        P("dp", "seq", None),
        P("dp", "seq", None),
        P("dp", "seq"),
        P("dp", "seq"),
        P("dp", "seq", None),
        P(),
        P(),
        P(),
        P(),
    )
    out_specs = (P("dp", "seq", None), P("dp", "seq", None))
    return jax.shard_map(
        on_device, mesh=mesh, in_specs=in_specs, out_specs=out_specs, check_vma=False
    )
```

```python
import functools
import math

import jax
import jax.numpy as jnp
from jax import lax
from jax.sharding import PartitionSpec as P
from jax.experimental import pallas as pl
from jax.experimental.pallas import tpu as pltpu

HEADS = 12
HEAD_DIM = 64
BLOCK = 16
WINDOW = 1024
LEVELS = 16


EPS = 1e-06
CLIP = 0.25


def from_behind(block, axis, distance):
    devices = range(lax.axis_size(axis))
    route = [(i - distance, i) for i in devices if i - distance in devices]
    return lax.ppermute(block, axis, route)


def group_stages(axes):
    stages = []
    for axis in axes:
        rest, stride = lax.axis_size(axis), 1
        while rest > 1:
            size = max(g for g in range(1, 9) if rest % g == 0)
            stages.append((axis, stride, size))
            stride, rest = stride * size, rest // size
    return stages


def stage_peer(axis, stride, size, offset):
    index = lax.axis_index(axis)
    digit = (index // stride) % size
    return index + ((digit + offset) % size - digit) * stride


def device_of(axes, axis, peer):
    return tuple(peer if name == axis else lax.axis_index(name) for name in axes)


def total_kernel(axes, stages, part_ref, out_ref, slots, send_sems, recv_sems):
    barrier = pltpu.get_barrier_semaphore()
    greeted = 0
    for axis, stride, size in stages:
        for offset in range(1, size):
            peer = stage_peer(axis, stride, size, offset)
            pl.semaphore_signal(
                barrier, 1, device_id=device_of(axes, axis, peer),
                device_id_type=pl.DeviceIdType.MESH,
            )
            greeted += 1
    pl.semaphore_wait(barrier, greeted)
    current = part_ref[...]
    for number, (axis, stride, size) in enumerate(stages):
        digit = (lax.axis_index(axis) // stride) % size
        slots[number, digit] = current
        copies = []
        for offset in range(1, size):
            peer = stage_peer(axis, stride, size, offset)
            copy = pltpu.make_async_remote_copy(
                src_ref=slots.at[number, digit],
                dst_ref=slots.at[number, digit],
                send_sem=send_sems.at[number, offset],
                recv_sem=recv_sems.at[number, offset],
                device_id=device_of(axes, axis, peer),
                device_id_type=pl.DeviceIdType.MESH,
            )
            copy.start()
            copies.append(copy)
        for copy in copies:
            copy.wait()
        current = slots[number, 0]
        for member in range(1, size):
            current = current + slots[number, member]
    out_ref[...] = current


def global_total(value, axes):
    stages = group_stages(axes)
    widest = max(size for _, _, size in stages)
    part = jnp.broadcast_to(value.astype(jnp.float32), (8, 128))
    summed = pl.pallas_call(
        functools.partial(total_kernel, axes, stages),
        out_shape=jax.ShapeDtypeStruct((8, 128), jnp.float32),
        in_specs=[pl.BlockSpec(memory_space=pltpu.VMEM)],
        out_specs=pl.BlockSpec(memory_space=pltpu.VMEM),
        scratch_shapes=[
            pltpu.VMEM((len(stages), widest, 8, 128), jnp.float32),
            pltpu.SemaphoreType.DMA((len(stages), widest)),
            pltpu.SemaphoreType.DMA((len(stages), widest)),
        ],
        compiler_params=pltpu.CompilerParams(collective_id=0, has_side_effects=True),
    )(part)
    return summed[0, 0]


def attention_kernel(place_ref, q_ref, kc_ref, vc_ref, kn_ref, vn_ref, g_ref,
                     out_ref, dk_ref, dv_ref):
    scale = 1.0 / math.sqrt(HEAD_DIM)
    query = q_ref[...]
    key_clean = kc_ref[...]
    value_clean = vc_ref[...]
    key_noisy = kn_ref[...]
    value_noisy = vn_ref[...]
    grad = g_ref[...]
    rows, lanes = query.shape
    context = key_clean.shape[0]
    row_block = lax.broadcasted_iota(jnp.int32, (rows, context), 0) // BLOCK * BLOCK
    col = lax.broadcasted_iota(jnp.int32, (rows, context), 1)
    allow_clean = (col >= row_block) & (col < row_block + WINDOW) & (col >= place_ref[0])
    own_row = lax.broadcasted_iota(jnp.int32, (rows, rows), 0) // BLOCK
    own_col = lax.broadcasted_iota(jnp.int32, (rows, rows), 1) // BLOCK
    allow_noisy = own_row == own_col
    lane = lax.broadcasted_iota(jnp.int32, (1, lanes), 1) // HEAD_DIM
    contract = (((1,), (1,)), ((), ()))
    lead = (((0,), (0,)), ((), ()))
    zero = jnp.zeros((), jnp.bfloat16)
    outs, dks, dvs = [], [], []
    for head in range(lanes // HEAD_DIM):
        mine = lane == head
        query_h = jnp.where(mine, query, zero)
        grad_h = jnp.where(mine, grad, zero)
        score_clean = lax.dot_general(query_h, key_clean, contract, preferred_element_type=jnp.float32) * scale
        score_noisy = lax.dot_general(query_h, key_noisy, contract, preferred_element_type=jnp.float32) * scale
        score_clean = jnp.where(allow_clean, score_clean, -jnp.inf)
        score_noisy = jnp.where(allow_noisy, score_noisy, -jnp.inf)
        peak = jnp.maximum(
            jnp.max(score_clean, axis=-1, keepdims=True), jnp.max(score_noisy, axis=-1, keepdims=True)
        )
        exp_clean = jnp.where(allow_clean, jnp.exp(score_clean - peak), 0.0)
        exp_noisy = jnp.where(allow_noisy, jnp.exp(score_noisy - peak), 0.0)
        denom = jnp.sum(exp_clean, axis=-1, keepdims=True) + jnp.sum(exp_noisy, axis=-1, keepdims=True)
        inverse = 1.0 / denom
        prob_clean = exp_clean * inverse
        weight_clean = prob_clean.astype(jnp.bfloat16)
        weight_noisy = (exp_noisy * inverse).astype(jnp.bfloat16)
        mixed = jnp.dot(weight_clean, value_clean, preferred_element_type=jnp.float32)
        mixed = mixed + jnp.dot(weight_noisy, value_noisy, preferred_element_type=jnp.float32)
        out_h = mixed.astype(jnp.bfloat16)
        delta = jnp.sum(
            jnp.where(mine, grad.astype(jnp.float32) * out_h.astype(jnp.float32), 0.0),
            axis=-1, keepdims=True,
        )
        dprob = lax.dot_general(grad_h, value_clean, contract, preferred_element_type=jnp.float32)
        dscore = (prob_clean * (dprob - delta) * scale).astype(jnp.bfloat16)
        outs.append(out_h)
        dks.append(lax.dot_general(dscore, query, lead, preferred_element_type=jnp.float32))
        dvs.append(lax.dot_general(weight_clean, grad, lead, preferred_element_type=jnp.float32))
    out, dk, dv = outs[0], dks[0], dvs[0]
    for head in range(1, len(outs)):
        mine = lane == head
        out = jnp.where(mine, outs[head], out)
        dk = jnp.where(mine, dks[head], dk)
        dv = jnp.where(mine, dvs[head], dv)
    out_ref[...] = out
    dk_ref[...] = dk
    dv_ref[...] = dv


def attention_heads(place, query, key_clean, value_clean, key_noisy, value_noisy, grad):
    rows, width = query.shape
    context = key_clean.shape[0]
    lanes = 2 * HEAD_DIM
    pairs = width // lanes
    row_spec = pl.BlockSpec((rows, lanes), lambda p, place: (0, p))
    ctx_spec = pl.BlockSpec((context, lanes), lambda p, place: (0, p))
    flops = pairs * 2 * 2 * lanes * (5 * rows * context + 3 * rows * rows)
    return pl.pallas_call(
        attention_kernel,
        out_shape=(
            jax.ShapeDtypeStruct((rows, width), jnp.bfloat16),
            jax.ShapeDtypeStruct((context, width), jnp.float32),
            jax.ShapeDtypeStruct((context, width), jnp.float32),
        ),
        grid_spec=pltpu.PrefetchScalarGridSpec(
            num_scalar_prefetch=1,
            grid=(pairs,),
            in_specs=[row_spec, ctx_spec, ctx_spec, row_spec, row_spec, row_spec],
            out_specs=[row_spec, ctx_spec, ctx_spec],
        ),
        cost_estimate=pl.CostEstimate(
            flops=flops,
            transcendentals=width // HEAD_DIM * rows * (context + rows),
            bytes_accessed=width * (8 * rows + 4 * context + 8 * context),
        ),
    )(place, query, key_clean, value_clean, key_noisy, value_noisy, grad)


def chain_barrier(axes, left, right, has_left, has_right):
    barrier = pltpu.get_barrier_semaphore()
    for peer, present in ((left, has_left), (right, has_right)):
        @pl.when(present)
        def _():
            pl.semaphore_signal(
                barrier, 1, device_id=device_of(axes, "seq", peer),
                device_id_type=pl.DeviceIdType.MESH,
            )
    pl.semaphore_wait(barrier, has_left.astype(jnp.int32) + has_right.astype(jnp.int32))


def chain_ends(axes):
    me = lax.axis_index("seq")
    size = lax.axis_size("seq")
    left = jnp.maximum(me - 1, 0)
    right = jnp.minimum(me + 1, size - 1)
    return me, left, right, me > 0, me < size - 1


def sum_back_kernel(axes, span, chunks, terms_ref, raw_ref, sent, got, send_sems, recv_sems):
    me, left, right, has_left, has_right = chain_ends(axes)
    chain_barrier(axes, left, right, has_left, has_right)
    rows = raw_ref.shape[0]
    piece = rows // chunks

    @pl.when(jnp.logical_not(has_right))
    def _():
        got[...] = jnp.zeros(got.shape, got.dtype)

    def copy(step, chunk):
        return pltpu.make_async_remote_copy(
            src_ref=sent.at[step, chunk], dst_ref=got.at[step, chunk],
            send_sem=send_sems.at[step, chunk], recv_sem=recv_sems.at[step, chunk],
            device_id=device_of(axes, "seq", left), device_id_type=pl.DeviceIdType.MESH,
        )

    for step in range(span + 1):
        for chunk in range(chunks):
            value = terms_ref[pl.ds(step * rows + chunk * piece, piece), :]
            if step > 0:
                @pl.when(has_right)
                def _():
                    copy(step - 1, chunk).wait_recv()

                value = value + got[step - 1, chunk].astype(jnp.float32)
            if step < span:
                sent[step, chunk] = value.astype(jnp.bfloat16)

                @pl.when(has_left)
                def _():
                    copy(step, chunk).start()
            else:
                raw_ref[pl.ds(chunk * piece, piece), :] = value
    for step in range(span):
        for chunk in range(chunks):
            @pl.when(has_left)
            def _():
                copy(step, chunk).wait_send()


def sum_back(terms, span, rows, axes, chunks=4):
    width = terms.shape[1]
    piece = rows // chunks
    return pl.pallas_call(
        functools.partial(sum_back_kernel, axes, span, chunks),
        out_shape=jax.ShapeDtypeStruct((rows, width), jnp.float32),
        in_specs=[pl.BlockSpec(memory_space=pltpu.VMEM)],
        out_specs=pl.BlockSpec(memory_space=pltpu.VMEM),
        scratch_shapes=[
            pltpu.VMEM((span, chunks, piece, width), jnp.bfloat16),
            pltpu.VMEM((span, chunks, piece, width), jnp.bfloat16),
            pltpu.SemaphoreType.DMA((span, chunks)),
            pltpu.SemaphoreType.DMA((span, chunks)),
        ],
        compiler_params=pltpu.CompilerParams(collective_id=1, has_side_effects=True),
    )(terms)


def gather_front_kernel(axes, span, chunks, own_ref, noisy_ref, wq_ref, wk_ref, wv_ref,
                        kc_ref, vc_ref, q_ref, kn_ref, vn_ref, got, send_sems, recv_sems):
    me, left, right, has_left, has_right = chain_ends(axes)
    chain_barrier(axes, left, right, has_left, has_right)
    rows = own_ref.shape[0]
    piece = rows // chunks
    for step in range(span):
        @pl.when(step >= me)
        def _():
            got[step] = jnp.zeros(got.shape[1:], got.dtype)

    def copy(step, chunk):
        if step == 0:
            source = own_ref.at[pl.ds(chunk * piece, piece)]
        else:
            source = got.at[step - 1, chunk]
        return pltpu.make_async_remote_copy(
            src_ref=source, dst_ref=got.at[step, chunk],
            send_sem=send_sems.at[step, chunk], recv_sem=recv_sems.at[step, chunk],
            device_id=device_of(axes, "seq", right), device_id_type=pl.DeviceIdType.MESH,
        )

    def project_rows(rows_in, weight_ref):
        return jnp.dot(rows_in, weight_ref[...], preferred_element_type=jnp.float32).astype(
            jnp.bfloat16
        )

    for chunk in range(chunks):
        @pl.when(has_right)
        def _():
            copy(0, chunk).start()
    noisy = noisy_ref[...]
    q_ref[...] = project_rows(noisy, wq_ref)
    kn_ref[...] = project_rows(noisy, wk_ref)
    vn_ref[...] = project_rows(noisy, wv_ref)
    own = own_ref[...]
    kc_ref[pl.ds(span * rows, rows), :] = project_rows(own, wk_ref)
    vc_ref[pl.ds(span * rows, rows), :] = project_rows(own, wv_ref)
    for step in range(1, span + 1):
        for chunk in range(chunks):
            @pl.when(step <= me)
            def _():
                copy(step - 1, chunk).wait_recv()
            if step < span:
                @pl.when(has_right & (step <= me))
                def _():
                    copy(step, chunk).start()
            arrived = got[step - 1, chunk]
            start = (span - step) * rows + chunk * piece
            kc_ref[pl.ds(start, piece), :] = project_rows(arrived, wk_ref)
            vc_ref[pl.ds(start, piece), :] = project_rows(arrived, wv_ref)
    for step in range(span):
        for chunk in range(chunks):
            @pl.when(has_right & (step <= me))
            def _():
                copy(step, chunk).wait_send()


def gather_front(own, noisy, w_query, w_key, w_value, span, axes, chunks=4):
    rows, width = own.shape
    piece = rows // chunks
    vmem = pl.BlockSpec(memory_space=pltpu.VMEM)
    context = jax.ShapeDtypeStruct(((span + 1) * rows, width), jnp.bfloat16)
    local = jax.ShapeDtypeStruct((rows, width), jnp.bfloat16)
    flops = 2 * width * width * rows * (2 * (span + 1) + 3)
    return pl.pallas_call(
        functools.partial(gather_front_kernel, axes, span, chunks),
        out_shape=(context, context, local, local, local),
        in_specs=[vmem] * 5,
        out_specs=[vmem] * 5,
        scratch_shapes=[
            pltpu.VMEM((span, chunks, piece, width), own.dtype),
            pltpu.SemaphoreType.DMA((span, chunks)),
            pltpu.SemaphoreType.DMA((span, chunks)),
        ],
        cost_estimate=pl.CostEstimate(
            flops=flops, transcendentals=0,
            bytes_accessed=2 * width * (3 * width + (2 * span + 7) * rows),
        ),
        compiler_params=pltpu.CompilerParams(collective_id=2, has_side_effects=True),
    )(own, noisy, w_query, w_key, w_value)

def project(rows, weight):
    high = rows.astype(jnp.bfloat16)
    low = (rows - high.astype(jnp.float32)).astype(jnp.bfloat16)
    contract = (((1,), (1,)), ((), ()))
    product = lax.dot_general(high, weight, contract, preferred_element_type=jnp.float32)
    return product + lax.dot_general(low, weight, contract, preferred_element_type=jnp.float32)


def on_device(clean, out_cot, mask_bits, levels, importance, w_query, w_key, w_value, mask_embed):
    clean_rows = clean[0]
    cotangent = out_cot[0]
    tok_count = clean_rows.shape[0]
    width = clean_rows.shape[1]
    span = WINDOW // tok_count
    scale = 1.0 / math.sqrt(HEAD_DIM)
    position = lax.axis_index("seq") * tok_count
    within = jnp.arange(BLOCK, dtype=jnp.int32)
    block_bits = jnp.right_shift(mask_bits[0][:, None], within[None, :]) & 1
    bits = block_bits.reshape(tok_count)
    masked = bits == 1
    noisy = jnp.where(masked[:, None], mask_embed[None, :], clean_rows)
    key_clean, value_clean, query, key_noisy, value_noisy = gather_front(
        clean_rows, noisy, w_query, w_key, w_value, span, ("dp", "seq")
    )
    level_f = levels[0].astype(jnp.float32)
    ratio_f = importance[0].astype(jnp.float32)
    block_weight = LEVELS / level_f * (ratio_f[:, 0] / ratio_f[:, 1])
    token_weight = (block_weight[:, None] * block_bits.astype(jnp.float32)).reshape(tok_count)
    grad_out = (cotangent.astype(jnp.float32) * token_weight[:, None]).astype(jnp.bfloat16)
    place = jnp.reshape(span * tok_count - position, (1,)).astype(jnp.int32)
    attn_rows, dkey_rows, dvalue_rows = attention_heads(
        place, query, key_clean, value_clean, key_noisy, value_noisy, grad_out
    )
    terms = project(dkey_rows, w_key) + project(dvalue_rows, w_value)
    raw = sum_back(terms, span, tok_count, ("dp", "seq"))
    squares = jnp.sum(raw * raw)
    total_squares = global_total(squares, ("dp", "seq"))
    entries = float(tok_count * width * lax.axis_size("dp") * lax.axis_size("seq"))
    rms = jnp.sqrt(total_squares / entries + EPS)
    factor = jnp.minimum(1.0, CLIP / rms)
    return (attn_rows[None], (raw * factor)[None])


def solution(mesh):
    in_specs = (
        P("dp", "seq", None),
        P("dp", "seq", None),
        P("dp", "seq"),
        P("dp", "seq"),
        P("dp", "seq", None),
        P(),
        P(),
        P(),
        P(),
    )
    out_specs = (P("dp", "seq", None), P("dp", "seq", None))
    return jax.shard_map(
        on_device, mesh=mesh, in_specs=in_specs, out_specs=out_specs, check_vma=False
    )
```

```python
import functools
import math

import jax
import jax.numpy as jnp
from jax import lax
from jax.sharding import PartitionSpec as P
from jax.experimental import pallas as pl
from jax.experimental.pallas import tpu as pltpu

HEADS = 12
HEAD_DIM = 64
BLOCK = 16
WINDOW = 1024
LEVELS = 16


EPS = 1e-06
CLIP = 0.25


def from_behind(block, axis, distance):
    devices = range(lax.axis_size(axis))
    route = [(i - distance, i) for i in devices if i - distance in devices]
    return lax.ppermute(block, axis, route)


def group_stages(axes):
    stages = []
    for axis in axes:
        rest, stride = lax.axis_size(axis), 1
        while rest > 1:
            size = max(g for g in range(1, 9) if rest % g == 0)
            stages.append((axis, stride, size))
            stride, rest = stride * size, rest // size
    return stages


def stage_peer(axis, stride, size, offset):
    index = lax.axis_index(axis)
    digit = (index // stride) % size
    return index + ((digit + offset) % size - digit) * stride


def device_of(axes, axis, peer):
    return tuple(peer if name == axis else lax.axis_index(name) for name in axes)


def total_kernel(axes, stages, part_ref, out_ref, slots, send_sems, recv_sems):
    barrier = pltpu.get_barrier_semaphore()
    greeted = 0
    for axis, stride, size in stages:
        for offset in range(1, size):
            peer = stage_peer(axis, stride, size, offset)
            pl.semaphore_signal(
                barrier, 1, device_id=device_of(axes, axis, peer),
                device_id_type=pl.DeviceIdType.MESH,
            )
            greeted += 1
    pl.semaphore_wait(barrier, greeted)
    current = part_ref[...]
    for number, (axis, stride, size) in enumerate(stages):
        digit = (lax.axis_index(axis) // stride) % size
        slots[number, digit] = current
        copies = []
        for offset in range(1, size):
            peer = stage_peer(axis, stride, size, offset)
            copy = pltpu.make_async_remote_copy(
                src_ref=slots.at[number, digit],
                dst_ref=slots.at[number, digit],
                send_sem=send_sems.at[number, offset],
                recv_sem=recv_sems.at[number, offset],
                device_id=device_of(axes, axis, peer),
                device_id_type=pl.DeviceIdType.MESH,
            )
            copy.start()
            copies.append(copy)
        for copy in copies:
            copy.wait()
        current = slots[number, 0]
        for member in range(1, size):
            current = current + slots[number, member]
    out_ref[...] = current


def global_total(value, axes):
    stages = group_stages(axes)
    widest = max(size for _, _, size in stages)
    part = jnp.broadcast_to(value.astype(jnp.float32), (8, 128))
    summed = pl.pallas_call(
        functools.partial(total_kernel, axes, stages),
        out_shape=jax.ShapeDtypeStruct((8, 128), jnp.float32),
        in_specs=[pl.BlockSpec(memory_space=pltpu.VMEM)],
        out_specs=pl.BlockSpec(memory_space=pltpu.VMEM),
        scratch_shapes=[
            pltpu.VMEM((len(stages), widest, 8, 128), jnp.float32),
            pltpu.SemaphoreType.DMA((len(stages), widest)),
            pltpu.SemaphoreType.DMA((len(stages), widest)),
        ],
        compiler_params=pltpu.CompilerParams(collective_id=0, has_side_effects=True),
    )(part)
    return summed[0, 0]


def attention_kernel(place_ref, q_ref, kc_ref, vc_ref, kn_ref, vn_ref, g_ref,
                     out_ref, dk_ref, dv_ref):
    scale = 1.0 / math.sqrt(HEAD_DIM)
    query = q_ref[...]
    key_clean = kc_ref[...]
    value_clean = vc_ref[...]
    key_noisy = kn_ref[...]
    value_noisy = vn_ref[...]
    grad = g_ref[...]
    rows, lanes = query.shape
    context = key_clean.shape[0]
    row_block = lax.broadcasted_iota(jnp.int32, (rows, context), 0) // BLOCK * BLOCK
    col = lax.broadcasted_iota(jnp.int32, (rows, context), 1)
    allow_clean = (col >= row_block) & (col < row_block + WINDOW) & (col >= place_ref[0])
    own_row = lax.broadcasted_iota(jnp.int32, (rows, rows), 0) // BLOCK
    own_col = lax.broadcasted_iota(jnp.int32, (rows, rows), 1) // BLOCK
    allow_noisy = own_row == own_col
    lane = lax.broadcasted_iota(jnp.int32, (1, lanes), 1) // HEAD_DIM
    contract = (((1,), (1,)), ((), ()))
    lead = (((0,), (0,)), ((), ()))
    zero = jnp.zeros((), jnp.bfloat16)
    outs, dks, dvs = [], [], []
    for head in range(lanes // HEAD_DIM):
        mine = lane == head
        query_h = jnp.where(mine, query, zero)
        grad_h = jnp.where(mine, grad, zero)
        score_clean = lax.dot_general(query_h, key_clean, contract, preferred_element_type=jnp.float32) * scale
        score_noisy = lax.dot_general(query_h, key_noisy, contract, preferred_element_type=jnp.float32) * scale
        score_clean = jnp.where(allow_clean, score_clean, -jnp.inf)
        score_noisy = jnp.where(allow_noisy, score_noisy, -jnp.inf)
        peak = jnp.maximum(
            jnp.max(score_clean, axis=-1, keepdims=True), jnp.max(score_noisy, axis=-1, keepdims=True)
        )
        exp_clean = jnp.where(allow_clean, jnp.exp(score_clean - peak), 0.0)
        exp_noisy = jnp.where(allow_noisy, jnp.exp(score_noisy - peak), 0.0)
        denom = jnp.sum(exp_clean, axis=-1, keepdims=True) + jnp.sum(exp_noisy, axis=-1, keepdims=True)
        inverse = 1.0 / denom
        prob_clean = exp_clean * inverse
        weight_clean = prob_clean.astype(jnp.bfloat16)
        weight_noisy = (exp_noisy * inverse).astype(jnp.bfloat16)
        mixed = jnp.dot(weight_clean, value_clean, preferred_element_type=jnp.float32)
        mixed = mixed + jnp.dot(weight_noisy, value_noisy, preferred_element_type=jnp.float32)
        out_h = mixed.astype(jnp.bfloat16)
        delta = jnp.sum(
            jnp.where(mine, grad.astype(jnp.float32) * out_h.astype(jnp.float32), 0.0),
            axis=-1, keepdims=True,
        )
        dprob = lax.dot_general(grad_h, value_clean, contract, preferred_element_type=jnp.float32)
        dscore = (prob_clean * (dprob - delta) * scale).astype(jnp.bfloat16)
        outs.append(out_h)
        dks.append(lax.dot_general(dscore, query, lead, preferred_element_type=jnp.float32))
        dvs.append(lax.dot_general(weight_clean, grad, lead, preferred_element_type=jnp.float32))
    out, dk, dv = outs[0], dks[0], dvs[0]
    for head in range(1, len(outs)):
        mine = lane == head
        out = jnp.where(mine, outs[head], out)
        dk = jnp.where(mine, dks[head], dk)
        dv = jnp.where(mine, dvs[head], dv)
    out_ref[...] = out
    dk_ref[...] = dk
    dv_ref[...] = dv


def attention_heads(place, query, key_clean, value_clean, key_noisy, value_noisy, grad):
    rows, width = query.shape
    context = key_clean.shape[0]
    lanes = 2 * HEAD_DIM
    pairs = width // lanes
    row_spec = pl.BlockSpec((rows, lanes), lambda p, place: (0, p))
    ctx_spec = pl.BlockSpec((context, lanes), lambda p, place: (0, p))
    flops = pairs * 2 * 2 * lanes * (5 * rows * context + 3 * rows * rows)
    return pl.pallas_call(
        attention_kernel,
        out_shape=(
            jax.ShapeDtypeStruct((rows, width), jnp.bfloat16),
            jax.ShapeDtypeStruct((context, width), jnp.float32),
            jax.ShapeDtypeStruct((context, width), jnp.float32),
        ),
        grid_spec=pltpu.PrefetchScalarGridSpec(
            num_scalar_prefetch=1,
            grid=(pairs,),
            in_specs=[row_spec, ctx_spec, ctx_spec, row_spec, row_spec, row_spec],
            out_specs=[row_spec, ctx_spec, ctx_spec],
        ),
        cost_estimate=pl.CostEstimate(
            flops=flops,
            transcendentals=width // HEAD_DIM * rows * (context + rows),
            bytes_accessed=width * (8 * rows + 4 * context + 8 * context),
        ),
    )(place, query, key_clean, value_clean, key_noisy, value_noisy, grad)


def chain_barrier(axes, left, right, has_left, has_right):
    barrier = pltpu.get_barrier_semaphore()
    for peer, present in ((left, has_left), (right, has_right)):
        @pl.when(present)
        def _():
            pl.semaphore_signal(
                barrier, 1, device_id=device_of(axes, "seq", peer),
                device_id_type=pl.DeviceIdType.MESH,
            )
    pl.semaphore_wait(barrier, has_left.astype(jnp.int32) + has_right.astype(jnp.int32))


def chain_ends(axes):
    me = lax.axis_index("seq")
    size = lax.axis_size("seq")
    left = jnp.maximum(me - 1, 0)
    right = jnp.minimum(me + 1, size - 1)
    return me, left, right, me > 0, me < size - 1


def sum_back_kernel(axes, span, chunks, dk_ref, dv_ref, wk_ref, wv_ref, raw_ref, sent, got,
                    send_sems, recv_sems):
    me, left, right, has_left, has_right = chain_ends(axes)
    chain_barrier(axes, left, right, has_left, has_right)
    rows = raw_ref.shape[0]
    piece = rows // chunks

    @pl.when(jnp.logical_not(has_right))
    def _():
        got[...] = jnp.zeros(got.shape, got.dtype)

    def copy(step, chunk):
        return pltpu.make_async_remote_copy(
            src_ref=sent.at[step, chunk], dst_ref=got.at[step, chunk],
            send_sem=send_sems.at[step, chunk], recv_sem=recv_sems.at[step, chunk],
            device_id=device_of(axes, "seq", left), device_id_type=pl.DeviceIdType.MESH,
        )

    for step in range(span + 1):
        for chunk in range(chunks):
            at = pl.ds(step * rows + chunk * piece, piece)
            value = project(dk_ref[at, :], wk_ref[...]) + project(dv_ref[at, :], wv_ref[...])
            if step > 0:
                @pl.when(has_right)
                def _():
                    copy(step - 1, chunk).wait_recv()

                value = value + got[step - 1, chunk].astype(jnp.float32)
            if step < span:
                sent[step, chunk] = value.astype(jnp.bfloat16)

                @pl.when(has_left)
                def _():
                    copy(step, chunk).start()
            else:
                raw_ref[pl.ds(chunk * piece, piece), :] = value
    for step in range(span):
        for chunk in range(chunks):
            @pl.when(has_left)
            def _():
                copy(step, chunk).wait_send()


def sum_back(dk, dv, w_key, w_value, span, rows, axes, chunks=4):
    width = dk.shape[1]
    piece = rows // chunks
    vmem = pl.BlockSpec(memory_space=pltpu.VMEM)
    return pl.pallas_call(
        functools.partial(sum_back_kernel, axes, span, chunks),
        out_shape=jax.ShapeDtypeStruct((rows, width), jnp.float32),
        in_specs=[vmem] * 4,
        out_specs=vmem,
        scratch_shapes=[
            pltpu.VMEM((span, chunks, piece, width), jnp.bfloat16),
            pltpu.VMEM((span, chunks, piece, width), jnp.bfloat16),
            pltpu.SemaphoreType.DMA((span, chunks)),
            pltpu.SemaphoreType.DMA((span, chunks)),
        ],
        cost_estimate=pl.CostEstimate(
            flops=8 * width * width * rows * (span + 1), transcendentals=0,
            bytes_accessed=4 * width * (2 * (span + 1) * rows + rows + width),
        ),
        compiler_params=pltpu.CompilerParams(collective_id=1, has_side_effects=True),
    )(dk, dv, w_key, w_value)


def gather_front_kernel(axes, span, chunks, own_ref, noisy_ref, wq_ref, wk_ref, wv_ref,
                        kc_ref, vc_ref, q_ref, kn_ref, vn_ref, got, send_sems, recv_sems):
    me, left, right, has_left, has_right = chain_ends(axes)
    chain_barrier(axes, left, right, has_left, has_right)
    rows = own_ref.shape[0]
    piece = rows // chunks
    for step in range(span):
        @pl.when(step >= me)
        def _():
            got[step] = jnp.zeros(got.shape[1:], got.dtype)

    def copy(step, chunk):
        if step == 0:
            source = own_ref.at[pl.ds(chunk * piece, piece)]
        else:
            source = got.at[step - 1, chunk]
        return pltpu.make_async_remote_copy(
            src_ref=source, dst_ref=got.at[step, chunk],
            send_sem=send_sems.at[step, chunk], recv_sem=recv_sems.at[step, chunk],
            device_id=device_of(axes, "seq", right), device_id_type=pl.DeviceIdType.MESH,
        )

    def project_rows(rows_in, weight_ref):
        return jnp.dot(rows_in, weight_ref[...], preferred_element_type=jnp.float32).astype(
            jnp.bfloat16
        )

    for chunk in range(chunks):
        @pl.when(has_right)
        def _():
            copy(0, chunk).start()
    noisy = noisy_ref[...]
    q_ref[...] = project_rows(noisy, wq_ref)
    kn_ref[...] = project_rows(noisy, wk_ref)
    vn_ref[...] = project_rows(noisy, wv_ref)
    own = own_ref[...]
    kc_ref[pl.ds(span * rows, rows), :] = project_rows(own, wk_ref)
    vc_ref[pl.ds(span * rows, rows), :] = project_rows(own, wv_ref)
    for step in range(1, span + 1):
        for chunk in range(chunks):
            @pl.when(step <= me)
            def _():
                copy(step - 1, chunk).wait_recv()
            if step < span:
                @pl.when(has_right & (step <= me))
                def _():
                    copy(step, chunk).start()
            arrived = got[step - 1, chunk]
            start = (span - step) * rows + chunk * piece
            kc_ref[pl.ds(start, piece), :] = project_rows(arrived, wk_ref)
            vc_ref[pl.ds(start, piece), :] = project_rows(arrived, wv_ref)
    for step in range(span):
        for chunk in range(chunks):
            @pl.when(has_right & (step <= me))
            def _():
                copy(step, chunk).wait_send()


def gather_front(own, noisy, w_query, w_key, w_value, span, axes, chunks=4):
    rows, width = own.shape
    piece = rows // chunks
    vmem = pl.BlockSpec(memory_space=pltpu.VMEM)
    context = jax.ShapeDtypeStruct(((span + 1) * rows, width), jnp.bfloat16)
    local = jax.ShapeDtypeStruct((rows, width), jnp.bfloat16)
    flops = 2 * width * width * rows * (2 * (span + 1) + 3)
    return pl.pallas_call(
        functools.partial(gather_front_kernel, axes, span, chunks),
        out_shape=(context, context, local, local, local),
        in_specs=[vmem] * 5,
        out_specs=[vmem] * 5,
        scratch_shapes=[
            pltpu.VMEM((span, chunks, piece, width), own.dtype),
            pltpu.SemaphoreType.DMA((span, chunks)),
            pltpu.SemaphoreType.DMA((span, chunks)),
        ],
        cost_estimate=pl.CostEstimate(
            flops=flops, transcendentals=0,
            bytes_accessed=2 * width * (3 * width + (2 * span + 7) * rows),
        ),
        compiler_params=pltpu.CompilerParams(collective_id=2, has_side_effects=True),
    )(own, noisy, w_query, w_key, w_value)

def project(rows, weight):
    high = rows.astype(jnp.bfloat16)
    low = (rows - high.astype(jnp.float32)).astype(jnp.bfloat16)
    contract = (((1,), (1,)), ((), ()))
    product = lax.dot_general(high, weight, contract, preferred_element_type=jnp.float32)
    return product + lax.dot_general(low, weight, contract, preferred_element_type=jnp.float32)


def on_device(clean, out_cot, mask_bits, levels, importance, w_query, w_key, w_value, mask_embed):
    clean_rows = clean[0]
    cotangent = out_cot[0]
    tok_count = clean_rows.shape[0]
    width = clean_rows.shape[1]
    span = WINDOW // tok_count
    scale = 1.0 / math.sqrt(HEAD_DIM)
    position = lax.axis_index("seq") * tok_count
    within = jnp.arange(BLOCK, dtype=jnp.int32)
    block_bits = jnp.right_shift(mask_bits[0][:, None], within[None, :]) & 1
    bits = block_bits.reshape(tok_count)
    masked = bits == 1
    noisy = jnp.where(masked[:, None], mask_embed[None, :], clean_rows)
    key_clean, value_clean, query, key_noisy, value_noisy = gather_front(
        clean_rows, noisy, w_query, w_key, w_value, span, ("dp", "seq")
    )
    level_f = levels[0].astype(jnp.float32)
    ratio_f = importance[0].astype(jnp.float32)
    block_weight = LEVELS / level_f * (ratio_f[:, 0] / ratio_f[:, 1])
    token_weight = (block_weight[:, None] * block_bits.astype(jnp.float32)).reshape(tok_count)
    grad_out = (cotangent.astype(jnp.float32) * token_weight[:, None]).astype(jnp.bfloat16)
    place = jnp.reshape(span * tok_count - position, (1,)).astype(jnp.int32)
    attn_rows, dkey_rows, dvalue_rows = attention_heads(
        place, query, key_clean, value_clean, key_noisy, value_noisy, grad_out
    )
    raw = sum_back(dkey_rows, dvalue_rows, w_key, w_value, span, tok_count, ("dp", "seq"))
    squares = jnp.sum(raw * raw)
    total_squares = global_total(squares, ("dp", "seq"))
    entries = float(tok_count * width * lax.axis_size("dp") * lax.axis_size("seq"))
    rms = jnp.sqrt(total_squares / entries + EPS)
    factor = jnp.minimum(1.0, CLIP / rms)
    return (attn_rows[None], (raw * factor)[None])


def solution(mesh):
    in_specs = (
        P("dp", "seq", None),
        P("dp", "seq", None),
        P("dp", "seq"),
        P("dp", "seq"),
        P("dp", "seq", None),
        P(),
        P(),
        P(),
        P(),
    )
    out_specs = (P("dp", "seq", None), P("dp", "seq", None))
    return jax.shard_map(
        on_device, mesh=mesh, in_specs=in_specs, out_specs=out_specs, check_vma=False
    )
```

```python
import functools
import math

import jax
import jax.numpy as jnp
from jax import lax
from jax.sharding import PartitionSpec as P
from jax.experimental import pallas as pl
from jax.experimental.pallas import tpu as pltpu

HEADS = 12
HEAD_DIM = 64
BLOCK = 16
WINDOW = 1024
LEVELS = 16


EPS = 1e-06
CLIP = 0.25


def from_behind(block, axis, distance):
    devices = range(lax.axis_size(axis))
    route = [(i - distance, i) for i in devices if i - distance in devices]
    return lax.ppermute(block, axis, route)


def group_stages(axes):
    stages = []
    for axis in axes:
        rest, stride = lax.axis_size(axis), 1
        while rest > 1:
            size = max(g for g in range(1, 9) if rest % g == 0)
            stages.append((axis, stride, size))
            stride, rest = stride * size, rest // size
    return stages


def stage_peer(axis, stride, size, offset):
    index = lax.axis_index(axis)
    digit = (index // stride) % size
    return index + ((digit + offset) % size - digit) * stride


def device_of(axes, axis, peer):
    return tuple(peer if name == axis else lax.axis_index(name) for name in axes)


def total_kernel(axes, stages, part_ref, out_ref, slots, send_sems, recv_sems):
    barrier = pltpu.get_barrier_semaphore()
    greeted = 0
    for axis, stride, size in stages:
        for offset in range(1, size):
            peer = stage_peer(axis, stride, size, offset)
            pl.semaphore_signal(
                barrier, 1, device_id=device_of(axes, axis, peer),
                device_id_type=pl.DeviceIdType.MESH,
            )
            greeted += 1
    pl.semaphore_wait(barrier, greeted)
    current = part_ref[...]
    for number, (axis, stride, size) in enumerate(stages):
        digit = (lax.axis_index(axis) // stride) % size
        slots[number, digit] = current
        copies = []
        for offset in range(1, size):
            peer = stage_peer(axis, stride, size, offset)
            copy = pltpu.make_async_remote_copy(
                src_ref=slots.at[number, digit],
                dst_ref=slots.at[number, digit],
                send_sem=send_sems.at[number, offset],
                recv_sem=recv_sems.at[number, offset],
                device_id=device_of(axes, axis, peer),
                device_id_type=pl.DeviceIdType.MESH,
            )
            copy.start()
            copies.append(copy)
        for copy in copies:
            copy.wait()
        current = slots[number, 0]
        for member in range(1, size):
            current = current + slots[number, member]
    out_ref[...] = current


def global_total(value, axes):
    stages = group_stages(axes)
    widest = max(size for _, _, size in stages)
    part = jnp.broadcast_to(value.astype(jnp.float32), (8, 128))
    summed = pl.pallas_call(
        functools.partial(total_kernel, axes, stages),
        out_shape=jax.ShapeDtypeStruct((8, 128), jnp.float32),
        in_specs=[pl.BlockSpec(memory_space=pltpu.VMEM)],
        out_specs=pl.BlockSpec(memory_space=pltpu.VMEM),
        scratch_shapes=[
            pltpu.VMEM((len(stages), widest, 8, 128), jnp.float32),
            pltpu.SemaphoreType.DMA((len(stages), widest)),
            pltpu.SemaphoreType.DMA((len(stages), widest)),
        ],
        compiler_params=pltpu.CompilerParams(collective_id=0, has_side_effects=True),
    )(part)
    return summed[0, 0]


def attention_kernel(place_ref, q_ref, kc_ref, vc_ref, kn_ref, vn_ref, g_ref,
                     out_ref, dk_ref, dv_ref):
    scale = 1.0 / math.sqrt(HEAD_DIM)
    query = q_ref[...]
    key_clean = kc_ref[...]
    value_clean = vc_ref[...]
    key_noisy = kn_ref[...]
    value_noisy = vn_ref[...]
    grad = g_ref[...]
    rows, lanes = query.shape
    context = key_clean.shape[0]
    row_block = lax.broadcasted_iota(jnp.int32, (rows, context), 0) // BLOCK * BLOCK
    col = lax.broadcasted_iota(jnp.int32, (rows, context), 1)
    allow_clean = (col >= row_block) & (col < row_block + WINDOW) & (col >= place_ref[0])
    own_row = lax.broadcasted_iota(jnp.int32, (rows, rows), 0) // BLOCK
    own_col = lax.broadcasted_iota(jnp.int32, (rows, rows), 1) // BLOCK
    allow_noisy = own_row == own_col
    lane = lax.broadcasted_iota(jnp.int32, (1, lanes), 1) // HEAD_DIM
    contract = (((1,), (1,)), ((), ()))
    lead = (((0,), (0,)), ((), ()))
    zero = jnp.zeros((), jnp.bfloat16)
    outs, dks, dvs = [], [], []
    for head in range(lanes // HEAD_DIM):
        mine = lane == head
        query_h = jnp.where(mine, query, zero)
        grad_h = jnp.where(mine, grad, zero)
        score_clean = lax.dot_general(query_h, key_clean, contract, preferred_element_type=jnp.float32) * scale
        score_noisy = lax.dot_general(query_h, key_noisy, contract, preferred_element_type=jnp.float32) * scale
        score_clean = jnp.where(allow_clean, score_clean, -jnp.inf)
        score_noisy = jnp.where(allow_noisy, score_noisy, -jnp.inf)
        peak = jnp.maximum(
            jnp.max(score_clean, axis=-1, keepdims=True), jnp.max(score_noisy, axis=-1, keepdims=True)
        )
        exp_clean = jnp.where(allow_clean, jnp.exp(score_clean - peak), 0.0)
        exp_noisy = jnp.where(allow_noisy, jnp.exp(score_noisy - peak), 0.0)
        denom = jnp.sum(exp_clean, axis=-1, keepdims=True) + jnp.sum(exp_noisy, axis=-1, keepdims=True)
        inverse = 1.0 / denom
        prob_clean = exp_clean * inverse
        weight_clean = prob_clean.astype(jnp.bfloat16)
        weight_noisy = (exp_noisy * inverse).astype(jnp.bfloat16)
        mixed = jnp.dot(weight_clean, value_clean, preferred_element_type=jnp.float32)
        mixed = mixed + jnp.dot(weight_noisy, value_noisy, preferred_element_type=jnp.float32)
        out_h = mixed.astype(jnp.bfloat16)
        delta = jnp.sum(
            jnp.where(mine, grad.astype(jnp.float32) * out_h.astype(jnp.float32), 0.0),
            axis=-1, keepdims=True,
        )
        dprob = lax.dot_general(grad_h, value_clean, contract, preferred_element_type=jnp.float32)
        dscore = (prob_clean * (dprob - delta) * scale).astype(jnp.bfloat16)
        outs.append(out_h)
        dks.append(lax.dot_general(dscore, query, lead, preferred_element_type=jnp.float32))
        dvs.append(lax.dot_general(weight_clean, grad, lead, preferred_element_type=jnp.float32))
    out, dk, dv = outs[0], dks[0], dvs[0]
    for head in range(1, len(outs)):
        mine = lane == head
        out = jnp.where(mine, outs[head], out)
        dk = jnp.where(mine, dks[head], dk)
        dv = jnp.where(mine, dvs[head], dv)
    out_ref[...] = out
    dk_ref[...] = dk
    dv_ref[...] = dv


def attention_heads(place, query, key_clean, value_clean, key_noisy, value_noisy, grad):
    rows, width = query.shape
    context = key_clean.shape[0]
    lanes = 2 * HEAD_DIM
    pairs = width // lanes
    row_spec = pl.BlockSpec((rows, lanes), lambda p, place: (0, p))
    ctx_spec = pl.BlockSpec((context, lanes), lambda p, place: (0, p))
    flops = pairs * 2 * 2 * lanes * (5 * rows * context + 3 * rows * rows)
    return pl.pallas_call(
        attention_kernel,
        out_shape=(
            jax.ShapeDtypeStruct((rows, width), jnp.bfloat16),
            jax.ShapeDtypeStruct((context, width), jnp.float32),
            jax.ShapeDtypeStruct((context, width), jnp.float32),
        ),
        grid_spec=pltpu.PrefetchScalarGridSpec(
            num_scalar_prefetch=1,
            grid=(pairs,),
            in_specs=[row_spec, ctx_spec, ctx_spec, row_spec, row_spec, row_spec],
            out_specs=[row_spec, ctx_spec, ctx_spec],
        ),
        cost_estimate=pl.CostEstimate(
            flops=flops,
            transcendentals=width // HEAD_DIM * rows * (context + rows),
            bytes_accessed=width * (8 * rows + 4 * context + 8 * context),
        ),
    )(place, query, key_clean, value_clean, key_noisy, value_noisy, grad)


def chain_barrier(axes, left, right, has_left, has_right):
    barrier = pltpu.get_barrier_semaphore()
    for peer, present in ((left, has_left), (right, has_right)):
        @pl.when(present)
        def _():
            pl.semaphore_signal(
                barrier, 1, device_id=device_of(axes, "seq", peer),
                device_id_type=pl.DeviceIdType.MESH,
            )
    pl.semaphore_wait(barrier, has_left.astype(jnp.int32) + has_right.astype(jnp.int32))


def chain_ends(axes):
    me = lax.axis_index("seq")
    size = lax.axis_size("seq")
    left = jnp.maximum(me - 1, 0)
    right = jnp.minimum(me + 1, size - 1)
    return me, left, right, me > 0, me < size - 1


def project_plain(rows, weight_ref):
    high = rows.astype(jnp.bfloat16)
    low = (rows - high.astype(jnp.float32)).astype(jnp.bfloat16)
    product = jnp.dot(high, weight_ref[...], preferred_element_type=jnp.float32)
    return product + jnp.dot(low, weight_ref[...], preferred_element_type=jnp.float32)


def sum_back_kernel(axes, span, chunks, dk_ref, dv_ref, wk_ref, wv_ref, raw_ref, sent, got,
                    send_sems, recv_sems):
    me, left, right, has_left, has_right = chain_ends(axes)
    chain_barrier(axes, left, right, has_left, has_right)
    rows = raw_ref.shape[0]
    piece = rows // chunks

    @pl.when(jnp.logical_not(has_right))
    def _():
        got[...] = jnp.zeros(got.shape, got.dtype)

    def copy(step, chunk):
        return pltpu.make_async_remote_copy(
            src_ref=sent.at[step, chunk], dst_ref=got.at[step, chunk],
            send_sem=send_sems.at[step, chunk], recv_sem=recv_sems.at[step, chunk],
            device_id=device_of(axes, "seq", left), device_id_type=pl.DeviceIdType.MESH,
        )

    for step in range(span + 1):
        for chunk in range(chunks):
            at = pl.ds(step * rows + chunk * piece, piece)
            value = project_plain(dk_ref[at, :], wk_ref) + project_plain(dv_ref[at, :], wv_ref)
            if step > 0:
                @pl.when(has_right)
                def _():
                    copy(step - 1, chunk).wait_recv()

                value = value + got[step - 1, chunk].astype(jnp.float32)
            if step < span:
                sent[step, chunk] = value.astype(jnp.bfloat16)

                @pl.when(has_left)
                def _():
                    copy(step, chunk).start()
            else:
                raw_ref[pl.ds(chunk * piece, piece), :] = value
    for step in range(span):
        for chunk in range(chunks):
            @pl.when(has_left)
            def _():
                copy(step, chunk).wait_send()


def sum_back(dk, dv, w_key, w_value, span, rows, axes, chunks=4):
    width = dk.shape[1]
    piece = rows // chunks
    vmem = pl.BlockSpec(memory_space=pltpu.VMEM)
    return pl.pallas_call(
        functools.partial(sum_back_kernel, axes, span, chunks),
        out_shape=jax.ShapeDtypeStruct((rows, width), jnp.float32),
        in_specs=[vmem] * 4,
        out_specs=vmem,
        scratch_shapes=[
            pltpu.VMEM((span, chunks, piece, width), jnp.bfloat16),
            pltpu.VMEM((span, chunks, piece, width), jnp.bfloat16),
            pltpu.SemaphoreType.DMA((span, chunks)),
            pltpu.SemaphoreType.DMA((span, chunks)),
        ],
        cost_estimate=pl.CostEstimate(
            flops=8 * width * width * rows * (span + 1), transcendentals=0,
            bytes_accessed=4 * width * (2 * (span + 1) * rows + rows + width),
        ),
        compiler_params=pltpu.CompilerParams(collective_id=1, has_side_effects=True),
    )(dk, dv, w_key, w_value)


def gather_front_kernel(axes, span, chunks, own_ref, noisy_ref, wq_ref, wk_ref, wv_ref,
                        kc_ref, vc_ref, q_ref, kn_ref, vn_ref, got, send_sems, recv_sems):
    me, left, right, has_left, has_right = chain_ends(axes)
    chain_barrier(axes, left, right, has_left, has_right)
    rows = own_ref.shape[0]
    piece = rows // chunks
    for step in range(span):
        @pl.when(step >= me)
        def _():
            got[step] = jnp.zeros(got.shape[1:], got.dtype)

    def copy(step, chunk):
        if step == 0:
            source = own_ref.at[pl.ds(chunk * piece, piece)]
        else:
            source = got.at[step - 1, chunk]
        return pltpu.make_async_remote_copy(
            src_ref=source, dst_ref=got.at[step, chunk],
            send_sem=send_sems.at[step, chunk], recv_sem=recv_sems.at[step, chunk],
            device_id=device_of(axes, "seq", right), device_id_type=pl.DeviceIdType.MESH,
        )

    def project_rows(rows_in, weight_ref):
        return jnp.dot(rows_in, weight_ref[...], preferred_element_type=jnp.float32).astype(
            jnp.bfloat16
        )

    for chunk in range(chunks):
        @pl.when(has_right)
        def _():
            copy(0, chunk).start()
    noisy = noisy_ref[...]
    q_ref[...] = project_rows(noisy, wq_ref)
    kn_ref[...] = project_rows(noisy, wk_ref)
    vn_ref[...] = project_rows(noisy, wv_ref)
    own = own_ref[...]
    kc_ref[pl.ds(span * rows, rows), :] = project_rows(own, wk_ref)
    vc_ref[pl.ds(span * rows, rows), :] = project_rows(own, wv_ref)
    for step in range(1, span + 1):
        for chunk in range(chunks):
            @pl.when(step <= me)
            def _():
                copy(step - 1, chunk).wait_recv()
            if step < span:
                @pl.when(has_right & (step <= me))
                def _():
                    copy(step, chunk).start()
            arrived = got[step - 1, chunk]
            start = (span - step) * rows + chunk * piece
            kc_ref[pl.ds(start, piece), :] = project_rows(arrived, wk_ref)
            vc_ref[pl.ds(start, piece), :] = project_rows(arrived, wv_ref)
    for step in range(span):
        for chunk in range(chunks):
            @pl.when(has_right & (step <= me))
            def _():
                copy(step, chunk).wait_send()


def gather_front(own, noisy, w_query, w_key, w_value, span, axes, chunks=4):
    rows, width = own.shape
    piece = rows // chunks
    vmem = pl.BlockSpec(memory_space=pltpu.VMEM)
    context = jax.ShapeDtypeStruct(((span + 1) * rows, width), jnp.bfloat16)
    local = jax.ShapeDtypeStruct((rows, width), jnp.bfloat16)
    flops = 2 * width * width * rows * (2 * (span + 1) + 3)
    return pl.pallas_call(
        functools.partial(gather_front_kernel, axes, span, chunks),
        out_shape=(context, context, local, local, local),
        in_specs=[vmem] * 5,
        out_specs=[vmem] * 5,
        scratch_shapes=[
            pltpu.VMEM((span, chunks, piece, width), own.dtype),
            pltpu.SemaphoreType.DMA((span, chunks)),
            pltpu.SemaphoreType.DMA((span, chunks)),
        ],
        cost_estimate=pl.CostEstimate(
            flops=flops, transcendentals=0,
            bytes_accessed=2 * width * (3 * width + (2 * span + 7) * rows),
        ),
        compiler_params=pltpu.CompilerParams(collective_id=2, has_side_effects=True),
    )(own, noisy, w_query, w_key, w_value)

def project(rows, weight):
    high = rows.astype(jnp.bfloat16)
    low = (rows - high.astype(jnp.float32)).astype(jnp.bfloat16)
    contract = (((1,), (1,)), ((), ()))
    product = lax.dot_general(high, weight, contract, preferred_element_type=jnp.float32)
    return product + lax.dot_general(low, weight, contract, preferred_element_type=jnp.float32)


def on_device(clean, out_cot, mask_bits, levels, importance, w_query, w_key, w_value, mask_embed):
    clean_rows = clean[0]
    cotangent = out_cot[0]
    tok_count = clean_rows.shape[0]
    width = clean_rows.shape[1]
    span = WINDOW // tok_count
    scale = 1.0 / math.sqrt(HEAD_DIM)
    position = lax.axis_index("seq") * tok_count
    within = jnp.arange(BLOCK, dtype=jnp.int32)
    block_bits = jnp.right_shift(mask_bits[0][:, None], within[None, :]) & 1
    bits = block_bits.reshape(tok_count)
    masked = bits == 1
    noisy = jnp.where(masked[:, None], mask_embed[None, :], clean_rows)
    key_clean, value_clean, query, key_noisy, value_noisy = gather_front(
        clean_rows, noisy, w_query, w_key, w_value, span, ("dp", "seq")
    )
    level_f = levels[0].astype(jnp.float32)
    ratio_f = importance[0].astype(jnp.float32)
    block_weight = LEVELS / level_f * (ratio_f[:, 0] / ratio_f[:, 1])
    token_weight = (block_weight[:, None] * block_bits.astype(jnp.float32)).reshape(tok_count)
    grad_out = (cotangent.astype(jnp.float32) * token_weight[:, None]).astype(jnp.bfloat16)
    place = jnp.reshape(span * tok_count - position, (1,)).astype(jnp.int32)
    attn_rows, dkey_rows, dvalue_rows = attention_heads(
        place, query, key_clean, value_clean, key_noisy, value_noisy, grad_out
    )
    raw = sum_back(dkey_rows, dvalue_rows, w_key.T, w_value.T, span, tok_count, ("dp", "seq"))
    squares = jnp.sum(raw * raw)
    total_squares = global_total(squares, ("dp", "seq"))
    entries = float(tok_count * width * lax.axis_size("dp") * lax.axis_size("seq"))
    rms = jnp.sqrt(total_squares / entries + EPS)
    factor = jnp.minimum(1.0, CLIP / rms)
    return (attn_rows[None], (raw * factor)[None])


def solution(mesh):
    in_specs = (
        P("dp", "seq", None),
        P("dp", "seq", None),
        P("dp", "seq"),
        P("dp", "seq"),
        P("dp", "seq", None),
        P(),
        P(),
        P(),
        P(),
    )
    out_specs = (P("dp", "seq", None), P("dp", "seq", None))
    return jax.shard_map(
        on_device, mesh=mesh, in_specs=in_specs, out_specs=out_specs, check_vma=False
    )
```

```python
import functools
import math

import jax
import jax.numpy as jnp
from jax import lax
from jax.sharding import PartitionSpec as P
from jax.experimental import pallas as pl
from jax.experimental.pallas import tpu as pltpu

HEADS = 12
HEAD_DIM = 64
BLOCK = 16
WINDOW = 1024
LEVELS = 16


EPS = 1e-06
CLIP = 0.25


def from_behind(block, axis, distance):
    devices = range(lax.axis_size(axis))
    route = [(i - distance, i) for i in devices if i - distance in devices]
    return lax.ppermute(block, axis, route)


def group_stages(axes):
    stages = []
    for axis in axes:
        rest, stride = lax.axis_size(axis), 1
        while rest > 1:
            size = max(g for g in range(1, 9) if rest % g == 0)
            stages.append((axis, stride, size))
            stride, rest = stride * size, rest // size
    return stages


def stage_peer(axis, stride, size, offset):
    index = lax.axis_index(axis)
    digit = (index // stride) % size
    return index + ((digit + offset) % size - digit) * stride


def device_of(axes, axis, peer):
    return tuple(peer if name == axis else lax.axis_index(name) for name in axes)


def greet_groups(axes, stages, barrier):
    count = 0
    for axis, stride, size in stages:
        for offset in range(1, size):
            peer = stage_peer(axis, stride, size, offset)
            pl.semaphore_signal(
                barrier, 1, device_id=device_of(axes, axis, peer),
                device_id_type=pl.DeviceIdType.MESH,
            )
            count += 1
    return count


def stage_total(axes, stages, current, slots, send_sems, recv_sems):
    for number, (axis, stride, size) in enumerate(stages):
        digit = (lax.axis_index(axis) // stride) % size
        slots[number, digit] = current
        copies = []
        for offset in range(1, size):
            peer = stage_peer(axis, stride, size, offset)
            copy = pltpu.make_async_remote_copy(
                src_ref=slots.at[number, digit],
                dst_ref=slots.at[number, digit],
                send_sem=send_sems.at[number, offset],
                recv_sem=recv_sems.at[number, offset],
                device_id=device_of(axes, axis, peer),
                device_id_type=pl.DeviceIdType.MESH,
            )
            copy.start()
            copies.append(copy)
        for copy in copies:
            copy.wait()
        current = slots[number, 0]
        for member in range(1, size):
            current = current + slots[number, member]
    return current


def total_kernel(axes, stages, part_ref, out_ref, slots, send_sems, recv_sems):
    barrier = pltpu.get_barrier_semaphore()
    pl.semaphore_wait(barrier, greet_groups(axes, stages, barrier))
    out_ref[...] = stage_total(axes, stages, part_ref[...], slots, send_sems, recv_sems)


def global_total(value, axes):
    stages = group_stages(axes)
    widest = max(size for _, _, size in stages)
    part = jnp.broadcast_to(value.astype(jnp.float32), (8, 128))
    summed = pl.pallas_call(
        functools.partial(total_kernel, axes, stages),
        out_shape=jax.ShapeDtypeStruct((8, 128), jnp.float32),
        in_specs=[pl.BlockSpec(memory_space=pltpu.VMEM)],
        out_specs=pl.BlockSpec(memory_space=pltpu.VMEM),
        scratch_shapes=[
            pltpu.VMEM((len(stages), widest, 8, 128), jnp.float32),
            pltpu.SemaphoreType.DMA((len(stages), widest)),
            pltpu.SemaphoreType.DMA((len(stages), widest)),
        ],
        compiler_params=pltpu.CompilerParams(collective_id=0, has_side_effects=True),
    )(part)
    return summed[0, 0]


def attention_kernel(place_ref, q_ref, kc_ref, vc_ref, kn_ref, vn_ref, g_ref,
                     out_ref, dk_ref, dv_ref):
    scale = 1.0 / math.sqrt(HEAD_DIM)
    query = q_ref[...]
    key_clean = kc_ref[...]
    value_clean = vc_ref[...]
    key_noisy = kn_ref[...]
    value_noisy = vn_ref[...]
    grad = g_ref[...]
    rows, lanes = query.shape
    context = key_clean.shape[0]
    row_block = lax.broadcasted_iota(jnp.int32, (rows, context), 0) // BLOCK * BLOCK
    col = lax.broadcasted_iota(jnp.int32, (rows, context), 1)
    allow_clean = (col >= row_block) & (col < row_block + WINDOW) & (col >= place_ref[0])
    own_row = lax.broadcasted_iota(jnp.int32, (rows, rows), 0) // BLOCK
    own_col = lax.broadcasted_iota(jnp.int32, (rows, rows), 1) // BLOCK
    allow_noisy = own_row == own_col
    lane = lax.broadcasted_iota(jnp.int32, (1, lanes), 1) // HEAD_DIM
    contract = (((1,), (1,)), ((), ()))
    lead = (((0,), (0,)), ((), ()))
    zero = jnp.zeros((), jnp.bfloat16)
    outs, dks, dvs = [], [], []
    for head in range(lanes // HEAD_DIM):
        mine = lane == head
        query_h = jnp.where(mine, query, zero)
        grad_h = jnp.where(mine, grad, zero)
        score_clean = lax.dot_general(query_h, key_clean, contract, preferred_element_type=jnp.float32) * scale
        score_noisy = lax.dot_general(query_h, key_noisy, contract, preferred_element_type=jnp.float32) * scale
        score_clean = jnp.where(allow_clean, score_clean, -jnp.inf)
        score_noisy = jnp.where(allow_noisy, score_noisy, -jnp.inf)
        peak = jnp.maximum(
            jnp.max(score_clean, axis=-1, keepdims=True), jnp.max(score_noisy, axis=-1, keepdims=True)
        )
        exp_clean = jnp.where(allow_clean, jnp.exp(score_clean - peak), 0.0)
        exp_noisy = jnp.where(allow_noisy, jnp.exp(score_noisy - peak), 0.0)
        denom = jnp.sum(exp_clean, axis=-1, keepdims=True) + jnp.sum(exp_noisy, axis=-1, keepdims=True)
        inverse = 1.0 / denom
        prob_clean = exp_clean * inverse
        weight_clean = prob_clean.astype(jnp.bfloat16)
        weight_noisy = (exp_noisy * inverse).astype(jnp.bfloat16)
        mixed = jnp.dot(weight_clean, value_clean, preferred_element_type=jnp.float32)
        mixed = mixed + jnp.dot(weight_noisy, value_noisy, preferred_element_type=jnp.float32)
        out_h = mixed.astype(jnp.bfloat16)
        delta = jnp.sum(
            jnp.where(mine, grad.astype(jnp.float32) * out_h.astype(jnp.float32), 0.0),
            axis=-1, keepdims=True,
        )
        dprob = lax.dot_general(grad_h, value_clean, contract, preferred_element_type=jnp.float32)
        dscore = (prob_clean * (dprob - delta) * scale).astype(jnp.bfloat16)
        outs.append(out_h)
        dks.append(lax.dot_general(dscore, query, lead, preferred_element_type=jnp.float32))
        dvs.append(lax.dot_general(weight_clean, grad, lead, preferred_element_type=jnp.float32))
    out, dk, dv = outs[0], dks[0], dvs[0]
    for head in range(1, len(outs)):
        mine = lane == head
        out = jnp.where(mine, outs[head], out)
        dk = jnp.where(mine, dks[head], dk)
        dv = jnp.where(mine, dvs[head], dv)
    out_ref[...] = out
    dk_ref[...] = dk
    dv_ref[...] = dv


def attention_heads(place, query, key_clean, value_clean, key_noisy, value_noisy, grad):
    rows, width = query.shape
    context = key_clean.shape[0]
    lanes = 2 * HEAD_DIM
    pairs = width // lanes
    row_spec = pl.BlockSpec((rows, lanes), lambda p, place: (0, p))
    ctx_spec = pl.BlockSpec((context, lanes), lambda p, place: (0, p))
    flops = pairs * 2 * 2 * lanes * (5 * rows * context + 3 * rows * rows)
    return pl.pallas_call(
        attention_kernel,
        out_shape=(
            jax.ShapeDtypeStruct((rows, width), jnp.bfloat16),
            jax.ShapeDtypeStruct((context, width), jnp.float32),
            jax.ShapeDtypeStruct((context, width), jnp.float32),
        ),
        grid_spec=pltpu.PrefetchScalarGridSpec(
            num_scalar_prefetch=1,
            grid=(pairs,),
            in_specs=[row_spec, ctx_spec, ctx_spec, row_spec, row_spec, row_spec],
            out_specs=[row_spec, ctx_spec, ctx_spec],
        ),
        cost_estimate=pl.CostEstimate(
            flops=flops,
            transcendentals=width // HEAD_DIM * rows * (context + rows),
            bytes_accessed=width * (8 * rows + 4 * context + 8 * context),
        ),
    )(place, query, key_clean, value_clean, key_noisy, value_noisy, grad)


def chain_barrier(axes, left, right, has_left, has_right, stages=()):
    barrier = pltpu.get_barrier_semaphore()
    greeted = greet_groups(axes, stages, barrier)
    for peer, present in ((left, has_left), (right, has_right)):
        @pl.when(present)
        def _():
            pl.semaphore_signal(
                barrier, 1, device_id=device_of(axes, "seq", peer),
                device_id_type=pl.DeviceIdType.MESH,
            )
    pl.semaphore_wait(barrier, has_left.astype(jnp.int32) + has_right.astype(jnp.int32) + greeted)


def chain_ends(axes):
    me = lax.axis_index("seq")
    size = lax.axis_size("seq")
    left = jnp.maximum(me - 1, 0)
    right = jnp.minimum(me + 1, size - 1)
    return me, left, right, me > 0, me < size - 1


def project_plain(rows, weight_ref):
    high = rows.astype(jnp.bfloat16)
    low = (rows - high.astype(jnp.float32)).astype(jnp.bfloat16)
    product = jnp.dot(high, weight_ref[...], preferred_element_type=jnp.float32)
    return product + jnp.dot(low, weight_ref[...], preferred_element_type=jnp.float32)


def sum_back_kernel(axes, span, chunks, stages, dk_ref, dv_ref, wk_ref, wv_ref, raw_ref, total_ref,
                    sent, got, send_sems, recv_sems, slots, total_send, total_recv):
    me, left, right, has_left, has_right = chain_ends(axes)
    chain_barrier(axes, left, right, has_left, has_right, stages)
    squares = jnp.zeros((1, 1), jnp.float32)
    rows = raw_ref.shape[0]
    piece = rows // chunks

    @pl.when(jnp.logical_not(has_right))
    def _():
        got[...] = jnp.zeros(got.shape, got.dtype)

    def copy(step, chunk):
        return pltpu.make_async_remote_copy(
            src_ref=sent.at[step, chunk], dst_ref=got.at[step, chunk],
            send_sem=send_sems.at[step, chunk], recv_sem=recv_sems.at[step, chunk],
            device_id=device_of(axes, "seq", left), device_id_type=pl.DeviceIdType.MESH,
        )

    for step in range(span + 1):
        for chunk in range(chunks):
            at = pl.ds(step * rows + chunk * piece, piece)
            value = project_plain(dk_ref[at, :], wk_ref) + project_plain(dv_ref[at, :], wv_ref)
            if step > 0:
                @pl.when(has_right)
                def _():
                    copy(step - 1, chunk).wait_recv()

                value = value + got[step - 1, chunk].astype(jnp.float32)
            if step < span:
                sent[step, chunk] = value.astype(jnp.bfloat16)

                @pl.when(has_left)
                def _():
                    copy(step, chunk).start()
            else:
                raw_ref[pl.ds(chunk * piece, piece), :] = value
                squares = squares + jnp.sum(value * value, axis=(0, 1), keepdims=True)
    total_ref[...] = stage_total(
        axes, stages, jnp.broadcast_to(squares, total_ref.shape), slots, total_send, total_recv
    )
    for step in range(span):
        for chunk in range(chunks):
            @pl.when(has_left)
            def _():
                copy(step, chunk).wait_send()


def sum_back(dk, dv, w_key, w_value, span, rows, axes, chunks=4):
    width = dk.shape[1]
    piece = rows // chunks
    stages = group_stages(axes)
    widest = max(size for _, _, size in stages)
    vmem = pl.BlockSpec(memory_space=pltpu.VMEM)
    return pl.pallas_call(
        functools.partial(sum_back_kernel, axes, span, chunks, stages),
        out_shape=(
            jax.ShapeDtypeStruct((rows, width), jnp.float32),
            jax.ShapeDtypeStruct((8, 128), jnp.float32),
        ),
        in_specs=[vmem] * 4,
        out_specs=[vmem, vmem],
        scratch_shapes=[
            pltpu.VMEM((span, chunks, piece, width), jnp.bfloat16),
            pltpu.VMEM((span, chunks, piece, width), jnp.bfloat16),
            pltpu.SemaphoreType.DMA((span, chunks)),
            pltpu.SemaphoreType.DMA((span, chunks)),
            pltpu.VMEM((len(stages), widest, 8, 128), jnp.float32),
            pltpu.SemaphoreType.DMA((len(stages), widest)),
            pltpu.SemaphoreType.DMA((len(stages), widest)),
        ],
        cost_estimate=pl.CostEstimate(
            flops=8 * width * width * rows * (span + 1), transcendentals=0,
            bytes_accessed=4 * width * (2 * (span + 1) * rows + rows + width),
        ),
        compiler_params=pltpu.CompilerParams(collective_id=1, has_side_effects=True),
    )(dk, dv, w_key, w_value)


def gather_front_kernel(axes, span, chunks, own_ref, noisy_ref, wq_ref, wk_ref, wv_ref,
                        kc_ref, vc_ref, q_ref, kn_ref, vn_ref, got, send_sems, recv_sems):
    me, left, right, has_left, has_right = chain_ends(axes)
    chain_barrier(axes, left, right, has_left, has_right)
    rows = own_ref.shape[0]
    piece = rows // chunks
    for step in range(span):
        @pl.when(step >= me)
        def _():
            got[step] = jnp.zeros(got.shape[1:], got.dtype)

    def copy(step, chunk):
        if step == 0:
            source = own_ref.at[pl.ds(chunk * piece, piece)]
        else:
            source = got.at[step - 1, chunk]
        return pltpu.make_async_remote_copy(
            src_ref=source, dst_ref=got.at[step, chunk],
            send_sem=send_sems.at[step, chunk], recv_sem=recv_sems.at[step, chunk],
            device_id=device_of(axes, "seq", right), device_id_type=pl.DeviceIdType.MESH,
        )

    def project_rows(rows_in, weight_ref):
        return jnp.dot(rows_in, weight_ref[...], preferred_element_type=jnp.float32).astype(
            jnp.bfloat16
        )

    for chunk in range(chunks):
        @pl.when(has_right)
        def _():
            copy(0, chunk).start()
    noisy = noisy_ref[...]
    q_ref[...] = project_rows(noisy, wq_ref)
    kn_ref[...] = project_rows(noisy, wk_ref)
    vn_ref[...] = project_rows(noisy, wv_ref)
    own = own_ref[...]
    kc_ref[pl.ds(span * rows, rows), :] = project_rows(own, wk_ref)
    vc_ref[pl.ds(span * rows, rows), :] = project_rows(own, wv_ref)
    for step in range(1, span + 1):
        for chunk in range(chunks):
            @pl.when(step <= me)
            def _():
                copy(step - 1, chunk).wait_recv()
            if step < span:
                @pl.when(has_right & (step <= me))
                def _():
                    copy(step, chunk).start()
            arrived = got[step - 1, chunk]
            start = (span - step) * rows + chunk * piece
            kc_ref[pl.ds(start, piece), :] = project_rows(arrived, wk_ref)
            vc_ref[pl.ds(start, piece), :] = project_rows(arrived, wv_ref)
    for step in range(span):
        for chunk in range(chunks):
            @pl.when(has_right & (step <= me))
            def _():
                copy(step, chunk).wait_send()


def gather_front(own, noisy, w_query, w_key, w_value, span, axes, chunks=4):
    rows, width = own.shape
    piece = rows // chunks
    vmem = pl.BlockSpec(memory_space=pltpu.VMEM)
    context = jax.ShapeDtypeStruct(((span + 1) * rows, width), jnp.bfloat16)
    local = jax.ShapeDtypeStruct((rows, width), jnp.bfloat16)
    flops = 2 * width * width * rows * (2 * (span + 1) + 3)
    return pl.pallas_call(
        functools.partial(gather_front_kernel, axes, span, chunks),
        out_shape=(context, context, local, local, local),
        in_specs=[vmem] * 5,
        out_specs=[vmem] * 5,
        scratch_shapes=[
            pltpu.VMEM((span, chunks, piece, width), own.dtype),
            pltpu.SemaphoreType.DMA((span, chunks)),
            pltpu.SemaphoreType.DMA((span, chunks)),
        ],
        cost_estimate=pl.CostEstimate(
            flops=flops, transcendentals=0,
            bytes_accessed=2 * width * (3 * width + (2 * span + 7) * rows),
        ),
        compiler_params=pltpu.CompilerParams(collective_id=2, has_side_effects=True),
    )(own, noisy, w_query, w_key, w_value)

def project(rows, weight):
    high = rows.astype(jnp.bfloat16)
    low = (rows - high.astype(jnp.float32)).astype(jnp.bfloat16)
    contract = (((1,), (1,)), ((), ()))
    product = lax.dot_general(high, weight, contract, preferred_element_type=jnp.float32)
    return product + lax.dot_general(low, weight, contract, preferred_element_type=jnp.float32)


def on_device(clean, out_cot, mask_bits, levels, importance, w_query, w_key, w_value, mask_embed):
    clean_rows = clean[0]
    cotangent = out_cot[0]
    tok_count = clean_rows.shape[0]
    width = clean_rows.shape[1]
    span = WINDOW // tok_count
    scale = 1.0 / math.sqrt(HEAD_DIM)
    position = lax.axis_index("seq") * tok_count
    within = jnp.arange(BLOCK, dtype=jnp.int32)
    block_bits = jnp.right_shift(mask_bits[0][:, None], within[None, :]) & 1
    bits = block_bits.reshape(tok_count)
    masked = bits == 1
    noisy = jnp.where(masked[:, None], mask_embed[None, :], clean_rows)
    key_clean, value_clean, query, key_noisy, value_noisy = gather_front(
        clean_rows, noisy, w_query, w_key, w_value, span, ("dp", "seq")
    )
    level_f = levels[0].astype(jnp.float32)
    ratio_f = importance[0].astype(jnp.float32)
    block_weight = LEVELS / level_f * (ratio_f[:, 0] / ratio_f[:, 1])
    token_weight = (block_weight[:, None] * block_bits.astype(jnp.float32)).reshape(tok_count)
    grad_out = (cotangent.astype(jnp.float32) * token_weight[:, None]).astype(jnp.bfloat16)
    place = jnp.reshape(span * tok_count - position, (1,)).astype(jnp.int32)
    attn_rows, dkey_rows, dvalue_rows = attention_heads(
        place, query, key_clean, value_clean, key_noisy, value_noisy, grad_out
    )
    raw, total = sum_back(dkey_rows, dvalue_rows, w_key.T, w_value.T, span, tok_count, ("dp", "seq"))
    total_squares = total[0, 0]
    entries = float(tok_count * width * lax.axis_size("dp") * lax.axis_size("seq"))
    rms = jnp.sqrt(total_squares / entries + EPS)
    factor = jnp.minimum(1.0, CLIP / rms)
    return (attn_rows[None], (raw * factor)[None])


def solution(mesh):
    in_specs = (
        P("dp", "seq", None),
        P("dp", "seq", None),
        P("dp", "seq"),
        P("dp", "seq"),
        P("dp", "seq", None),
        P(),
        P(),
        P(),
        P(),
    )
    out_specs = (P("dp", "seq", None), P("dp", "seq", None))
    return jax.shard_map(
        on_device, mesh=mesh, in_specs=in_specs, out_specs=out_specs, check_vma=False
    )
```

```python
import functools
import math

import jax
import jax.numpy as jnp
from jax import lax
from jax.sharding import PartitionSpec as P
from jax.experimental import pallas as pl
from jax.experimental.pallas import tpu as pltpu

HEADS = 12
HEAD_DIM = 64
BLOCK = 16
WINDOW = 1024
LEVELS = 16


EPS = 1e-06
CLIP = 0.25


def from_behind(block, axis, distance):
    devices = range(lax.axis_size(axis))
    route = [(i - distance, i) for i in devices if i - distance in devices]
    return lax.ppermute(block, axis, route)


def group_stages(axes):
    stages = []
    for axis in axes:
        rest, stride = lax.axis_size(axis), 1
        while rest > 1:
            size = max(g for g in range(1, 9) if rest % g == 0)
            stages.append((axis, stride, size))
            stride, rest = stride * size, rest // size
    return stages


def stage_peer(axis, stride, size, offset):
    index = lax.axis_index(axis)
    digit = (index // stride) % size
    return index + ((digit + offset) % size - digit) * stride


def device_of(axes, axis, peer):
    return tuple(peer if name == axis else lax.axis_index(name) for name in axes)


def greet_groups(axes, stages, barrier):
    count = 0
    for axis, stride, size in stages:
        for offset in range(1, size):
            peer = stage_peer(axis, stride, size, offset)
            pl.semaphore_signal(
                barrier, 1, device_id=device_of(axes, axis, peer),
                device_id_type=pl.DeviceIdType.MESH,
            )
            count += 1
    return count


def stage_total(axes, stages, current, slots, send_sems, recv_sems):
    for number, (axis, stride, size) in enumerate(stages):
        digit = (lax.axis_index(axis) // stride) % size
        slots[number, digit] = current
        copies = []
        for offset in range(1, size):
            peer = stage_peer(axis, stride, size, offset)
            copy = pltpu.make_async_remote_copy(
                src_ref=slots.at[number, digit],
                dst_ref=slots.at[number, digit],
                send_sem=send_sems.at[number, offset],
                recv_sem=recv_sems.at[number, offset],
                device_id=device_of(axes, axis, peer),
                device_id_type=pl.DeviceIdType.MESH,
            )
            copy.start()
            copies.append(copy)
        for copy in copies:
            copy.wait()
        current = slots[number, 0]
        for member in range(1, size):
            current = current + slots[number, member]
    return current


def total_kernel(axes, stages, part_ref, out_ref, slots, send_sems, recv_sems):
    barrier = pltpu.get_barrier_semaphore()
    pl.semaphore_wait(barrier, greet_groups(axes, stages, barrier))
    out_ref[...] = stage_total(axes, stages, part_ref[...], slots, send_sems, recv_sems)


def global_total(value, axes):
    stages = group_stages(axes)
    widest = max(size for _, _, size in stages)
    part = jnp.broadcast_to(value.astype(jnp.float32), (8, 128))
    summed = pl.pallas_call(
        functools.partial(total_kernel, axes, stages),
        out_shape=jax.ShapeDtypeStruct((8, 128), jnp.float32),
        in_specs=[pl.BlockSpec(memory_space=pltpu.VMEM)],
        out_specs=pl.BlockSpec(memory_space=pltpu.VMEM),
        scratch_shapes=[
            pltpu.VMEM((len(stages), widest, 8, 128), jnp.float32),
            pltpu.SemaphoreType.DMA((len(stages), widest)),
            pltpu.SemaphoreType.DMA((len(stages), widest)),
        ],
        compiler_params=pltpu.CompilerParams(collective_id=0, has_side_effects=True),
    )(part)
    return summed[0, 0]


def attention_kernel(place_ref, q_ref, kc_ref, vc_ref, kn_ref, vn_ref, g_ref,
                     out_ref, dk_ref, dv_ref):
    scale = 1.0 / math.sqrt(HEAD_DIM)
    query = q_ref[...]
    key_clean = kc_ref[...]
    value_clean = vc_ref[...]
    key_noisy = kn_ref[...]
    value_noisy = vn_ref[...]
    grad = g_ref[...]
    rows, lanes = query.shape
    context = key_clean.shape[0]
    row_block = lax.broadcasted_iota(jnp.int32, (rows, context), 0) // BLOCK * BLOCK
    col = lax.broadcasted_iota(jnp.int32, (rows, context), 1)
    allow_clean = (col >= row_block) & (col < row_block + WINDOW) & (col >= place_ref[0])
    own_row = lax.broadcasted_iota(jnp.int32, (rows, rows), 0) // BLOCK
    own_col = lax.broadcasted_iota(jnp.int32, (rows, rows), 1) // BLOCK
    allow_noisy = own_row == own_col
    lane = lax.broadcasted_iota(jnp.int32, (1, lanes), 1) // HEAD_DIM
    contract = (((1,), (1,)), ((), ()))
    lead = (((0,), (0,)), ((), ()))
    zero = jnp.zeros((), jnp.bfloat16)
    outs, dks, dvs = [], [], []
    for head in range(lanes // HEAD_DIM):
        mine = lane == head
        query_h = jnp.where(mine, query, zero)
        grad_h = jnp.where(mine, grad, zero)
        score_clean = lax.dot_general(query_h, key_clean, contract, preferred_element_type=jnp.float32) * scale
        score_noisy = lax.dot_general(query_h, key_noisy, contract, preferred_element_type=jnp.float32) * scale
        score_clean = jnp.where(allow_clean, score_clean, -jnp.inf)
        score_noisy = jnp.where(allow_noisy, score_noisy, -jnp.inf)
        peak = jnp.maximum(
            jnp.max(score_clean, axis=-1, keepdims=True), jnp.max(score_noisy, axis=-1, keepdims=True)
        )
        exp_clean = jnp.where(allow_clean, jnp.exp(score_clean - peak), 0.0)
        exp_noisy = jnp.where(allow_noisy, jnp.exp(score_noisy - peak), 0.0)
        denom = jnp.sum(exp_clean, axis=-1, keepdims=True) + jnp.sum(exp_noisy, axis=-1, keepdims=True)
        inverse = 1.0 / denom
        prob_clean = exp_clean * inverse
        weight_clean = prob_clean.astype(jnp.bfloat16)
        weight_noisy = (exp_noisy * inverse).astype(jnp.bfloat16)
        mixed = jnp.dot(weight_clean, value_clean, preferred_element_type=jnp.float32)
        mixed = mixed + jnp.dot(weight_noisy, value_noisy, preferred_element_type=jnp.float32)
        out_h = mixed.astype(jnp.bfloat16)
        delta = jnp.sum(
            jnp.where(mine, grad.astype(jnp.float32) * out_h.astype(jnp.float32), 0.0),
            axis=-1, keepdims=True,
        )
        dprob = lax.dot_general(grad_h, value_clean, contract, preferred_element_type=jnp.float32)
        dscore = (prob_clean * (dprob - delta) * scale).astype(jnp.bfloat16)
        outs.append(out_h)
        dks.append(lax.dot_general(dscore, query, lead, preferred_element_type=jnp.float32))
        dvs.append(lax.dot_general(weight_clean, grad, lead, preferred_element_type=jnp.float32))
    out, dk, dv = outs[0], dks[0], dvs[0]
    for head in range(1, len(outs)):
        mine = lane == head
        out = jnp.where(mine, outs[head], out)
        dk = jnp.where(mine, dks[head], dk)
        dv = jnp.where(mine, dvs[head], dv)
    out_ref[...] = out
    dk_ref[...] = dk
    dv_ref[...] = dv


def attention_heads(place, query, key_clean, value_clean, key_noisy, value_noisy, grad):
    rows, width = query.shape
    context = key_clean.shape[0]
    lanes = 2 * HEAD_DIM
    pairs = width // lanes
    row_spec = pl.BlockSpec((rows, lanes), lambda p, place: (0, p))
    ctx_spec = pl.BlockSpec((context, lanes), lambda p, place: (0, p))
    flops = pairs * 2 * 2 * lanes * (5 * rows * context + 3 * rows * rows)
    return pl.pallas_call(
        attention_kernel,
        out_shape=(
            jax.ShapeDtypeStruct((rows, width), jnp.bfloat16),
            jax.ShapeDtypeStruct((context, width), jnp.float32),
            jax.ShapeDtypeStruct((context, width), jnp.float32),
        ),
        grid_spec=pltpu.PrefetchScalarGridSpec(
            num_scalar_prefetch=1,
            grid=(pairs,),
            in_specs=[row_spec, ctx_spec, ctx_spec, row_spec, row_spec, row_spec],
            out_specs=[row_spec, ctx_spec, ctx_spec],
        ),
        cost_estimate=pl.CostEstimate(
            flops=flops,
            transcendentals=width // HEAD_DIM * rows * (context + rows),
            bytes_accessed=width * (8 * rows + 4 * context + 8 * context),
        ),
    )(place, query, key_clean, value_clean, key_noisy, value_noisy, grad)


def chain_barrier(axes, left, right, has_left, has_right, stages=()):
    barrier = pltpu.get_barrier_semaphore()
    greeted = greet_groups(axes, stages, barrier)
    for peer, present in ((left, has_left), (right, has_right)):
        @pl.when(present)
        def _():
            pl.semaphore_signal(
                barrier, 1, device_id=device_of(axes, "seq", peer),
                device_id_type=pl.DeviceIdType.MESH,
            )
    pl.semaphore_wait(barrier, has_left.astype(jnp.int32) + has_right.astype(jnp.int32) + greeted)


def chain_ends(axes):
    me = lax.axis_index("seq")
    size = lax.axis_size("seq")
    left = jnp.maximum(me - 1, 0)
    right = jnp.minimum(me + 1, size - 1)
    return me, left, right, me > 0, me < size - 1


def project_plain(rows, weight_ref):
    high = rows.astype(jnp.bfloat16)
    low = (rows - high.astype(jnp.float32)).astype(jnp.bfloat16)
    product = jnp.dot(high, weight_ref[...], preferred_element_type=jnp.float32)
    return product + jnp.dot(low, weight_ref[...], preferred_element_type=jnp.float32)


def sum_back_kernel(axes, span, chunks, stages, dk_ref, dv_ref, wk_ref, wv_ref, raw_ref, total_ref,
                    sent, got, send_sems, recv_sems, slots, total_send, total_recv):
    me, left, right, has_left, has_right = chain_ends(axes)
    chain_barrier(axes, left, right, has_left, has_right, stages)
    squares = jnp.zeros((1, 1), jnp.float32)
    rows = raw_ref.shape[0]
    piece = rows // chunks

    @pl.when(jnp.logical_not(has_right))
    def _():
        got[...] = jnp.zeros(got.shape, got.dtype)

    def copy(step, chunk):
        return pltpu.make_async_remote_copy(
            src_ref=sent.at[step, chunk], dst_ref=got.at[step, chunk],
            send_sem=send_sems.at[step, chunk], recv_sem=recv_sems.at[step, chunk],
            device_id=device_of(axes, "seq", left), device_id_type=pl.DeviceIdType.MESH,
        )

    for step in range(span + 1):
        at = pl.ds(step * rows, rows)
        term = project_plain(dk_ref[at, :], wk_ref) + project_plain(dv_ref[at, :], wv_ref)
        for chunk in range(chunks):
            value = term[chunk * piece:(chunk + 1) * piece]
            if step > 0:
                @pl.when(has_right)
                def _():
                    copy(step - 1, chunk).wait_recv()

                value = value + got[step - 1, chunk].astype(jnp.float32)
            if step < span:
                sent[step, chunk] = value.astype(jnp.bfloat16)

                @pl.when(has_left)
                def _():
                    copy(step, chunk).start()
            else:
                raw_ref[pl.ds(chunk * piece, piece), :] = value
                squares = squares + jnp.sum(value * value, axis=(0, 1), keepdims=True)
    total_ref[...] = stage_total(
        axes, stages, jnp.broadcast_to(squares, total_ref.shape), slots, total_send, total_recv
    )
    for step in range(span):
        for chunk in range(chunks):
            @pl.when(has_left)
            def _():
                copy(step, chunk).wait_send()


def sum_back(dk, dv, w_key, w_value, span, rows, axes, chunks=4):
    width = dk.shape[1]
    piece = rows // chunks
    stages = group_stages(axes)
    widest = max(size for _, _, size in stages)
    vmem = pl.BlockSpec(memory_space=pltpu.VMEM)
    return pl.pallas_call(
        functools.partial(sum_back_kernel, axes, span, chunks, stages),
        out_shape=(
            jax.ShapeDtypeStruct((rows, width), jnp.float32),
            jax.ShapeDtypeStruct((8, 128), jnp.float32),
        ),
        in_specs=[vmem] * 4,
        out_specs=[vmem, vmem],
        scratch_shapes=[
            pltpu.VMEM((span, chunks, piece, width), jnp.bfloat16),
            pltpu.VMEM((span, chunks, piece, width), jnp.bfloat16),
            pltpu.SemaphoreType.DMA((span, chunks)),
            pltpu.SemaphoreType.DMA((span, chunks)),
            pltpu.VMEM((len(stages), widest, 8, 128), jnp.float32),
            pltpu.SemaphoreType.DMA((len(stages), widest)),
            pltpu.SemaphoreType.DMA((len(stages), widest)),
        ],
        cost_estimate=pl.CostEstimate(
            flops=8 * width * width * rows * (span + 1), transcendentals=0,
            bytes_accessed=4 * width * (2 * (span + 1) * rows + rows + width),
        ),
        compiler_params=pltpu.CompilerParams(collective_id=1, has_side_effects=True),
    )(dk, dv, w_key, w_value)


def gather_front_kernel(axes, span, chunks, own_ref, noisy_ref, wq_ref, wk_ref, wv_ref,
                        kc_ref, vc_ref, q_ref, kn_ref, vn_ref, got, send_sems, recv_sems):
    me, left, right, has_left, has_right = chain_ends(axes)
    chain_barrier(axes, left, right, has_left, has_right)
    rows = own_ref.shape[0]
    piece = rows // chunks
    for step in range(span):
        @pl.when(step >= me)
        def _():
            got[step] = jnp.zeros(got.shape[1:], got.dtype)

    def copy(step, chunk):
        if step == 0:
            source = own_ref.at[pl.ds(chunk * piece, piece)]
        else:
            source = got.at[step - 1, chunk]
        return pltpu.make_async_remote_copy(
            src_ref=source, dst_ref=got.at[step, chunk],
            send_sem=send_sems.at[step, chunk], recv_sem=recv_sems.at[step, chunk],
            device_id=device_of(axes, "seq", right), device_id_type=pl.DeviceIdType.MESH,
        )

    def project_rows(rows_in, weight_ref):
        return jnp.dot(rows_in, weight_ref[...], preferred_element_type=jnp.float32).astype(
            jnp.bfloat16
        )

    for chunk in range(chunks):
        @pl.when(has_right)
        def _():
            copy(0, chunk).start()
    noisy = noisy_ref[...]
    q_ref[...] = project_rows(noisy, wq_ref)
    kn_ref[...] = project_rows(noisy, wk_ref)
    vn_ref[...] = project_rows(noisy, wv_ref)
    own = own_ref[...]
    kc_ref[pl.ds(span * rows, rows), :] = project_rows(own, wk_ref)
    vc_ref[pl.ds(span * rows, rows), :] = project_rows(own, wv_ref)
    for step in range(1, span + 1):
        for chunk in range(chunks):
            @pl.when(step <= me)
            def _():
                copy(step - 1, chunk).wait_recv()
            if step < span:
                @pl.when(has_right & (step <= me))
                def _():
                    copy(step, chunk).start()
        arrived = got[step - 1].reshape(rows, -1)
        kc_ref[pl.ds((span - step) * rows, rows), :] = project_rows(arrived, wk_ref)
        vc_ref[pl.ds((span - step) * rows, rows), :] = project_rows(arrived, wv_ref)
    for step in range(span):
        for chunk in range(chunks):
            @pl.when(has_right & (step <= me))
            def _():
                copy(step, chunk).wait_send()


def gather_front(own, noisy, w_query, w_key, w_value, span, axes, chunks=4):
    rows, width = own.shape
    piece = rows // chunks
    vmem = pl.BlockSpec(memory_space=pltpu.VMEM)
    context = jax.ShapeDtypeStruct(((span + 1) * rows, width), jnp.bfloat16)
    local = jax.ShapeDtypeStruct((rows, width), jnp.bfloat16)
    flops = 2 * width * width * rows * (2 * (span + 1) + 3)
    return pl.pallas_call(
        functools.partial(gather_front_kernel, axes, span, chunks),
        out_shape=(context, context, local, local, local),
        in_specs=[vmem] * 5,
        out_specs=[vmem] * 5,
        scratch_shapes=[
            pltpu.VMEM((span, chunks, piece, width), own.dtype),
            pltpu.SemaphoreType.DMA((span, chunks)),
            pltpu.SemaphoreType.DMA((span, chunks)),
        ],
        cost_estimate=pl.CostEstimate(
            flops=flops, transcendentals=0,
            bytes_accessed=2 * width * (3 * width + (2 * span + 7) * rows),
        ),
        compiler_params=pltpu.CompilerParams(collective_id=2, has_side_effects=True),
    )(own, noisy, w_query, w_key, w_value)

def project(rows, weight):
    high = rows.astype(jnp.bfloat16)
    low = (rows - high.astype(jnp.float32)).astype(jnp.bfloat16)
    contract = (((1,), (1,)), ((), ()))
    product = lax.dot_general(high, weight, contract, preferred_element_type=jnp.float32)
    return product + lax.dot_general(low, weight, contract, preferred_element_type=jnp.float32)


def on_device(clean, out_cot, mask_bits, levels, importance, w_query, w_key, w_value, mask_embed):
    clean_rows = clean[0]
    cotangent = out_cot[0]
    tok_count = clean_rows.shape[0]
    width = clean_rows.shape[1]
    span = WINDOW // tok_count
    scale = 1.0 / math.sqrt(HEAD_DIM)
    position = lax.axis_index("seq") * tok_count
    within = jnp.arange(BLOCK, dtype=jnp.int32)
    block_bits = jnp.right_shift(mask_bits[0][:, None], within[None, :]) & 1
    bits = block_bits.reshape(tok_count)
    masked = bits == 1
    noisy = jnp.where(masked[:, None], mask_embed[None, :], clean_rows)
    key_clean, value_clean, query, key_noisy, value_noisy = gather_front(
        clean_rows, noisy, w_query, w_key, w_value, span, ("dp", "seq")
    )
    level_f = levels[0].astype(jnp.float32)
    ratio_f = importance[0].astype(jnp.float32)
    block_weight = LEVELS / level_f * (ratio_f[:, 0] / ratio_f[:, 1])
    token_weight = (block_weight[:, None] * block_bits.astype(jnp.float32)).reshape(tok_count)
    grad_out = (cotangent.astype(jnp.float32) * token_weight[:, None]).astype(jnp.bfloat16)
    place = jnp.reshape(span * tok_count - position, (1,)).astype(jnp.int32)
    attn_rows, dkey_rows, dvalue_rows = attention_heads(
        place, query, key_clean, value_clean, key_noisy, value_noisy, grad_out
    )
    raw, total = sum_back(dkey_rows, dvalue_rows, w_key.T, w_value.T, span, tok_count, ("dp", "seq"))
    total_squares = total[0, 0]
    entries = float(tok_count * width * lax.axis_size("dp") * lax.axis_size("seq"))
    rms = jnp.sqrt(total_squares / entries + EPS)
    factor = jnp.minimum(1.0, CLIP / rms)
    return (attn_rows[None], (raw * factor)[None])


def solution(mesh):
    in_specs = (
        P("dp", "seq", None),
        P("dp", "seq", None),
        P("dp", "seq"),
        P("dp", "seq"),
        P("dp", "seq", None),
        P(),
        P(),
        P(),
        P(),
    )
    out_specs = (P("dp", "seq", None), P("dp", "seq", None))
    return jax.shard_map(
        on_device, mesh=mesh, in_specs=in_specs, out_specs=out_specs, check_vma=False
    )
```

```python
import functools
import math

import jax
import jax.numpy as jnp
from jax import lax
from jax.sharding import PartitionSpec as P
from jax.experimental import pallas as pl
from jax.experimental.pallas import tpu as pltpu

HEADS = 12
HEAD_DIM = 64
BLOCK = 16
WINDOW = 1024
LEVELS = 16


EPS = 1e-06
CLIP = 0.25


def from_behind(block, axis, distance):
    devices = range(lax.axis_size(axis))
    route = [(i - distance, i) for i in devices if i - distance in devices]
    return lax.ppermute(block, axis, route)


def group_stages(axes):
    stages = []
    for axis in axes:
        rest, stride = lax.axis_size(axis), 1
        while rest > 1:
            size = max(g for g in range(1, 9) if rest % g == 0)
            stages.append((axis, stride, size))
            stride, rest = stride * size, rest // size
    return stages


def stage_peer(axis, stride, size, offset):
    index = lax.axis_index(axis)
    digit = (index // stride) % size
    return index + ((digit + offset) % size - digit) * stride


def device_of(axes, axis, peer):
    return tuple(peer if name == axis else lax.axis_index(name) for name in axes)


def greet_groups(axes, stages, barrier):
    count = 0
    for axis, stride, size in stages:
        for offset in range(1, size):
            peer = stage_peer(axis, stride, size, offset)
            pl.semaphore_signal(
                barrier, 1, device_id=device_of(axes, axis, peer),
                device_id_type=pl.DeviceIdType.MESH,
            )
            count += 1
    return count


def stage_total(axes, stages, current, slots, send_sems, recv_sems):
    for number, (axis, stride, size) in enumerate(stages):
        digit = (lax.axis_index(axis) // stride) % size
        slots[number, digit] = current
        copies = []
        for offset in range(1, size):
            peer = stage_peer(axis, stride, size, offset)
            copy = pltpu.make_async_remote_copy(
                src_ref=slots.at[number, digit],
                dst_ref=slots.at[number, digit],
                send_sem=send_sems.at[number, offset],
                recv_sem=recv_sems.at[number, offset],
                device_id=device_of(axes, axis, peer),
                device_id_type=pl.DeviceIdType.MESH,
            )
            copy.start()
            copies.append(copy)
        for copy in copies:
            copy.wait()
        current = slots[number, 0]
        for member in range(1, size):
            current = current + slots[number, member]
    return current


def total_kernel(axes, stages, part_ref, out_ref, slots, send_sems, recv_sems):
    barrier = pltpu.get_barrier_semaphore()
    pl.semaphore_wait(barrier, greet_groups(axes, stages, barrier))
    out_ref[...] = stage_total(axes, stages, part_ref[...], slots, send_sems, recv_sems)


def global_total(value, axes):
    stages = group_stages(axes)
    widest = max(size for _, _, size in stages)
    part = jnp.broadcast_to(value.astype(jnp.float32), (8, 128))
    summed = pl.pallas_call(
        functools.partial(total_kernel, axes, stages),
        out_shape=jax.ShapeDtypeStruct((8, 128), jnp.float32),
        in_specs=[pl.BlockSpec(memory_space=pltpu.VMEM)],
        out_specs=pl.BlockSpec(memory_space=pltpu.VMEM),
        scratch_shapes=[
            pltpu.VMEM((len(stages), widest, 8, 128), jnp.float32),
            pltpu.SemaphoreType.DMA((len(stages), widest)),
            pltpu.SemaphoreType.DMA((len(stages), widest)),
        ],
        compiler_params=pltpu.CompilerParams(collective_id=0, has_side_effects=True),
    )(part)
    return summed[0, 0]


def attention_kernel(place_ref, q_ref, kc_ref, vc_ref, kn_ref, vn_ref, g_ref,
                     out_ref, dk_ref, dv_ref):
    scale = 1.0 / math.sqrt(HEAD_DIM)
    query = q_ref[...]
    key_clean = kc_ref[...]
    value_clean = vc_ref[...]
    key_noisy = kn_ref[...]
    value_noisy = vn_ref[...]
    grad = g_ref[...]
    rows, lanes = query.shape
    context = key_clean.shape[0]
    row_block = lax.broadcasted_iota(jnp.int32, (rows, context), 0) // BLOCK * BLOCK
    col = lax.broadcasted_iota(jnp.int32, (rows, context), 1)
    allow_clean = (col >= row_block) & (col < row_block + WINDOW) & (col >= place_ref[0])
    own_row = lax.broadcasted_iota(jnp.int32, (rows, rows), 0) // BLOCK
    own_col = lax.broadcasted_iota(jnp.int32, (rows, rows), 1) // BLOCK
    allow_noisy = own_row == own_col
    lane = lax.broadcasted_iota(jnp.int32, (1, lanes), 1) // HEAD_DIM
    contract = (((1,), (1,)), ((), ()))
    lead = (((0,), (0,)), ((), ()))
    zero = jnp.zeros((), jnp.bfloat16)
    outs, dks, dvs = [], [], []
    for head in range(lanes // HEAD_DIM):
        mine = lane == head
        query_h = jnp.where(mine, query, zero)
        grad_h = jnp.where(mine, grad, zero)
        score_clean = lax.dot_general(query_h, key_clean, contract, preferred_element_type=jnp.float32) * scale
        score_noisy = lax.dot_general(query_h, key_noisy, contract, preferred_element_type=jnp.float32) * scale
        score_clean = jnp.where(allow_clean, score_clean, -jnp.inf)
        score_noisy = jnp.where(allow_noisy, score_noisy, -jnp.inf)
        peak = jnp.maximum(
            jnp.max(score_clean, axis=-1, keepdims=True), jnp.max(score_noisy, axis=-1, keepdims=True)
        )
        exp_clean = jnp.where(allow_clean, jnp.exp(score_clean - peak), 0.0)
        exp_noisy = jnp.where(allow_noisy, jnp.exp(score_noisy - peak), 0.0)
        denom = jnp.sum(exp_clean, axis=-1, keepdims=True) + jnp.sum(exp_noisy, axis=-1, keepdims=True)
        inverse = 1.0 / denom
        prob_clean = exp_clean * inverse
        weight_clean = prob_clean.astype(jnp.bfloat16)
        weight_noisy = (exp_noisy * inverse).astype(jnp.bfloat16)
        mixed = jnp.dot(weight_clean, value_clean, preferred_element_type=jnp.float32)
        mixed = mixed + jnp.dot(weight_noisy, value_noisy, preferred_element_type=jnp.float32)
        out_h = mixed.astype(jnp.bfloat16)
        delta = jnp.sum(
            jnp.where(mine, grad.astype(jnp.float32) * out_h.astype(jnp.float32), 0.0),
            axis=-1, keepdims=True,
        )
        dprob = lax.dot_general(grad_h, value_clean, contract, preferred_element_type=jnp.float32)
        dscore = (prob_clean * (dprob - delta) * scale).astype(jnp.bfloat16)
        outs.append(out_h)
        dks.append(lax.dot_general(dscore, query, lead, preferred_element_type=jnp.float32))
        dvs.append(lax.dot_general(weight_clean, grad, lead, preferred_element_type=jnp.float32))
    out, dk, dv = outs[0], dks[0], dvs[0]
    for head in range(1, len(outs)):
        mine = lane == head
        out = jnp.where(mine, outs[head], out)
        dk = jnp.where(mine, dks[head], dk)
        dv = jnp.where(mine, dvs[head], dv)
    out_ref[...] = out
    dk_ref[...] = dk
    dv_ref[...] = dv


def attention_heads(place, query, key_clean, value_clean, key_noisy, value_noisy, grad):
    rows, width = query.shape
    context = key_clean.shape[0]
    lanes = 2 * HEAD_DIM
    pairs = width // lanes
    row_spec = pl.BlockSpec((rows, lanes), lambda p, place: (0, p))
    ctx_spec = pl.BlockSpec((context, lanes), lambda p, place: (0, p))
    flops = pairs * 2 * 2 * lanes * (5 * rows * context + 3 * rows * rows)
    return pl.pallas_call(
        attention_kernel,
        out_shape=(
            jax.ShapeDtypeStruct((rows, width), jnp.bfloat16),
            jax.ShapeDtypeStruct((context, width), jnp.float32),
            jax.ShapeDtypeStruct((context, width), jnp.float32),
        ),
        grid_spec=pltpu.PrefetchScalarGridSpec(
            num_scalar_prefetch=1,
            grid=(pairs,),
            in_specs=[row_spec, ctx_spec, ctx_spec, row_spec, row_spec, row_spec],
            out_specs=[row_spec, ctx_spec, ctx_spec],
        ),
        cost_estimate=pl.CostEstimate(
            flops=flops,
            transcendentals=width // HEAD_DIM * rows * (context + rows),
            bytes_accessed=width * (8 * rows + 4 * context + 8 * context),
        ),
    )(place, query, key_clean, value_clean, key_noisy, value_noisy, grad)


def chain_barrier(axes, left, right, has_left, has_right, stages=()):
    barrier = pltpu.get_barrier_semaphore()
    greeted = greet_groups(axes, stages, barrier)
    for peer, present in ((left, has_left), (right, has_right)):
        @pl.when(present)
        def _():
            pl.semaphore_signal(
                barrier, 1, device_id=device_of(axes, "seq", peer),
                device_id_type=pl.DeviceIdType.MESH,
            )
    pl.semaphore_wait(barrier, has_left.astype(jnp.int32) + has_right.astype(jnp.int32) + greeted)


def chain_ends(axes):
    me = lax.axis_index("seq")
    size = lax.axis_size("seq")
    left = jnp.maximum(me - 1, 0)
    right = jnp.minimum(me + 1, size - 1)
    return me, left, right, me > 0, me < size - 1


def project_plain(rows, weight_ref):
    high = rows.astype(jnp.bfloat16)
    low = (rows - high.astype(jnp.float32)).astype(jnp.bfloat16)
    product = jnp.dot(high, weight_ref[...], preferred_element_type=jnp.float32)
    return product + jnp.dot(low, weight_ref[...], preferred_element_type=jnp.float32)


def sum_back_kernel(axes, span, chunks, stages, dk_ref, dv_ref, wk_ref, wv_ref, raw_ref, total_ref,
                    sent, got, send_sems, recv_sems, slots, total_send, total_recv):
    me, left, right, has_left, has_right = chain_ends(axes)
    chain_barrier(axes, left, right, has_left, has_right, stages)
    squares = jnp.zeros((1, 1), jnp.float32)
    rows = raw_ref.shape[0]
    piece = rows // chunks

    @pl.when(jnp.logical_not(has_right))
    def _():
        got[...] = jnp.zeros(got.shape, got.dtype)

    def copy(step, chunk):
        return pltpu.make_async_remote_copy(
            src_ref=sent.at[step, chunk], dst_ref=got.at[step, chunk],
            send_sem=send_sems.at[step, chunk], recv_sem=recv_sems.at[step, chunk],
            device_id=device_of(axes, "seq", left), device_id_type=pl.DeviceIdType.MESH,
        )

    for step in range(span + 1):
        at = pl.ds(step * rows, rows)
        term = project_plain(dk_ref[at, :], wk_ref) + project_plain(dv_ref[at, :], wv_ref)
        for chunk in range(chunks):
            value = term[chunk * piece:(chunk + 1) * piece]
            if step > 0:
                @pl.when(has_right)
                def _():
                    copy(step - 1, chunk).wait_recv()

                value = value + got[step - 1, chunk].astype(jnp.float32)
            if step < span:
                sent[step, chunk] = value.astype(jnp.bfloat16)

                @pl.when(has_left)
                def _():
                    copy(step, chunk).start()
            else:
                raw_ref[pl.ds(chunk * piece, piece), :] = value
                squares = squares + jnp.sum(value * value, axis=(0, 1), keepdims=True)
    total_ref[...] = stage_total(
        axes, stages, jnp.broadcast_to(squares, total_ref.shape), slots, total_send, total_recv
    )
    for step in range(span):
        for chunk in range(chunks):
            @pl.when(has_left)
            def _():
                copy(step, chunk).wait_send()


def sum_back(dk, dv, w_key, w_value, span, rows, axes, chunks=8):
    width = dk.shape[1]
    piece = rows // chunks
    stages = group_stages(axes)
    widest = max(size for _, _, size in stages)
    vmem = pl.BlockSpec(memory_space=pltpu.VMEM)
    return pl.pallas_call(
        functools.partial(sum_back_kernel, axes, span, chunks, stages),
        out_shape=(
            jax.ShapeDtypeStruct((rows, width), jnp.float32),
            jax.ShapeDtypeStruct((8, 128), jnp.float32),
        ),
        in_specs=[vmem] * 4,
        out_specs=[vmem, vmem],
        scratch_shapes=[
            pltpu.VMEM((span, chunks, piece, width), jnp.bfloat16),
            pltpu.VMEM((span, chunks, piece, width), jnp.bfloat16),
            pltpu.SemaphoreType.DMA((span, chunks)),
            pltpu.SemaphoreType.DMA((span, chunks)),
            pltpu.VMEM((len(stages), widest, 8, 128), jnp.float32),
            pltpu.SemaphoreType.DMA((len(stages), widest)),
            pltpu.SemaphoreType.DMA((len(stages), widest)),
        ],
        cost_estimate=pl.CostEstimate(
            flops=8 * width * width * rows * (span + 1), transcendentals=0,
            bytes_accessed=4 * width * (2 * (span + 1) * rows + rows + width),
        ),
        compiler_params=pltpu.CompilerParams(collective_id=1, has_side_effects=True),
    )(dk, dv, w_key, w_value)


def gather_front_kernel(axes, span, chunks, own_ref, noisy_ref, wq_ref, wk_ref, wv_ref,
                        kc_ref, vc_ref, q_ref, kn_ref, vn_ref, got, send_sems, recv_sems):
    me, left, right, has_left, has_right = chain_ends(axes)
    chain_barrier(axes, left, right, has_left, has_right)
    rows = own_ref.shape[0]
    piece = rows // chunks
    for step in range(span):
        @pl.when(step >= me)
        def _():
            got[step] = jnp.zeros(got.shape[1:], got.dtype)

    def copy(step, chunk):
        if step == 0:
            source = own_ref.at[pl.ds(chunk * piece, piece)]
        else:
            source = got.at[step - 1, chunk]
        return pltpu.make_async_remote_copy(
            src_ref=source, dst_ref=got.at[step, chunk],
            send_sem=send_sems.at[step, chunk], recv_sem=recv_sems.at[step, chunk],
            device_id=device_of(axes, "seq", right), device_id_type=pl.DeviceIdType.MESH,
        )

    def project_rows(rows_in, weight_ref):
        return jnp.dot(rows_in, weight_ref[...], preferred_element_type=jnp.float32).astype(
            jnp.bfloat16
        )

    for chunk in range(chunks):
        @pl.when(has_right)
        def _():
            copy(0, chunk).start()
    noisy = noisy_ref[...]
    q_ref[...] = project_rows(noisy, wq_ref)
    kn_ref[...] = project_rows(noisy, wk_ref)
    vn_ref[...] = project_rows(noisy, wv_ref)
    own = own_ref[...]
    kc_ref[pl.ds(span * rows, rows), :] = project_rows(own, wk_ref)
    vc_ref[pl.ds(span * rows, rows), :] = project_rows(own, wv_ref)
    for step in range(1, span + 1):
        for chunk in range(chunks):
            @pl.when(step <= me)
            def _():
                copy(step - 1, chunk).wait_recv()
            if step < span:
                @pl.when(has_right & (step <= me))
                def _():
                    copy(step, chunk).start()
        arrived = got[step - 1].reshape(rows, -1)
        kc_ref[pl.ds((span - step) * rows, rows), :] = project_rows(arrived, wk_ref)
        vc_ref[pl.ds((span - step) * rows, rows), :] = project_rows(arrived, wv_ref)
    for step in range(span):
        for chunk in range(chunks):
            @pl.when(has_right & (step <= me))
            def _():
                copy(step, chunk).wait_send()


def gather_front(own, noisy, w_query, w_key, w_value, span, axes, chunks=8):
    rows, width = own.shape
    piece = rows // chunks
    vmem = pl.BlockSpec(memory_space=pltpu.VMEM)
    context = jax.ShapeDtypeStruct(((span + 1) * rows, width), jnp.bfloat16)
    local = jax.ShapeDtypeStruct((rows, width), jnp.bfloat16)
    flops = 2 * width * width * rows * (2 * (span + 1) + 3)
    return pl.pallas_call(
        functools.partial(gather_front_kernel, axes, span, chunks),
        out_shape=(context, context, local, local, local),
        in_specs=[vmem] * 5,
        out_specs=[vmem] * 5,
        scratch_shapes=[
            pltpu.VMEM((span, chunks, piece, width), own.dtype),
            pltpu.SemaphoreType.DMA((span, chunks)),
            pltpu.SemaphoreType.DMA((span, chunks)),
        ],
        cost_estimate=pl.CostEstimate(
            flops=flops, transcendentals=0,
            bytes_accessed=2 * width * (3 * width + (2 * span + 7) * rows),
        ),
        compiler_params=pltpu.CompilerParams(collective_id=2, has_side_effects=True),
    )(own, noisy, w_query, w_key, w_value)

def project(rows, weight):
    high = rows.astype(jnp.bfloat16)
    low = (rows - high.astype(jnp.float32)).astype(jnp.bfloat16)
    contract = (((1,), (1,)), ((), ()))
    product = lax.dot_general(high, weight, contract, preferred_element_type=jnp.float32)
    return product + lax.dot_general(low, weight, contract, preferred_element_type=jnp.float32)


def on_device(clean, out_cot, mask_bits, levels, importance, w_query, w_key, w_value, mask_embed):
    clean_rows = clean[0]
    cotangent = out_cot[0]
    tok_count = clean_rows.shape[0]
    width = clean_rows.shape[1]
    span = WINDOW // tok_count
    scale = 1.0 / math.sqrt(HEAD_DIM)
    position = lax.axis_index("seq") * tok_count
    within = jnp.arange(BLOCK, dtype=jnp.int32)
    block_bits = jnp.right_shift(mask_bits[0][:, None], within[None, :]) & 1
    bits = block_bits.reshape(tok_count)
    masked = bits == 1
    noisy = jnp.where(masked[:, None], mask_embed[None, :], clean_rows)
    key_clean, value_clean, query, key_noisy, value_noisy = gather_front(
        clean_rows, noisy, w_query, w_key, w_value, span, ("dp", "seq")
    )
    level_f = levels[0].astype(jnp.float32)
    ratio_f = importance[0].astype(jnp.float32)
    block_weight = LEVELS / level_f * (ratio_f[:, 0] / ratio_f[:, 1])
    token_weight = (block_weight[:, None] * block_bits.astype(jnp.float32)).reshape(tok_count)
    grad_out = (cotangent.astype(jnp.float32) * token_weight[:, None]).astype(jnp.bfloat16)
    place = jnp.reshape(span * tok_count - position, (1,)).astype(jnp.int32)
    attn_rows, dkey_rows, dvalue_rows = attention_heads(
        place, query, key_clean, value_clean, key_noisy, value_noisy, grad_out
    )
    raw, total = sum_back(dkey_rows, dvalue_rows, w_key.T, w_value.T, span, tok_count, ("dp", "seq"))
    total_squares = total[0, 0]
    entries = float(tok_count * width * lax.axis_size("dp") * lax.axis_size("seq"))
    rms = jnp.sqrt(total_squares / entries + EPS)
    factor = jnp.minimum(1.0, CLIP / rms)
    return (attn_rows[None], (raw * factor)[None])


def solution(mesh):
    in_specs = (
        P("dp", "seq", None),
        P("dp", "seq", None),
        P("dp", "seq"),
        P("dp", "seq"),
        P("dp", "seq", None),
        P(),
        P(),
        P(),
        P(),
    )
    out_specs = (P("dp", "seq", None), P("dp", "seq", None))
    return jax.shard_map(
        on_device, mesh=mesh, in_specs=in_specs, out_specs=out_specs, check_vma=False
    )
```

```python
import functools
import math

import jax
import jax.numpy as jnp
from jax import lax
from jax.sharding import PartitionSpec as P
from jax.experimental import pallas as pl
from jax.experimental.pallas import tpu as pltpu

HEADS = 12
HEAD_DIM = 64
BLOCK = 16
WINDOW = 1024
LEVELS = 16


EPS = 1e-06
CLIP = 0.25


def from_behind(block, axis, distance):
    devices = range(lax.axis_size(axis))
    route = [(i - distance, i) for i in devices if i - distance in devices]
    return lax.ppermute(block, axis, route)


def group_stages(axes):
    stages = []
    for axis in axes:
        rest, stride = lax.axis_size(axis), 1
        while rest > 1:
            size = max(g for g in range(1, 9) if rest % g == 0)
            stages.append((axis, stride, size))
            stride, rest = stride * size, rest // size
    return stages


def stage_peer(axis, stride, size, offset):
    index = lax.axis_index(axis)
    digit = (index // stride) % size
    return index + ((digit + offset) % size - digit) * stride


def device_of(axes, axis, peer):
    return tuple(peer if name == axis else lax.axis_index(name) for name in axes)


def greet_groups(axes, stages, barrier):
    count = 0
    for axis, stride, size in stages:
        for offset in range(1, size):
            peer = stage_peer(axis, stride, size, offset)
            pl.semaphore_signal(
                barrier, 1, device_id=device_of(axes, axis, peer),
                device_id_type=pl.DeviceIdType.MESH,
            )
            count += 1
    return count


def stage_total(axes, stages, current, slots, send_sems, recv_sems):
    for number, (axis, stride, size) in enumerate(stages):
        digit = (lax.axis_index(axis) // stride) % size
        slots[number, digit] = current
        copies = []
        for offset in range(1, size):
            peer = stage_peer(axis, stride, size, offset)
            copy = pltpu.make_async_remote_copy(
                src_ref=slots.at[number, digit],
                dst_ref=slots.at[number, digit],
                send_sem=send_sems.at[number, offset],
                recv_sem=recv_sems.at[number, offset],
                device_id=device_of(axes, axis, peer),
                device_id_type=pl.DeviceIdType.MESH,
            )
            copy.start()
            copies.append(copy)
        for copy in copies:
            copy.wait()
        current = slots[number, 0]
        for member in range(1, size):
            current = current + slots[number, member]
    return current


def total_kernel(axes, stages, part_ref, out_ref, slots, send_sems, recv_sems):
    barrier = pltpu.get_barrier_semaphore()
    pl.semaphore_wait(barrier, greet_groups(axes, stages, barrier))
    out_ref[...] = stage_total(axes, stages, part_ref[...], slots, send_sems, recv_sems)


def global_total(value, axes):
    stages = group_stages(axes)
    widest = max(size for _, _, size in stages)
    part = jnp.broadcast_to(value.astype(jnp.float32), (8, 128))
    summed = pl.pallas_call(
        functools.partial(total_kernel, axes, stages),
        out_shape=jax.ShapeDtypeStruct((8, 128), jnp.float32),
        in_specs=[pl.BlockSpec(memory_space=pltpu.VMEM)],
        out_specs=pl.BlockSpec(memory_space=pltpu.VMEM),
        scratch_shapes=[
            pltpu.VMEM((len(stages), widest, 8, 128), jnp.float32),
            pltpu.SemaphoreType.DMA((len(stages), widest)),
            pltpu.SemaphoreType.DMA((len(stages), widest)),
        ],
        compiler_params=pltpu.CompilerParams(collective_id=0, has_side_effects=True),
    )(part)
    return summed[0, 0]


def attention_kernel(place_ref, q_ref, kc_ref, vc_ref, kn_ref, vn_ref, g_ref,
                     out_ref, dk_ref, dv_ref):
    scale = 1.0 / math.sqrt(HEAD_DIM)
    query = q_ref[...]
    key_clean = kc_ref[...]
    value_clean = vc_ref[...]
    key_noisy = kn_ref[...]
    value_noisy = vn_ref[...]
    grad = g_ref[...]
    rows, lanes = query.shape
    context = key_clean.shape[0]
    row_block = lax.broadcasted_iota(jnp.int32, (rows, context), 0) // BLOCK * BLOCK
    col = lax.broadcasted_iota(jnp.int32, (rows, context), 1)
    allow_clean = (col >= row_block) & (col < row_block + WINDOW) & (col >= place_ref[0])
    own_row = lax.broadcasted_iota(jnp.int32, (rows, rows), 0) // BLOCK
    own_col = lax.broadcasted_iota(jnp.int32, (rows, rows), 1) // BLOCK
    allow_noisy = own_row == own_col
    lane = lax.broadcasted_iota(jnp.int32, (1, lanes), 1) // HEAD_DIM
    contract = (((1,), (1,)), ((), ()))
    lead = (((0,), (0,)), ((), ()))
    zero = jnp.zeros((), jnp.bfloat16)
    query_scaled = query * jnp.asarray(scale, jnp.bfloat16)
    grad_scaled = grad * jnp.asarray(scale, jnp.bfloat16)
    outs, dks, dvs = [], [], []
    for head in range(lanes // HEAD_DIM):
        mine = lane == head
        query_h = jnp.where(mine, query_scaled, zero)
        grad_h = jnp.where(mine, grad_scaled, zero)
        score_clean = lax.dot_general(query_h, key_clean, contract, preferred_element_type=jnp.float32)
        score_noisy = lax.dot_general(query_h, key_noisy, contract, preferred_element_type=jnp.float32)
        score_clean = jnp.where(allow_clean, score_clean, -jnp.inf)
        score_noisy = jnp.where(allow_noisy, score_noisy, -jnp.inf)
        peak = jnp.maximum(
            jnp.max(score_clean, axis=-1, keepdims=True), jnp.max(score_noisy, axis=-1, keepdims=True)
        )
        exp_clean = jnp.exp(score_clean - peak)
        exp_noisy = jnp.exp(score_noisy - peak)
        denom = jnp.sum(exp_clean, axis=-1, keepdims=True) + jnp.sum(exp_noisy, axis=-1, keepdims=True)
        inverse = 1.0 / denom
        prob_clean = exp_clean * inverse
        weight_clean = prob_clean.astype(jnp.bfloat16)
        weight_noisy = (exp_noisy * inverse).astype(jnp.bfloat16)
        mixed = jnp.dot(weight_clean, value_clean, preferred_element_type=jnp.float32)
        mixed = mixed + jnp.dot(weight_noisy, value_noisy, preferred_element_type=jnp.float32)
        out_h = mixed.astype(jnp.bfloat16)
        delta = jnp.sum(
            jnp.where(mine, grad_scaled.astype(jnp.float32) * out_h.astype(jnp.float32), 0.0),
            axis=-1, keepdims=True,
        )
        dprob = lax.dot_general(grad_h, value_clean, contract, preferred_element_type=jnp.float32)
        dscore = (prob_clean * (dprob - delta)).astype(jnp.bfloat16)
        outs.append(out_h)
        dks.append(lax.dot_general(dscore, query, lead, preferred_element_type=jnp.float32))
        dvs.append(lax.dot_general(weight_clean, grad, lead, preferred_element_type=jnp.float32))
    out, dk, dv = outs[0], dks[0], dvs[0]
    for head in range(1, len(outs)):
        mine = lane == head
        out = jnp.where(mine, outs[head], out)
        dk = jnp.where(mine, dks[head], dk)
        dv = jnp.where(mine, dvs[head], dv)
    out_ref[...] = out
    dk_ref[...] = dk
    dv_ref[...] = dv


def attention_heads(place, query, key_clean, value_clean, key_noisy, value_noisy, grad):
    rows, width = query.shape
    context = key_clean.shape[0]
    lanes = 2 * HEAD_DIM
    pairs = width // lanes
    row_spec = pl.BlockSpec((rows, lanes), lambda p, place: (0, p))
    ctx_spec = pl.BlockSpec((context, lanes), lambda p, place: (0, p))
    flops = pairs * 2 * 2 * lanes * (5 * rows * context + 3 * rows * rows)
    return pl.pallas_call(
        attention_kernel,
        out_shape=(
            jax.ShapeDtypeStruct((rows, width), jnp.bfloat16),
            jax.ShapeDtypeStruct((context, width), jnp.float32),
            jax.ShapeDtypeStruct((context, width), jnp.float32),
        ),
        grid_spec=pltpu.PrefetchScalarGridSpec(
            num_scalar_prefetch=1,
            grid=(pairs,),
            in_specs=[row_spec, ctx_spec, ctx_spec, row_spec, row_spec, row_spec],
            out_specs=[row_spec, ctx_spec, ctx_spec],
        ),
        cost_estimate=pl.CostEstimate(
            flops=flops,
            transcendentals=width // HEAD_DIM * rows * (context + rows),
            bytes_accessed=width * (8 * rows + 4 * context + 8 * context),
        ),
    )(place, query, key_clean, value_clean, key_noisy, value_noisy, grad)


def chain_barrier(axes, left, right, has_left, has_right, stages=()):
    barrier = pltpu.get_barrier_semaphore()
    greeted = greet_groups(axes, stages, barrier)
    for peer, present in ((left, has_left), (right, has_right)):
        @pl.when(present)
        def _():
            pl.semaphore_signal(
                barrier, 1, device_id=device_of(axes, "seq", peer),
                device_id_type=pl.DeviceIdType.MESH,
            )
    pl.semaphore_wait(barrier, has_left.astype(jnp.int32) + has_right.astype(jnp.int32) + greeted)


def chain_ends(axes):
    me = lax.axis_index("seq")
    size = lax.axis_size("seq")
    left = jnp.maximum(me - 1, 0)
    right = jnp.minimum(me + 1, size - 1)
    return me, left, right, me > 0, me < size - 1


def project_plain(rows, weight_ref):
    high = rows.astype(jnp.bfloat16)
    low = (rows - high.astype(jnp.float32)).astype(jnp.bfloat16)
    product = jnp.dot(high, weight_ref[...], preferred_element_type=jnp.float32)
    return product + jnp.dot(low, weight_ref[...], preferred_element_type=jnp.float32)


def sum_back_kernel(axes, span, chunks, stages, dk_ref, dv_ref, wk_ref, wv_ref, raw_ref, total_ref,
                    sent, got, send_sems, recv_sems, slots, total_send, total_recv):
    me, left, right, has_left, has_right = chain_ends(axes)
    chain_barrier(axes, left, right, has_left, has_right, stages)
    squares = jnp.zeros((1, 1), jnp.float32)
    rows = raw_ref.shape[0]
    piece = rows // chunks

    @pl.when(jnp.logical_not(has_right))
    def _():
        got[...] = jnp.zeros(got.shape, got.dtype)

    def copy(step, chunk):
        return pltpu.make_async_remote_copy(
            src_ref=sent.at[step, chunk], dst_ref=got.at[step, chunk],
            send_sem=send_sems.at[step, chunk], recv_sem=recv_sems.at[step, chunk],
            device_id=device_of(axes, "seq", left), device_id_type=pl.DeviceIdType.MESH,
        )

    for step in range(span + 1):
        at = pl.ds(step * rows, rows)
        term = project_plain(dk_ref[at, :], wk_ref) + project_plain(dv_ref[at, :], wv_ref)
        for chunk in range(chunks):
            value = term[chunk * piece:(chunk + 1) * piece]
            if step > 0:
                @pl.when(has_right)
                def _():
                    copy(step - 1, chunk).wait_recv()

                value = value + got[step - 1, chunk].astype(jnp.float32)
            if step < span:
                sent[step, chunk] = value.astype(jnp.bfloat16)

                @pl.when(has_left)
                def _():
                    copy(step, chunk).start()
            else:
                raw_ref[pl.ds(chunk * piece, piece), :] = value
                squares = squares + jnp.sum(value * value, axis=(0, 1), keepdims=True)
    total_ref[...] = stage_total(
        axes, stages, jnp.broadcast_to(squares, total_ref.shape), slots, total_send, total_recv
    )
    for step in range(span):
        for chunk in range(chunks):
            @pl.when(has_left)
            def _():
                copy(step, chunk).wait_send()


def sum_back(dk, dv, w_key, w_value, span, rows, axes, chunks=8):
    width = dk.shape[1]
    piece = rows // chunks
    stages = group_stages(axes)
    widest = max(size for _, _, size in stages)
    vmem = pl.BlockSpec(memory_space=pltpu.VMEM)
    return pl.pallas_call(
        functools.partial(sum_back_kernel, axes, span, chunks, stages),
        out_shape=(
            jax.ShapeDtypeStruct((rows, width), jnp.float32),
            jax.ShapeDtypeStruct((8, 128), jnp.float32),
        ),
        in_specs=[vmem] * 4,
        out_specs=[vmem, vmem],
        scratch_shapes=[
            pltpu.VMEM((span, chunks, piece, width), jnp.bfloat16),
            pltpu.VMEM((span, chunks, piece, width), jnp.bfloat16),
            pltpu.SemaphoreType.DMA((span, chunks)),
            pltpu.SemaphoreType.DMA((span, chunks)),
            pltpu.VMEM((len(stages), widest, 8, 128), jnp.float32),
            pltpu.SemaphoreType.DMA((len(stages), widest)),
            pltpu.SemaphoreType.DMA((len(stages), widest)),
        ],
        cost_estimate=pl.CostEstimate(
            flops=8 * width * width * rows * (span + 1), transcendentals=0,
            bytes_accessed=4 * width * (2 * (span + 1) * rows + rows + width),
        ),
        compiler_params=pltpu.CompilerParams(collective_id=1, has_side_effects=True),
    )(dk, dv, w_key, w_value)


def gather_front_kernel(axes, span, chunks, own_ref, noisy_ref, wq_ref, wk_ref, wv_ref,
                        kc_ref, vc_ref, q_ref, kn_ref, vn_ref, got, send_sems, recv_sems):
    me, left, right, has_left, has_right = chain_ends(axes)
    chain_barrier(axes, left, right, has_left, has_right)
    rows = own_ref.shape[0]
    piece = rows // chunks
    for step in range(span):
        @pl.when(step >= me)
        def _():
            got[step] = jnp.zeros(got.shape[1:], got.dtype)

    def copy(step, chunk):
        if step == 0:
            source = own_ref.at[pl.ds(chunk * piece, piece)]
        else:
            source = got.at[step - 1, chunk]
        return pltpu.make_async_remote_copy(
            src_ref=source, dst_ref=got.at[step, chunk],
            send_sem=send_sems.at[step, chunk], recv_sem=recv_sems.at[step, chunk],
            device_id=device_of(axes, "seq", right), device_id_type=pl.DeviceIdType.MESH,
        )

    def project_rows(rows_in, weight_ref):
        return jnp.dot(rows_in, weight_ref[...], preferred_element_type=jnp.float32).astype(
            jnp.bfloat16
        )

    for chunk in range(chunks):
        @pl.when(has_right)
        def _():
            copy(0, chunk).start()
    noisy = noisy_ref[...]
    q_ref[...] = project_rows(noisy, wq_ref)
    kn_ref[...] = project_rows(noisy, wk_ref)
    vn_ref[...] = project_rows(noisy, wv_ref)
    own = own_ref[...]
    kc_ref[pl.ds(span * rows, rows), :] = project_rows(own, wk_ref)
    vc_ref[pl.ds(span * rows, rows), :] = project_rows(own, wv_ref)
    for step in range(1, span + 1):
        for chunk in range(chunks):
            @pl.when(step <= me)
            def _():
                copy(step - 1, chunk).wait_recv()
            if step < span:
                @pl.when(has_right & (step <= me))
                def _():
                    copy(step, chunk).start()
        arrived = got[step - 1].reshape(rows, -1)
        kc_ref[pl.ds((span - step) * rows, rows), :] = project_rows(arrived, wk_ref)
        vc_ref[pl.ds((span - step) * rows, rows), :] = project_rows(arrived, wv_ref)
    for step in range(span):
        for chunk in range(chunks):
            @pl.when(has_right & (step <= me))
            def _():
                copy(step, chunk).wait_send()


def gather_front(own, noisy, w_query, w_key, w_value, span, axes, chunks=8):
    rows, width = own.shape
    piece = rows // chunks
    vmem = pl.BlockSpec(memory_space=pltpu.VMEM)
    context = jax.ShapeDtypeStruct(((span + 1) * rows, width), jnp.bfloat16)
    local = jax.ShapeDtypeStruct((rows, width), jnp.bfloat16)
    flops = 2 * width * width * rows * (2 * (span + 1) + 3)
    return pl.pallas_call(
        functools.partial(gather_front_kernel, axes, span, chunks),
        out_shape=(context, context, local, local, local),
        in_specs=[vmem] * 5,
        out_specs=[vmem] * 5,
        scratch_shapes=[
            pltpu.VMEM((span, chunks, piece, width), own.dtype),
            pltpu.SemaphoreType.DMA((span, chunks)),
            pltpu.SemaphoreType.DMA((span, chunks)),
        ],
        cost_estimate=pl.CostEstimate(
            flops=flops, transcendentals=0,
            bytes_accessed=2 * width * (3 * width + (2 * span + 7) * rows),
        ),
        compiler_params=pltpu.CompilerParams(collective_id=2, has_side_effects=True),
    )(own, noisy, w_query, w_key, w_value)

def project(rows, weight):
    high = rows.astype(jnp.bfloat16)
    low = (rows - high.astype(jnp.float32)).astype(jnp.bfloat16)
    contract = (((1,), (1,)), ((), ()))
    product = lax.dot_general(high, weight, contract, preferred_element_type=jnp.float32)
    return product + lax.dot_general(low, weight, contract, preferred_element_type=jnp.float32)


def on_device(clean, out_cot, mask_bits, levels, importance, w_query, w_key, w_value, mask_embed):
    clean_rows = clean[0]
    cotangent = out_cot[0]
    tok_count = clean_rows.shape[0]
    width = clean_rows.shape[1]
    span = WINDOW // tok_count
    scale = 1.0 / math.sqrt(HEAD_DIM)
    position = lax.axis_index("seq") * tok_count
    within = jnp.arange(BLOCK, dtype=jnp.int32)
    block_bits = jnp.right_shift(mask_bits[0][:, None], within[None, :]) & 1
    bits = block_bits.reshape(tok_count)
    masked = bits == 1
    noisy = jnp.where(masked[:, None], mask_embed[None, :], clean_rows)
    key_clean, value_clean, query, key_noisy, value_noisy = gather_front(
        clean_rows, noisy, w_query, w_key, w_value, span, ("dp", "seq")
    )
    level_f = levels[0].astype(jnp.float32)
    ratio_f = importance[0].astype(jnp.float32)
    block_weight = LEVELS / level_f * (ratio_f[:, 0] / ratio_f[:, 1])
    token_weight = (block_weight[:, None] * block_bits.astype(jnp.float32)).reshape(tok_count)
    grad_out = (cotangent.astype(jnp.float32) * token_weight[:, None]).astype(jnp.bfloat16)
    place = jnp.reshape(span * tok_count - position, (1,)).astype(jnp.int32)
    attn_rows, dkey_rows, dvalue_rows = attention_heads(
        place, query, key_clean, value_clean, key_noisy, value_noisy, grad_out
    )
    raw, total = sum_back(dkey_rows, dvalue_rows, w_key.T, w_value.T, span, tok_count, ("dp", "seq"))
    total_squares = total[0, 0]
    entries = float(tok_count * width * lax.axis_size("dp") * lax.axis_size("seq"))
    rms = jnp.sqrt(total_squares / entries + EPS)
    factor = jnp.minimum(1.0, CLIP / rms)
    return (attn_rows[None], (raw * factor)[None])


def solution(mesh):
    in_specs = (
        P("dp", "seq", None),
        P("dp", "seq", None),
        P("dp", "seq"),
        P("dp", "seq"),
        P("dp", "seq", None),
        P(),
        P(),
        P(),
        P(),
    )
    out_specs = (P("dp", "seq", None), P("dp", "seq", None))
    return jax.shard_map(
        on_device, mesh=mesh, in_specs=in_specs, out_specs=out_specs, check_vma=False
    )
```

```python
import functools
import math

import jax
import jax.numpy as jnp
from jax import lax
from jax.sharding import PartitionSpec as P
from jax.experimental import pallas as pl
from jax.experimental.pallas import tpu as pltpu

HEADS = 12
HEAD_DIM = 64
BLOCK = 16
WINDOW = 1024
LEVELS = 16


EPS = 1e-06
CLIP = 0.25


def from_behind(block, axis, distance):
    devices = range(lax.axis_size(axis))
    route = [(i - distance, i) for i in devices if i - distance in devices]
    return lax.ppermute(block, axis, route)


def group_stages(axes):
    stages = []
    for axis in axes:
        rest, stride = lax.axis_size(axis), 1
        while rest > 1:
            size = max(g for g in range(1, 9) if rest % g == 0)
            stages.append((axis, stride, size))
            stride, rest = stride * size, rest // size
    return stages


def stage_peer(axis, stride, size, offset):
    index = lax.axis_index(axis)
    digit = (index // stride) % size
    return index + ((digit + offset) % size - digit) * stride


def device_of(axes, axis, peer):
    return tuple(peer if name == axis else lax.axis_index(name) for name in axes)


def greet_groups(axes, stages, barrier):
    count = 0
    for axis, stride, size in stages:
        for offset in range(1, size):
            peer = stage_peer(axis, stride, size, offset)
            pl.semaphore_signal(
                barrier, 1, device_id=device_of(axes, axis, peer),
                device_id_type=pl.DeviceIdType.MESH,
            )
            count += 1
    return count


def stage_total(axes, stages, current, slots, send_sems, recv_sems):
    for number, (axis, stride, size) in enumerate(stages):
        digit = (lax.axis_index(axis) // stride) % size
        slots[number, digit] = current
        copies = []
        for offset in range(1, size):
            peer = stage_peer(axis, stride, size, offset)
            copy = pltpu.make_async_remote_copy(
                src_ref=slots.at[number, digit],
                dst_ref=slots.at[number, digit],
                send_sem=send_sems.at[number, offset],
                recv_sem=recv_sems.at[number, offset],
                device_id=device_of(axes, axis, peer),
                device_id_type=pl.DeviceIdType.MESH,
            )
            copy.start()
            copies.append(copy)
        for copy in copies:
            copy.wait()
        current = slots[number, 0]
        for member in range(1, size):
            current = current + slots[number, member]
    return current


def total_kernel(axes, stages, part_ref, out_ref, slots, send_sems, recv_sems):
    barrier = pltpu.get_barrier_semaphore()
    pl.semaphore_wait(barrier, greet_groups(axes, stages, barrier))
    out_ref[...] = stage_total(axes, stages, part_ref[...], slots, send_sems, recv_sems)


def global_total(value, axes):
    stages = group_stages(axes)
    widest = max(size for _, _, size in stages)
    part = jnp.broadcast_to(value.astype(jnp.float32), (8, 128))
    summed = pl.pallas_call(
        functools.partial(total_kernel, axes, stages),
        out_shape=jax.ShapeDtypeStruct((8, 128), jnp.float32),
        in_specs=[pl.BlockSpec(memory_space=pltpu.VMEM)],
        out_specs=pl.BlockSpec(memory_space=pltpu.VMEM),
        scratch_shapes=[
            pltpu.VMEM((len(stages), widest, 8, 128), jnp.float32),
            pltpu.SemaphoreType.DMA((len(stages), widest)),
            pltpu.SemaphoreType.DMA((len(stages), widest)),
        ],
        compiler_params=pltpu.CompilerParams(collective_id=0, has_side_effects=True),
    )(part)
    return summed[0, 0]


def attention_kernel(place_ref, q_ref, kc_ref, vc_ref, kn_ref, vn_ref, g_ref,
                     out_ref, dk_ref, dv_ref, clean_bias, noisy_bias):
    scale = 1.0 / math.sqrt(HEAD_DIM)
    query = q_ref[...]
    key_clean = kc_ref[...]
    value_clean = vc_ref[...]
    key_noisy = kn_ref[...]
    value_noisy = vn_ref[...]
    grad = g_ref[...]
    rows, lanes = query.shape
    context = key_clean.shape[0]

    @pl.when(pl.program_id(0) == 0)
    def _():
        row_block = lax.broadcasted_iota(jnp.int32, (rows, context), 0) // BLOCK * BLOCK
        col = lax.broadcasted_iota(jnp.int32, (rows, context), 1)
        allow_clean = (col >= row_block) & (col < row_block + WINDOW) & (col >= place_ref[0])
        own_row = lax.broadcasted_iota(jnp.int32, (rows, rows), 0) // BLOCK
        own_col = lax.broadcasted_iota(jnp.int32, (rows, rows), 1) // BLOCK
        clean_bias[...] = jnp.where(allow_clean, 0.0, -jnp.inf)
        noisy_bias[...] = jnp.where(own_row == own_col, 0.0, -jnp.inf)

    lane = lax.broadcasted_iota(jnp.int32, (1, lanes), 1) // HEAD_DIM
    contract = (((1,), (1,)), ((), ()))
    lead = (((0,), (0,)), ((), ()))
    zero = jnp.zeros((), jnp.bfloat16)
    query_scaled = query * jnp.asarray(scale, jnp.bfloat16)
    grad_scaled = grad * jnp.asarray(scale, jnp.bfloat16)
    outs, dks, dvs = [], [], []
    for head in range(lanes // HEAD_DIM):
        mine = lane == head
        query_h = jnp.where(mine, query_scaled, zero)
        grad_h = jnp.where(mine, grad_scaled, zero)
        score_clean = lax.dot_general(query_h, key_clean, contract, preferred_element_type=jnp.float32)
        score_noisy = lax.dot_general(query_h, key_noisy, contract, preferred_element_type=jnp.float32)
        score_clean = score_clean + clean_bias[...]
        score_noisy = score_noisy + noisy_bias[...]
        peak = jnp.maximum(
            jnp.max(score_clean, axis=-1, keepdims=True), jnp.max(score_noisy, axis=-1, keepdims=True)
        )
        exp_clean = jnp.exp(score_clean - peak)
        exp_noisy = jnp.exp(score_noisy - peak)
        denom = jnp.sum(exp_clean, axis=-1, keepdims=True) + jnp.sum(exp_noisy, axis=-1, keepdims=True)
        inverse = 1.0 / denom
        prob_clean = exp_clean * inverse
        weight_clean = prob_clean.astype(jnp.bfloat16)
        weight_noisy = (exp_noisy * inverse).astype(jnp.bfloat16)
        mixed = jnp.dot(weight_clean, value_clean, preferred_element_type=jnp.float32)
        mixed = mixed + jnp.dot(weight_noisy, value_noisy, preferred_element_type=jnp.float32)
        out_h = mixed.astype(jnp.bfloat16)
        delta = jnp.sum(
            jnp.where(mine, grad_scaled.astype(jnp.float32) * out_h.astype(jnp.float32), 0.0),
            axis=-1, keepdims=True,
        )
        dprob = lax.dot_general(grad_h, value_clean, contract, preferred_element_type=jnp.float32)
        dscore = (prob_clean * (dprob - delta)).astype(jnp.bfloat16)
        outs.append(out_h)
        dks.append(lax.dot_general(dscore, query, lead, preferred_element_type=jnp.float32))
        dvs.append(lax.dot_general(weight_clean, grad, lead, preferred_element_type=jnp.float32))
    out, dk, dv = outs[0], dks[0], dvs[0]
    for head in range(1, len(outs)):
        mine = lane == head
        out = jnp.where(mine, outs[head], out)
        dk = jnp.where(mine, dks[head], dk)
        dv = jnp.where(mine, dvs[head], dv)
    out_ref[...] = out
    dk_ref[...] = dk
    dv_ref[...] = dv


def attention_heads(place, query, key_clean, value_clean, key_noisy, value_noisy, grad):
    rows, width = query.shape
    context = key_clean.shape[0]
    lanes = 2 * HEAD_DIM
    pairs = width // lanes
    row_spec = pl.BlockSpec((rows, lanes), lambda p, place: (0, p))
    ctx_spec = pl.BlockSpec((context, lanes), lambda p, place: (0, p))
    flops = pairs * 2 * 2 * lanes * (5 * rows * context + 3 * rows * rows)
    return pl.pallas_call(
        attention_kernel,
        out_shape=(
            jax.ShapeDtypeStruct((rows, width), jnp.bfloat16),
            jax.ShapeDtypeStruct((context, width), jnp.float32),
            jax.ShapeDtypeStruct((context, width), jnp.float32),
        ),
        grid_spec=pltpu.PrefetchScalarGridSpec(
            num_scalar_prefetch=1,
            grid=(pairs,),
            in_specs=[row_spec, ctx_spec, ctx_spec, row_spec, row_spec, row_spec],
            out_specs=[row_spec, ctx_spec, ctx_spec],
            scratch_shapes=[
                pltpu.VMEM((rows, context), jnp.float32),
                pltpu.VMEM((rows, rows), jnp.float32),
            ],
        ),
        cost_estimate=pl.CostEstimate(
            flops=flops,
            transcendentals=width // HEAD_DIM * rows * (context + rows),
            bytes_accessed=width * (8 * rows + 4 * context + 8 * context),
        ),
    )(place, query, key_clean, value_clean, key_noisy, value_noisy, grad)


def chain_barrier(axes, left, right, has_left, has_right, stages=()):
    barrier = pltpu.get_barrier_semaphore()
    greeted = greet_groups(axes, stages, barrier)
    for peer, present in ((left, has_left), (right, has_right)):
        @pl.when(present)
        def _():
            pl.semaphore_signal(
                barrier, 1, device_id=device_of(axes, "seq", peer),
                device_id_type=pl.DeviceIdType.MESH,
            )
    pl.semaphore_wait(barrier, has_left.astype(jnp.int32) + has_right.astype(jnp.int32) + greeted)


def chain_ends(axes):
    me = lax.axis_index("seq")
    size = lax.axis_size("seq")
    left = jnp.maximum(me - 1, 0)
    right = jnp.minimum(me + 1, size - 1)
    return me, left, right, me > 0, me < size - 1


def project_plain(rows, weight_ref):
    high = rows.astype(jnp.bfloat16)
    low = (rows - high.astype(jnp.float32)).astype(jnp.bfloat16)
    product = jnp.dot(high, weight_ref[...], preferred_element_type=jnp.float32)
    return product + jnp.dot(low, weight_ref[...], preferred_element_type=jnp.float32)


def sum_back_kernel(axes, span, chunks, stages, dk_ref, dv_ref, wk_ref, wv_ref, raw_ref, total_ref,
                    sent, got, send_sems, recv_sems, slots, total_send, total_recv):
    me, left, right, has_left, has_right = chain_ends(axes)
    chain_barrier(axes, left, right, has_left, has_right, stages)
    squares = jnp.zeros((1, 1), jnp.float32)
    rows = raw_ref.shape[0]
    piece = rows // chunks

    @pl.when(jnp.logical_not(has_right))
    def _():
        got[...] = jnp.zeros(got.shape, got.dtype)

    def copy(step, chunk):
        return pltpu.make_async_remote_copy(
            src_ref=sent.at[step, chunk], dst_ref=got.at[step, chunk],
            send_sem=send_sems.at[step, chunk], recv_sem=recv_sems.at[step, chunk],
            device_id=device_of(axes, "seq", left), device_id_type=pl.DeviceIdType.MESH,
        )

    for step in range(span + 1):
        at = pl.ds(step * rows, rows)
        term = project_plain(dk_ref[at, :], wk_ref) + project_plain(dv_ref[at, :], wv_ref)
        for chunk in range(chunks):
            value = term[chunk * piece:(chunk + 1) * piece]
            if step > 0:
                @pl.when(has_right)
                def _():
                    copy(step - 1, chunk).wait_recv()

                value = value + got[step - 1, chunk].astype(jnp.float32)
            if step < span:
                sent[step, chunk] = value.astype(jnp.bfloat16)

                @pl.when(has_left)
                def _():
                    copy(step, chunk).start()
            else:
                raw_ref[pl.ds(chunk * piece, piece), :] = value
                squares = squares + jnp.sum(value * value, axis=(0, 1), keepdims=True)
    total_ref[...] = stage_total(
        axes, stages, jnp.broadcast_to(squares, total_ref.shape), slots, total_send, total_recv
    )
    for step in range(span):
        for chunk in range(chunks):
            @pl.when(has_left)
            def _():
                copy(step, chunk).wait_send()


def sum_back(dk, dv, w_key, w_value, span, rows, axes, chunks=8):
    width = dk.shape[1]
    piece = rows // chunks
    stages = group_stages(axes)
    widest = max(size for _, _, size in stages)
    vmem = pl.BlockSpec(memory_space=pltpu.VMEM)
    return pl.pallas_call(
        functools.partial(sum_back_kernel, axes, span, chunks, stages),
        out_shape=(
            jax.ShapeDtypeStruct((rows, width), jnp.float32),
            jax.ShapeDtypeStruct((8, 128), jnp.float32),
        ),
        in_specs=[vmem] * 4,
        out_specs=[vmem, vmem],
        scratch_shapes=[
            pltpu.VMEM((span, chunks, piece, width), jnp.bfloat16),
            pltpu.VMEM((span, chunks, piece, width), jnp.bfloat16),
            pltpu.SemaphoreType.DMA((span, chunks)),
            pltpu.SemaphoreType.DMA((span, chunks)),
            pltpu.VMEM((len(stages), widest, 8, 128), jnp.float32),
            pltpu.SemaphoreType.DMA((len(stages), widest)),
            pltpu.SemaphoreType.DMA((len(stages), widest)),
        ],
        cost_estimate=pl.CostEstimate(
            flops=8 * width * width * rows * (span + 1), transcendentals=0,
            bytes_accessed=4 * width * (2 * (span + 1) * rows + rows + width),
        ),
        compiler_params=pltpu.CompilerParams(collective_id=1, has_side_effects=True),
    )(dk, dv, w_key, w_value)


def gather_front_kernel(axes, span, chunks, own_ref, noisy_ref, wq_ref, wk_ref, wv_ref,
                        kc_ref, vc_ref, q_ref, kn_ref, vn_ref, got, send_sems, recv_sems):
    me, left, right, has_left, has_right = chain_ends(axes)
    chain_barrier(axes, left, right, has_left, has_right)
    rows = own_ref.shape[0]
    piece = rows // chunks
    for step in range(span):
        @pl.when(step >= me)
        def _():
            got[step] = jnp.zeros(got.shape[1:], got.dtype)

    def copy(step, chunk):
        if step == 0:
            source = own_ref.at[pl.ds(chunk * piece, piece)]
        else:
            source = got.at[step - 1, chunk]
        return pltpu.make_async_remote_copy(
            src_ref=source, dst_ref=got.at[step, chunk],
            send_sem=send_sems.at[step, chunk], recv_sem=recv_sems.at[step, chunk],
            device_id=device_of(axes, "seq", right), device_id_type=pl.DeviceIdType.MESH,
        )

    def project_rows(rows_in, weight_ref):
        return jnp.dot(rows_in, weight_ref[...], preferred_element_type=jnp.float32).astype(
            jnp.bfloat16
        )

    for chunk in range(chunks):
        @pl.when(has_right)
        def _():
            copy(0, chunk).start()
    noisy = noisy_ref[...]
    q_ref[...] = project_rows(noisy, wq_ref)
    kn_ref[...] = project_rows(noisy, wk_ref)
    vn_ref[...] = project_rows(noisy, wv_ref)
    own = own_ref[...]
    kc_ref[pl.ds(span * rows, rows), :] = project_rows(own, wk_ref)
    vc_ref[pl.ds(span * rows, rows), :] = project_rows(own, wv_ref)
    for step in range(1, span + 1):
        for chunk in range(chunks):
            @pl.when(step <= me)
            def _():
                copy(step - 1, chunk).wait_recv()
            if step < span:
                @pl.when(has_right & (step <= me))
                def _():
                    copy(step, chunk).start()
        arrived = got[step - 1].reshape(rows, -1)
        kc_ref[pl.ds((span - step) * rows, rows), :] = project_rows(arrived, wk_ref)
        vc_ref[pl.ds((span - step) * rows, rows), :] = project_rows(arrived, wv_ref)
    for step in range(span):
        for chunk in range(chunks):
            @pl.when(has_right & (step <= me))
            def _():
                copy(step, chunk).wait_send()


def gather_front(own, noisy, w_query, w_key, w_value, span, axes, chunks=8):
    rows, width = own.shape
    piece = rows // chunks
    vmem = pl.BlockSpec(memory_space=pltpu.VMEM)
    context = jax.ShapeDtypeStruct(((span + 1) * rows, width), jnp.bfloat16)
    local = jax.ShapeDtypeStruct((rows, width), jnp.bfloat16)
    flops = 2 * width * width * rows * (2 * (span + 1) + 3)
    return pl.pallas_call(
        functools.partial(gather_front_kernel, axes, span, chunks),
        out_shape=(context, context, local, local, local),
        in_specs=[vmem] * 5,
        out_specs=[vmem] * 5,
        scratch_shapes=[
            pltpu.VMEM((span, chunks, piece, width), own.dtype),
            pltpu.SemaphoreType.DMA((span, chunks)),
            pltpu.SemaphoreType.DMA((span, chunks)),
        ],
        cost_estimate=pl.CostEstimate(
            flops=flops, transcendentals=0,
            bytes_accessed=2 * width * (3 * width + (2 * span + 7) * rows),
        ),
        compiler_params=pltpu.CompilerParams(collective_id=2, has_side_effects=True),
    )(own, noisy, w_query, w_key, w_value)

def project(rows, weight):
    high = rows.astype(jnp.bfloat16)
    low = (rows - high.astype(jnp.float32)).astype(jnp.bfloat16)
    contract = (((1,), (1,)), ((), ()))
    product = lax.dot_general(high, weight, contract, preferred_element_type=jnp.float32)
    return product + lax.dot_general(low, weight, contract, preferred_element_type=jnp.float32)


def on_device(clean, out_cot, mask_bits, levels, importance, w_query, w_key, w_value, mask_embed):
    clean_rows = clean[0]
    cotangent = out_cot[0]
    tok_count = clean_rows.shape[0]
    width = clean_rows.shape[1]
    span = WINDOW // tok_count
    scale = 1.0 / math.sqrt(HEAD_DIM)
    position = lax.axis_index("seq") * tok_count
    within = jnp.arange(BLOCK, dtype=jnp.int32)
    block_bits = jnp.right_shift(mask_bits[0][:, None], within[None, :]) & 1
    bits = block_bits.reshape(tok_count)
    masked = bits == 1
    noisy = jnp.where(masked[:, None], mask_embed[None, :], clean_rows)
    key_clean, value_clean, query, key_noisy, value_noisy = gather_front(
        clean_rows, noisy, w_query, w_key, w_value, span, ("dp", "seq")
    )
    level_f = levels[0].astype(jnp.float32)
    ratio_f = importance[0].astype(jnp.float32)
    block_weight = LEVELS / level_f * (ratio_f[:, 0] / ratio_f[:, 1])
    token_weight = (block_weight[:, None] * block_bits.astype(jnp.float32)).reshape(tok_count)
    grad_out = (cotangent.astype(jnp.float32) * token_weight[:, None]).astype(jnp.bfloat16)
    place = jnp.reshape(span * tok_count - position, (1,)).astype(jnp.int32)
    attn_rows, dkey_rows, dvalue_rows = attention_heads(
        place, query, key_clean, value_clean, key_noisy, value_noisy, grad_out
    )
    raw, total = sum_back(dkey_rows, dvalue_rows, w_key.T, w_value.T, span, tok_count, ("dp", "seq"))
    total_squares = total[0, 0]
    entries = float(tok_count * width * lax.axis_size("dp") * lax.axis_size("seq"))
    rms = jnp.sqrt(total_squares / entries + EPS)
    factor = jnp.minimum(1.0, CLIP / rms)
    return (attn_rows[None], (raw * factor)[None])


def solution(mesh):
    in_specs = (
        P("dp", "seq", None),
        P("dp", "seq", None),
        P("dp", "seq"),
        P("dp", "seq"),
        P("dp", "seq", None),
        P(),
        P(),
        P(),
        P(),
    )
    out_specs = (P("dp", "seq", None), P("dp", "seq", None))
    return jax.shard_map(
        on_device, mesh=mesh, in_specs=in_specs, out_specs=out_specs, check_vma=False
    )
```

```python
import functools
import math

import jax
import jax.numpy as jnp
from jax import lax
from jax.sharding import PartitionSpec as P
from jax.experimental import pallas as pl
from jax.experimental.pallas import tpu as pltpu

HEADS = 12
HEAD_DIM = 64
BLOCK = 16
WINDOW = 1024
LEVELS = 16


EPS = 1e-06
CLIP = 0.25


def from_behind(block, axis, distance):
    devices = range(lax.axis_size(axis))
    route = [(i - distance, i) for i in devices if i - distance in devices]
    return lax.ppermute(block, axis, route)


def group_stages(axes):
    stages = []
    for axis in axes:
        rest, stride = lax.axis_size(axis), 1
        while rest > 1:
            size = max(g for g in range(1, 9) if rest % g == 0)
            stages.append((axis, stride, size))
            stride, rest = stride * size, rest // size
    return stages


def stage_peer(axis, stride, size, offset):
    index = lax.axis_index(axis)
    digit = (index // stride) % size
    return index + ((digit + offset) % size - digit) * stride


def device_of(axes, axis, peer):
    return tuple(peer if name == axis else lax.axis_index(name) for name in axes)


def greet_groups(axes, stages, barrier):
    count = 0
    for axis, stride, size in stages:
        for offset in range(1, size):
            peer = stage_peer(axis, stride, size, offset)
            pl.semaphore_signal(
                barrier, 1, device_id=device_of(axes, axis, peer),
                device_id_type=pl.DeviceIdType.MESH,
            )
            count += 1
    return count


def stage_total(axes, stages, current, slots, send_sems, recv_sems):
    for number, (axis, stride, size) in enumerate(stages):
        digit = (lax.axis_index(axis) // stride) % size
        slots[number, digit] = current
        copies = []
        for offset in range(1, size):
            peer = stage_peer(axis, stride, size, offset)
            copy = pltpu.make_async_remote_copy(
                src_ref=slots.at[number, digit],
                dst_ref=slots.at[number, digit],
                send_sem=send_sems.at[number, offset],
                recv_sem=recv_sems.at[number, offset],
                device_id=device_of(axes, axis, peer),
                device_id_type=pl.DeviceIdType.MESH,
            )
            copy.start()
            copies.append(copy)
        for copy in copies:
            copy.wait()
        current = slots[number, 0]
        for member in range(1, size):
            current = current + slots[number, member]
    return current


def total_kernel(axes, stages, part_ref, out_ref, slots, send_sems, recv_sems):
    barrier = pltpu.get_barrier_semaphore()
    pl.semaphore_wait(barrier, greet_groups(axes, stages, barrier))
    out_ref[...] = stage_total(axes, stages, part_ref[...], slots, send_sems, recv_sems)


def global_total(value, axes):
    stages = group_stages(axes)
    widest = max(size for _, _, size in stages)
    part = jnp.broadcast_to(value.astype(jnp.float32), (8, 128))
    summed = pl.pallas_call(
        functools.partial(total_kernel, axes, stages),
        out_shape=jax.ShapeDtypeStruct((8, 128), jnp.float32),
        in_specs=[pl.BlockSpec(memory_space=pltpu.VMEM)],
        out_specs=pl.BlockSpec(memory_space=pltpu.VMEM),
        scratch_shapes=[
            pltpu.VMEM((len(stages), widest, 8, 128), jnp.float32),
            pltpu.SemaphoreType.DMA((len(stages), widest)),
            pltpu.SemaphoreType.DMA((len(stages), widest)),
        ],
        compiler_params=pltpu.CompilerParams(collective_id=0, has_side_effects=True),
    )(part)
    return summed[0, 0]


def attention_kernel(place_ref, q_ref, kc_ref, vc_ref, kn_ref, vn_ref, g_ref,
                     out_ref, dk_ref, dv_ref, clean_bias, noisy_bias):
    scale = 1.0 / math.sqrt(HEAD_DIM)
    query = q_ref[...]
    key_clean = kc_ref[...]
    value_clean = vc_ref[...]
    key_noisy = kn_ref[...]
    value_noisy = vn_ref[...]
    grad = g_ref[...]
    rows, lanes = query.shape
    context = key_clean.shape[0]

    @pl.when(pl.program_id(0) == 0)
    def _():
        row_block = lax.broadcasted_iota(jnp.int32, (rows, context), 0) // BLOCK * BLOCK
        col = lax.broadcasted_iota(jnp.int32, (rows, context), 1)
        allow_clean = (col >= row_block) & (col < row_block + WINDOW) & (col >= place_ref[0])
        own_row = lax.broadcasted_iota(jnp.int32, (rows, rows), 0) // BLOCK
        own_col = lax.broadcasted_iota(jnp.int32, (rows, rows), 1) // BLOCK
        clean_bias[...] = jnp.where(allow_clean, 0.0, -jnp.inf)
        noisy_bias[...] = jnp.where(own_row == own_col, 0.0, -jnp.inf)

    lane = lax.broadcasted_iota(jnp.int32, (1, lanes), 1) // HEAD_DIM
    contract = (((1,), (1,)), ((), ()))
    lead = (((0,), (0,)), ((), ()))
    zero = jnp.zeros((), jnp.bfloat16)
    query_scaled = query * jnp.asarray(scale, jnp.bfloat16)
    grad_scaled = grad * jnp.asarray(scale, jnp.bfloat16)
    outs, dks, dvs = [], [], []
    for head in range(lanes // HEAD_DIM):
        mine = lane == head
        query_h = jnp.where(mine, query_scaled, zero)
        grad_h = jnp.where(mine, grad_scaled, zero)
        score_clean = lax.dot_general(query_h, key_clean, contract, preferred_element_type=jnp.float32)
        score_noisy = lax.dot_general(query_h, key_noisy, contract, preferred_element_type=jnp.float32)
        score_clean = score_clean + clean_bias[...]
        score_noisy = score_noisy + noisy_bias[...]
        peak = jnp.maximum(
            jnp.max(score_clean, axis=-1, keepdims=True), jnp.max(score_noisy, axis=-1, keepdims=True)
        )
        exp_clean = jnp.exp(score_clean - peak)
        exp_noisy = jnp.exp(score_noisy - peak)
        denom = jnp.sum(exp_clean, axis=-1, keepdims=True) + jnp.sum(exp_noisy, axis=-1, keepdims=True)
        inverse = 1.0 / denom
        prob_clean = exp_clean * inverse
        weight_clean = prob_clean.astype(jnp.bfloat16)
        weight_noisy = (exp_noisy * inverse).astype(jnp.bfloat16)
        mixed = jnp.dot(weight_clean, value_clean, preferred_element_type=jnp.float32)
        mixed = mixed + jnp.dot(weight_noisy, value_noisy, preferred_element_type=jnp.float32)
        out_h = mixed.astype(jnp.bfloat16)
        delta = jnp.sum(
            jnp.where(mine, grad_scaled.astype(jnp.float32) * out_h.astype(jnp.float32), 0.0),
            axis=-1, keepdims=True,
        )
        dprob = lax.dot_general(grad_h, value_clean, contract, preferred_element_type=jnp.float32)
        dscore = (prob_clean * (dprob - delta)).astype(jnp.bfloat16)
        outs.append(out_h)
        dks.append(lax.dot_general(dscore, query, lead, preferred_element_type=jnp.float32))
        dvs.append(lax.dot_general(weight_clean, grad, lead, preferred_element_type=jnp.float32))
    out, dk, dv = outs[0], dks[0], dvs[0]
    for head in range(1, len(outs)):
        mine = lane == head
        out = jnp.where(mine, outs[head], out)
        dk = jnp.where(mine, dks[head], dk)
        dv = jnp.where(mine, dvs[head], dv)
    out_ref[...] = out
    dk_ref[...] = dk
    dv_ref[...] = dv


def attention_heads(place, query, key_clean, value_clean, key_noisy, value_noisy, grad):
    rows, width = query.shape
    context = key_clean.shape[0]
    lanes = 2 * HEAD_DIM
    pairs = width // lanes
    row_spec = pl.BlockSpec((rows, lanes), lambda p, place: (0, p))
    ctx_spec = pl.BlockSpec((context, lanes), lambda p, place: (0, p))
    flops = pairs * 2 * 2 * lanes * (5 * rows * context + 3 * rows * rows)
    return pl.pallas_call(
        attention_kernel,
        out_shape=(
            jax.ShapeDtypeStruct((rows, width), jnp.bfloat16),
            jax.ShapeDtypeStruct((context, width), jnp.float32),
            jax.ShapeDtypeStruct((context, width), jnp.float32),
        ),
        grid_spec=pltpu.PrefetchScalarGridSpec(
            num_scalar_prefetch=1,
            grid=(pairs,),
            in_specs=[row_spec, ctx_spec, ctx_spec, row_spec, row_spec, row_spec],
            out_specs=[row_spec, ctx_spec, ctx_spec],
            scratch_shapes=[
                pltpu.VMEM((rows, context), jnp.float32),
                pltpu.VMEM((rows, rows), jnp.float32),
            ],
        ),
        cost_estimate=pl.CostEstimate(
            flops=flops,
            transcendentals=width // HEAD_DIM * rows * (context + rows),
            bytes_accessed=width * (8 * rows + 4 * context + 8 * context),
        ),
    )(place, query, key_clean, value_clean, key_noisy, value_noisy, grad)


def chain_barrier(axes, left, right, has_left, has_right, stages=()):
    barrier = pltpu.get_barrier_semaphore()
    greeted = greet_groups(axes, stages, barrier)
    for peer, present in ((left, has_left), (right, has_right)):
        @pl.when(present)
        def _():
            pl.semaphore_signal(
                barrier, 1, device_id=device_of(axes, "seq", peer),
                device_id_type=pl.DeviceIdType.MESH,
            )
    pl.semaphore_wait(barrier, has_left.astype(jnp.int32) + has_right.astype(jnp.int32) + greeted)


def chain_ends(axes):
    me = lax.axis_index("seq")
    size = lax.axis_size("seq")
    left = jnp.maximum(me - 1, 0)
    right = jnp.minimum(me + 1, size - 1)
    return me, left, right, me > 0, me < size - 1


def project_plain(rows, weight_ref):
    high = rows.astype(jnp.bfloat16)
    low = (rows - high.astype(jnp.float32)).astype(jnp.bfloat16)
    product = jnp.dot(high, weight_ref[...], preferred_element_type=jnp.float32)
    return product + jnp.dot(low, weight_ref[...], preferred_element_type=jnp.float32)


def sum_back_kernel(axes, span, chunks, stages, dk_ref, dv_ref, wk_ref, wv_ref, raw_ref, total_ref,
                    sent, got, send_sems, recv_sems, slots, total_send, total_recv):
    me, left, right, has_left, has_right = chain_ends(axes)
    chain_barrier(axes, left, right, has_left, has_right, stages)
    squares = jnp.zeros((1, 1), jnp.float32)
    rows = raw_ref.shape[0]
    piece = rows // chunks

    @pl.when(jnp.logical_not(has_right))
    def _():
        got[...] = jnp.zeros(got.shape, got.dtype)

    def copy(step, chunk):
        return pltpu.make_async_remote_copy(
            src_ref=sent.at[step, chunk], dst_ref=got.at[step, chunk],
            send_sem=send_sems.at[step, chunk], recv_sem=recv_sems.at[step, chunk],
            device_id=device_of(axes, "seq", left), device_id_type=pl.DeviceIdType.MESH,
        )

    for step in range(span + 1):
        at = pl.ds(step * rows, rows)
        term = project_plain(dk_ref[at, :], wk_ref) + project_plain(dv_ref[at, :], wv_ref)
        for chunk in range(chunks):
            value = term[chunk * piece:(chunk + 1) * piece]
            if step > 0:
                @pl.when(has_right)
                def _():
                    copy(step - 1, chunk).wait_recv()

                value = value + got[step - 1, chunk].astype(jnp.float32)
            if step < span:
                sent[step, chunk] = value.astype(jnp.bfloat16)

                @pl.when(has_left)
                def _():
                    copy(step, chunk).start()
            else:
                raw_ref[pl.ds(chunk * piece, piece), :] = value
                squares = squares + jnp.sum(value * value, axis=(0, 1), keepdims=True)
    total_ref[...] = stage_total(
        axes, stages, jnp.broadcast_to(squares, total_ref.shape), slots, total_send, total_recv
    )
    for step in range(span):
        for chunk in range(chunks):
            @pl.when(has_left)
            def _():
                copy(step, chunk).wait_send()


def sum_back(dk, dv, w_key, w_value, span, rows, axes, chunks=8):
    width = dk.shape[1]
    piece = rows // chunks
    stages = group_stages(axes)
    widest = max(size for _, _, size in stages)
    vmem = pl.BlockSpec(memory_space=pltpu.VMEM)
    return pl.pallas_call(
        functools.partial(sum_back_kernel, axes, span, chunks, stages),
        out_shape=(
            jax.ShapeDtypeStruct((rows, width), jnp.float32),
            jax.ShapeDtypeStruct((8, 128), jnp.float32),
        ),
        in_specs=[vmem] * 4,
        out_specs=[vmem, vmem],
        scratch_shapes=[
            pltpu.VMEM((span, chunks, piece, width), jnp.bfloat16),
            pltpu.VMEM((span, chunks, piece, width), jnp.bfloat16),
            pltpu.SemaphoreType.DMA((span, chunks)),
            pltpu.SemaphoreType.DMA((span, chunks)),
            pltpu.VMEM((len(stages), widest, 8, 128), jnp.float32),
            pltpu.SemaphoreType.DMA((len(stages), widest)),
            pltpu.SemaphoreType.DMA((len(stages), widest)),
        ],
        cost_estimate=pl.CostEstimate(
            flops=8 * width * width * rows * (span + 1), transcendentals=0,
            bytes_accessed=4 * width * (2 * (span + 1) * rows + rows + width),
        ),
        compiler_params=pltpu.CompilerParams(collective_id=1, has_side_effects=True),
    )(dk, dv, w_key, w_value)


def gather_front_kernel(axes, span, chunks, own_ref, noisy_ref, wq_ref, wk_ref, wv_ref,
                        kc_ref, vc_ref, q_ref, kn_ref, vn_ref, wkt_ref, wvt_ref,
                        got, send_sems, recv_sems):
    me, left, right, has_left, has_right = chain_ends(axes)
    chain_barrier(axes, left, right, has_left, has_right)
    rows = own_ref.shape[0]
    piece = rows // chunks
    for step in range(span):
        @pl.when(step >= me)
        def _():
            got[step] = jnp.zeros(got.shape[1:], got.dtype)

    def copy(step, chunk):
        if step == 0:
            source = own_ref.at[pl.ds(chunk * piece, piece)]
        else:
            source = got.at[step - 1, chunk]
        return pltpu.make_async_remote_copy(
            src_ref=source, dst_ref=got.at[step, chunk],
            send_sem=send_sems.at[step, chunk], recv_sem=recv_sems.at[step, chunk],
            device_id=device_of(axes, "seq", right), device_id_type=pl.DeviceIdType.MESH,
        )

    def project_rows(rows_in, weight_ref):
        return jnp.dot(rows_in, weight_ref[...], preferred_element_type=jnp.float32).astype(
            jnp.bfloat16
        )

    for chunk in range(chunks):
        @pl.when(has_right)
        def _():
            copy(0, chunk).start()
    wkt_ref[...] = wk_ref[...].T
    wvt_ref[...] = wv_ref[...].T
    noisy = noisy_ref[...]
    q_ref[...] = project_rows(noisy, wq_ref)
    kn_ref[...] = project_rows(noisy, wk_ref)
    vn_ref[...] = project_rows(noisy, wv_ref)
    own = own_ref[...]
    kc_ref[pl.ds(span * rows, rows), :] = project_rows(own, wk_ref)
    vc_ref[pl.ds(span * rows, rows), :] = project_rows(own, wv_ref)
    for step in range(1, span + 1):
        for chunk in range(chunks):
            @pl.when(step <= me)
            def _():
                copy(step - 1, chunk).wait_recv()
            if step < span:
                @pl.when(has_right & (step <= me))
                def _():
                    copy(step, chunk).start()
        arrived = got[step - 1].reshape(rows, -1)
        kc_ref[pl.ds((span - step) * rows, rows), :] = project_rows(arrived, wk_ref)
        vc_ref[pl.ds((span - step) * rows, rows), :] = project_rows(arrived, wv_ref)
    for step in range(span):
        for chunk in range(chunks):
            @pl.when(has_right & (step <= me))
            def _():
                copy(step, chunk).wait_send()


def gather_front(own, noisy, w_query, w_key, w_value, span, axes, chunks=8):
    rows, width = own.shape
    piece = rows // chunks
    vmem = pl.BlockSpec(memory_space=pltpu.VMEM)
    context = jax.ShapeDtypeStruct(((span + 1) * rows, width), jnp.bfloat16)
    local = jax.ShapeDtypeStruct((rows, width), jnp.bfloat16)
    square = jax.ShapeDtypeStruct(w_key.shape[::-1], w_key.dtype)
    flops = 2 * width * width * rows * (2 * (span + 1) + 3)
    return pl.pallas_call(
        functools.partial(gather_front_kernel, axes, span, chunks),
        out_shape=(context, context, local, local, local, square, square),
        in_specs=[vmem] * 5,
        out_specs=[vmem] * 7,
        scratch_shapes=[
            pltpu.VMEM((span, chunks, piece, width), own.dtype),
            pltpu.SemaphoreType.DMA((span, chunks)),
            pltpu.SemaphoreType.DMA((span, chunks)),
        ],
        cost_estimate=pl.CostEstimate(
            flops=flops, transcendentals=0,
            bytes_accessed=2 * width * (3 * width + (2 * span + 7) * rows),
        ),
        compiler_params=pltpu.CompilerParams(collective_id=2, has_side_effects=True),
    )(own, noisy, w_query, w_key, w_value)

def project(rows, weight):
    high = rows.astype(jnp.bfloat16)
    low = (rows - high.astype(jnp.float32)).astype(jnp.bfloat16)
    contract = (((1,), (1,)), ((), ()))
    product = lax.dot_general(high, weight, contract, preferred_element_type=jnp.float32)
    return product + lax.dot_general(low, weight, contract, preferred_element_type=jnp.float32)


def on_device(clean, out_cot, mask_bits, levels, importance, w_query, w_key, w_value, mask_embed):
    clean_rows = clean[0]
    cotangent = out_cot[0]
    tok_count = clean_rows.shape[0]
    width = clean_rows.shape[1]
    span = WINDOW // tok_count
    scale = 1.0 / math.sqrt(HEAD_DIM)
    position = lax.axis_index("seq") * tok_count
    within = jnp.arange(BLOCK, dtype=jnp.int32)
    block_bits = jnp.right_shift(mask_bits[0][:, None], within[None, :]) & 1
    bits = block_bits.reshape(tok_count)
    masked = bits == 1
    noisy = jnp.where(masked[:, None], mask_embed[None, :], clean_rows)
    key_clean, value_clean, query, key_noisy, value_noisy, key_back, value_back = gather_front(
        clean_rows, noisy, w_query, w_key, w_value, span, ("dp", "seq")
    )
    level_f = levels[0].astype(jnp.float32)
    ratio_f = importance[0].astype(jnp.float32)
    block_weight = LEVELS / level_f * (ratio_f[:, 0] / ratio_f[:, 1])
    token_weight = (block_weight[:, None] * block_bits.astype(jnp.float32)).reshape(tok_count)
    grad_out = (cotangent.astype(jnp.float32) * token_weight[:, None]).astype(jnp.bfloat16)
    place = jnp.reshape(span * tok_count - position, (1,)).astype(jnp.int32)
    attn_rows, dkey_rows, dvalue_rows = attention_heads(
        place, query, key_clean, value_clean, key_noisy, value_noisy, grad_out
    )
    raw, total = sum_back(dkey_rows, dvalue_rows, key_back, value_back, span, tok_count, ("dp", "seq"))
    total_squares = total[0, 0]
    entries = float(tok_count * width * lax.axis_size("dp") * lax.axis_size("seq"))
    rms = jnp.sqrt(total_squares / entries + EPS)
    factor = jnp.minimum(1.0, CLIP / rms)
    return (attn_rows[None], (raw * factor)[None])


def solution(mesh):
    in_specs = (
        P("dp", "seq", None),
        P("dp", "seq", None),
        P("dp", "seq"),
        P("dp", "seq"),
        P("dp", "seq", None),
        P(),
        P(),
        P(),
        P(),
    )
    out_specs = (P("dp", "seq", None), P("dp", "seq", None))
    return jax.shard_map(
        on_device, mesh=mesh, in_specs=in_specs, out_specs=out_specs, check_vma=False
    )
```
